512 devices in a mesh: dom: 128 (over x, z, core), rep: 4 (over y).
Axes of the slice: x: 4, y: 4, z: 16, core: 2. Of those that a mesh axis runs over, the one named last changes fastest.
Arguments:
- features: float32 [128, 65536], P('rep', 'dom'), may hold values from -6 to 6
- tiles: bfloat16 [5120, 128, 128], P('dom'), may hold values from -0.25 to 0.25
- tile_row: int32 [5120], P('dom'), may hold values from 0 to 3
- tile_col: int32 [5120], P('dom'), may hold values from 0 to 511, as said below
- tile_count: int32 [128], P('dom'), may hold values from 16 to 40, as said below
- dest_slot: int32 [65536], P('dom'), may hold values from 0 to 65535, as said below
- w_in: bfloat16 [128, 1024], replicated, may hold values from -0.5 to 0.5
- w_mid: bfloat16 [1024, 1024], replicated, may hold values from -0.1875 to 0.1875
- w_out: bfloat16 [172, 1024], replicated, may hold values from -0.1875 to 0.1875
- cotangent: bfloat16 [172, 65536], P(None, ('dom', 'rep')), may hold values from -0.0234375 to 0.0234375
Outputs:
- batch_features: float32 [128, 65536], P(None, ('dom', 'rep'))
- grad_w_in: float32 [128, 1024], replicated
- grad_w_mid: float32 [1024, 1024], P('dom')
- grad_w_out: float32 [172, 1024], replicated
The draws below stay inside these ranges and needn't reach their ends.
Inputs may be any that keep to these rules, and one draw needn't show every extreme that they name: `tile_col`: every slot of partition p, live or not, names a block column within 4 blocks of p's own blocks p * 4 to (p+1) * 4 - 1, counted modulo 512; each of the 8 blocks just before and just after p's own is named by one of p's first 8 slots. `tile_count`: counts vary from partition to partition (several partitions may share a count); at least one partition holds exactly 40 live slots. `dest_slot`: A permutation of the batch positions; each graph partition sends exactly 1 node into each block of 128 consecutive batch positions.
All inputs are finite; a program needn't handle non-finite values.
Results may differ from the reference program's by a relative error of at most 0.006.
Values sent between devices are 32-bit elements; how exact they have to be, the bound alone decides.
A program may use at most 64 MiB of HBM per device.

```python
import jax
import jax.numpy as jnp
from jax import lax

FEAT = 128
TB = 128
BLK_DEV = 4
HALO_B = 4
TILE_CAP = 40
HID = 1024
CLASSES = 172
NODES_DEV = 512
NB = 512
NODES = 65536
TILES = 5120
MLP_ROWS = 128
SEG = 1
N_DOM = 128
DEVICES = 512


def draw_tile_row(key, part):
    return jax.random.randint(jax.random.fold_in(key, 11), (TILES,), 0, BLK_DEV, dtype=jnp.int32)


def draw_tile_col(key, part):
    index = jnp.arange(TILES, dtype=jnp.int32)
    owner = index // TILE_CAP
    slot_id = index % TILE_CAP
    spread = jax.random.randint(jax.random.fold_in(key, 12), (TILES,), 0, BLK_DEV + 2 * HALO_B, dtype=jnp.int32)
    offset = jnp.where(slot_id < HALO_B, slot_id, jnp.where(slot_id < 2 * HALO_B, BLK_DEV + slot_id, spread))
    return jnp.mod(owner * BLK_DEV - HALO_B + offset, NB).astype(jnp.int32)


def draw_tile_count(key, part):
    lowest = 2 * HALO_B + 8
    counts = jax.random.randint(jax.random.fold_in(key, 13), (N_DOM,), lowest, lowest + TILE_CAP // 4 + 1, dtype=jnp.int32)
    busiest = jax.random.randint(jax.random.fold_in(key, 14), (), 0, N_DOM, dtype=jnp.int32)
    return jnp.where(jnp.arange(N_DOM, dtype=jnp.int32) == busiest, TILE_CAP, counts).astype(jnp.int32)


def draw_dest_slot(key, part):
    scores = jax.random.randint(jax.random.fold_in(key, 15), (N_DOM, NODES_DEV), 0, 2 ** 14, dtype=jnp.int32)
    scores = scores * NODES_DEV + jnp.arange(NODES_DEV, dtype=jnp.int32)[None, :]
    ranking = jnp.argsort(jnp.argsort(scores, axis=1), axis=1).astype(jnp.int32)
    owner = ranking // SEG
    within = jnp.arange(N_DOM, dtype=jnp.int32)[:, None] * SEG + ranking % SEG
    mixing = jax.random.randint(jax.random.fold_in(key, 16), (DEVICES, MLP_ROWS), 0, 2 ** 14, dtype=jnp.int32)
    mixing = mixing * MLP_ROWS + jnp.arange(MLP_ROWS, dtype=jnp.int32)[None, :]
    shuffle = jnp.argsort(mixing, axis=1).astype(jnp.int32)
    placed_blocks = owner * MLP_ROWS + shuffle[owner, within]
    return placed_blocks.reshape(NODES).astype(jnp.int32)


def shard_levels(key, shape, shards, low, high):
    def one(dim, shards_of):
        steps = jax.random.uniform(jax.random.fold_in(jax.random.fold_in(key, 6), dim), (shards_of,), jnp.float32, low / len(shards), high / len(shards))
        return jnp.repeat(jnp.exp(steps), shape[dim] // shards_of).reshape((-1,) + (1,) * (len(shape) - dim - 1))

    level = one(*shards[0])
    for cut in shards[1:]:
        level = level * one(*cut)
    return level


def normal_values(key, dims, scale, limit, split=(), held_as=jnp.bfloat16):
    level = shard_levels(key, dims, split, -0.22, 0.18) if split else 1.0
    entries = jax.random.normal(key, dims, jnp.float32) * scale * level
    return jnp.minimum(jnp.maximum(entries, -limit), limit).astype(held_as)


def setup_inputs(seed: int = 0) -> dict:
    keys = jax.random.split(jax.random.key(seed), 11)
    return {
        "features": normal_values(keys[0], (FEAT, NODES), 1.0, 6.0, ((0, 4), (1, 128)), jnp.float32),
        "tiles": normal_values(keys[1], (TILES, TB, TB), (4 * TB) ** -0.5, 0.25, ((0, 128),)),
        "tile_row": draw_tile_row(jax.random.fold_in(keys[10], 71), 0),
        "tile_col": draw_tile_col(jax.random.fold_in(keys[10], 71), 0),
        "tile_count": draw_tile_count(jax.random.fold_in(keys[10], 71), 0),
        "dest_slot": draw_dest_slot(jax.random.fold_in(keys[10], 71), 0),
        "w_in": normal_values(keys[6], (FEAT, HID), FEAT ** -0.5, 0.5),
        "w_mid": normal_values(keys[7], (HID, HID), HID ** -0.5, 0.1875),
        "w_out": normal_values(keys[8], (CLASSES, HID), HID ** -0.5, 0.1875),
        "cotangent": normal_values(keys[9], (CLASSES, NODES), (2.0 * NODES ** -0.5), 0.0234375, ((1, 512),)),
    }


series_zero = 0.3085083
series_one = -0.4305395
series_two = 0.1864784
LEADING = (((0,), (0,)), ((), ()))
TRAILING = (((1,), (1,)), ((), ()))


def silu_slope(pre):
    sigma = jax.nn.sigmoid(pre)
    return sigma * (1.0 + pre * (1.0 - sigma))


def apply_operator(field, tiles, tile_row, tile_col, tile_count):
    blocks = field.reshape(FEAT, NB, TB)
    tile_groups = tiles.reshape(N_DOM, TILE_CAP, TB, TB)
    row_groups = tile_row.reshape(N_DOM, TILE_CAP)
    col_groups = tile_col.reshape(N_DOM, TILE_CAP)
    slot_ids = jnp.arange(TILE_CAP, dtype=jnp.int32)
    targets = jnp.arange(BLK_DEV, dtype=jnp.int32)

    def one_part(packed):
        partition_tiles, part_rows, part_cols, part_count = packed
        input_values = jnp.take(blocks, part_cols, axis=1)
        block_products = jnp.einsum("lkz,glz->glk", partition_tiles.astype(jnp.float32), input_values, precision=lax.Precision.HIGHEST)
        live_mask = (slot_ids < part_count).astype(jnp.float32)
        assignment_map = (part_rows[None, :] == targets[:, None]).astype(jnp.float32) * live_mask[None, :]
        return jnp.einsum("wy,kya->kwa", assignment_map, block_products, precision=lax.Precision.HIGHEST)

    stacked = lax.map(one_part, (tile_groups, row_groups, col_groups, tile_count))
    return jnp.transpose(stacked, (1, 0, 2, 3)).reshape(FEAT, NODES)


def reference(features, tiles, tile_row, tile_col, tile_count, dest_slot, w_in, w_mid, w_out, cotangent):
    first = apply_operator(features, tiles, tile_row, tile_col, tile_count)
    second = 2.0 * apply_operator(first, tiles, tile_row, tile_col, tile_count) - features
    diffused = series_zero * features + series_one * first + series_two * second
    batch_features = jnp.zeros_like(diffused).at[:, dest_slot].set(diffused)
    inputs_bf = batch_features.astype(jnp.bfloat16)

    def one_block(carry, block_index):
        grad_in, grad_mid, grad_out = carry
        first_row = block_index * MLP_ROWS
        input_block = lax.dynamic_slice_in_dim(inputs_bf, first_row, MLP_ROWS, 1)
        cot_block = lax.dynamic_slice_in_dim(cotangent, first_row, MLP_ROWS, 1)
        pre_one = lax.dot_general(input_block, w_in, LEADING, preferred_element_type=jnp.float32)
        hidden_one = jax.nn.silu(pre_one).astype(jnp.bfloat16)
        pre_two = jnp.dot(hidden_one, w_mid, preferred_element_type=jnp.float32)
        hidden_two = jax.nn.silu(pre_two).astype(jnp.bfloat16)
        out_term = jnp.dot(cot_block, hidden_two, preferred_element_type=jnp.float32)
        back_two = lax.dot_general(cot_block, w_out, LEADING, preferred_element_type=jnp.float32)
        delta_two = (back_two * silu_slope(pre_two)).astype(jnp.bfloat16)
        mid_term = lax.dot_general(hidden_one, delta_two, LEADING, preferred_element_type=jnp.float32)
        back_one = lax.dot_general(delta_two, w_mid, TRAILING, preferred_element_type=jnp.float32)
        delta_one = (back_one * silu_slope(pre_one)).astype(jnp.bfloat16)
        in_term = jnp.dot(input_block, delta_one, preferred_element_type=jnp.float32)
        return (grad_in + in_term, grad_mid + mid_term, grad_out + out_term), None

    start_state = (jnp.zeros((FEAT, HID), jnp.float32), jnp.zeros((HID, HID), jnp.float32), jnp.zeros((CLASSES, HID), jnp.float32))
    totals, unused = lax.scan(one_block, start_state, jnp.arange(DEVICES, dtype=jnp.int32))
    return batch_features, totals[0], totals[1], totals[2]
```

```python
import jax
import jax.numpy as jnp
from jax import lax
from jax.experimental import pallas as pl
from jax.experimental.pallas import tpu as pltpu
from jax.sharding import PartitionSpec as P

series_zero = 0.3085083
series_one = -0.4305395
series_two = 0.1864784
LEADING = (((0,), (0,)), ((), ()))
TRAILING = (((1,), (1,)), ((), ()))
MESH = pl.DeviceIdType.MESH
NX, NY, NZ = 4, 4, 16
F32 = jnp.float32
BF16 = jnp.bfloat16


EX_X, EX_C, EX_B = 0, 1, 2
A_MID, A_IO, B_MID, B_IO = 3, 6, 9, 12
A_TWO, B_TWO = 15, 18
Z_ONE, Z_TWO, Z_ALL = 21, 25, 29
MID_ALL = 53
A_THREE, B_THREE, A_FOUR, B_FOUR, PAIR = 61, 64, 67, 70, 73
HALO_ONE, HALO_TWO = 74, 76
REP_X, Z_X, XC_X = 78, 82, 98
Z_P, XC_P = 106, 122
SEMS = 130


def sigmoid(v):
    return 0.5 + 0.5 * jnp.tanh(0.5 * v)


def split(v):
    high = v.astype(BF16)
    rest = v - high.astype(F32)
    middle = rest.astype(BF16)
    low = (rest - middle.astype(F32)).astype(BF16)
    return high, middle, low


def train_kernel(
    row_hbm, col_hbm, count_hbm, feat_hbm, tiles_hbm, dest_hbm, cot_hbm, w_in_hbm, w_mid_hbm, w_out_hbm,
    out_x, out_in, out_mid, out_out,
    row_ref, col_ref, count_ref, feat, tiles, dest, cot, w_in_ref, w_mid_ref, w_out_ref,
    ext, ext_two, parts, hot, moved, within, amsg, rf, t2, rz2, rx, rq, p2, pz2, px, pq, put,
    x2, cot2, xt, ct, wo, h1, slope1, d2, send_b, recv_b,
    mid, io, ra_mid, ra_io, rb_mid, rb_io, sa, sb, r2a, r2b, zs, rz, zs_two, rz_two, mine, ri, r4, full,
    ssem, rsem, lsem,
):
    loads = []
    for i, (src, dst) in enumerate((
        (feat_hbm, feat), (dest_hbm, dest), (cot_hbm, cot), (row_hbm, row_ref),
        (col_hbm, col_ref), (count_hbm, count_ref), (tiles_hbm, tiles),
        (w_in_hbm, w_in_ref), (w_out_hbm, w_out_ref), (w_mid_hbm, w_mid_ref),
    )):
        loads.append(pltpu.make_async_copy(src, dst, lsem.at[i]))
        loads[-1].start()
    d = lax.axis_index("dom")
    y = lax.axis_index("rep")
    c = d % 2
    z = (d // 2) % NZ
    x = d // (2 * NZ)

    def place(xx, yy, zz, cc):
        return ((xx * NZ + zz) * 2 + cc, yy)

    def copy(src, dst, slot, dev):
        return pltpu.make_async_remote_copy(
            src_ref=src, dst_ref=dst, send_sem=ssem.at[slot], recv_sem=rsem.at[slot],
            device_id=dev, device_id_type=MESH,
        )

    def lanes(index, width):
        return pl.ds(pl.multiple_of(index * width, width), width)

    partner = place(x, y, z, 1 - c)
    far = ((d + 2 * c - 1 + 2 * NX * NZ) % (2 * NX * NZ), y)
    xs = [place((x + k) % NX, y, z, c) for k in range(1, NX)]
    xo = [place((x + k) % NX, y, z, 1 - c) for k in range(1, NX)]
    ys = [place(x, (y + k) % NY, z, c) for k in range(1, NY)]
    yo = [place(x, (y + k) % NY, z, 1 - c) for k in range(1, NY)]
    barrier = pltpu.get_barrier_semaphore()
    for dev in [partner, far] + xs + xo + ys + yo:
        pl.semaphore_signal(barrier, inc=1, device_id=dev, device_id_type=MESH)

    def greet(k, carry):
        pl.semaphore_signal(
            barrier, inc=1, device_id=place(x, y, (z + k) % NZ, c), device_id_type=MESH
        )
        return carry

    lax.fori_loop(1, NZ, greet, 0)

    for one in loads[:3]:
        one.wait()
    own = jnp.stack([feat[:, pl.ds(128 * b, 128)] for b in range(4)])
    ext[4:8] = own
    for i, part in enumerate(split(own)):
        parts[4:8, pl.ds(32 * i, 32)] = part
    cot2[c] = jnp.zeros((192, 128), F32)
    cot2[c, 0:172] = cot[...].astype(F32)
    pl.semaphore_wait(barrier, 2 + 3 + 3 + 3 + 3 + NZ - 1)

    def halo(field, slot):
        one = copy(field.at[pl.ds(4, 4)], field.at[pl.ds(8 * c, 4)], slot, partner)
        two = copy(field.at[pl.ds(4, 4)], field.at[pl.ds(8 * (1 - c), 4)], slot + 1, far)
        two.start()
        one.start()
        return one, two

    near, wide = halo(ext, HALO_ONE)
    ex_c = copy(cot2.at[c], cot2.at[c], EX_C, partner)
    ex_c.start()
    copies = [near, wide, ex_c]

    j = lax.broadcasted_iota(jnp.int32, (512, 128), 0)
    target = ((((j >> 1) & 3) * NZ + ((j >> 3) & 15)) * 2 + (j & 1)) * NY + (j >> 7)
    for b in range(4):
        line = dest[pl.ds(b, 1), :]
        hot[:, pl.ds(128 * b, 128)] = jnp.where(target == (line >> 7), 1.0, 0.0).astype(BF16)
        within[:, pl.ds(128 * b, 128)] = jnp.broadcast_to(
            (line & 127).astype(F32), (128, 128)
        ).astype(BF16)

    p2[...] = lax.dot_general(
        hot[lanes(y, 128), :], within[...], TRAILING, preferred_element_type=F32
    ).reshape(NZ, 8, 128)
    mine_xc = x * 2 + c

    def over_z(src, dst, slot):
        def one(k):
            to = (z + k) % NZ
            return copy(src.at[to], dst.at[z], slot + k, place(x, y, to, c))

        def start(k, carry):
            one(k).start()
            return carry

        def recv(k, carry):
            one(k).wait_recv()
            return carry

        def sent(k, carry):
            one(k).wait_send()
            return carry

        return start, recv, sent

    def over_xc(src, dst, slot):
        made = []
        for k in (2, 1, 3, 0):
            to = (x + k) % NX
            if k:
                made.append(copy(src.at[to * 2 + c], dst.at[mine_xc], slot + k, xs[k - 1]))
                made[-1].start()
            dev = xo[k - 1] if k else partner
            made.append(copy(src.at[to * 2 + 1 - c], dst.at[mine_xc], slot + 4 + k, dev))
            made[-1].start()
        return made

    pz_start, pz_recv, pz_sent = over_z(p2, pz2, Z_P)
    lax.fori_loop(1, NZ, pz_start, 0)
    pz2[z] = p2[z]
    wo[...] = jnp.zeros((192, 1024), BF16)
    for one in loads[3:]:
        one.wait()
    wo[0:172, :] = w_out_ref[...]

    count = count_ref[0]

    def spread(field, near, wide):
        near.wait_recv()
        for i, part in enumerate(split(field[pl.ds(8 * (1 - c), 4)])):
            parts[pl.ds(8 * (1 - c), 4), pl.ds(32 * i, 32)] = part
        wide.wait_recv()
        for i, part in enumerate(split(field[pl.ds(8 * c, 4)])):
            parts[pl.ds(8 * c, 4), pl.ds(32 * i, 32)] = part

        def slots(i, sums):
            for u in range(5):
                s = i * 5 + u
                at = jnp.minimum((col_ref[s] - 4 * d + 4) & 511, 11)
                product = lax.dot_general(
                    parts[at], tiles[s], TRAILING, preferred_element_type=F32
                )
                total = product[0:32] + product[32:64] + product[64:96]
                row = jnp.where(s < count, row_ref[s], -1)
                sums = tuple(
                    v + jnp.where(row == b, 1.0, 0.0) * total for b, v in enumerate(sums)
                )
            return sums

        zero = jnp.zeros((32, 128), F32)
        return jnp.stack(lax.fori_loop(0, 8, slots, (zero,) * 4))

    first = spread(ext, near, wide)
    ext_two[4:8] = first
    near, wide = halo(ext_two, HALO_TWO)
    copies += [near, wide]
    for i, part in enumerate(split(first)):
        parts[4:8, pl.ds(32 * i, 32)] = part
    lax.fori_loop(1, NZ, pz_recv, 0)
    for i in range(8):
        px[i] = pz2[:, i, :]
    xc_p = over_xc(px, pq, XC_P)
    pq[mine_xc] = px[mine_xc]
    copies += xc_p
    second = spread(ext_two, near, wide)
    second = 2.0 * second - ext[4:8]
    diffused = series_zero * ext[4:8] + series_one * ext_two[4:8] + series_two * second

    for i, part in enumerate(split(diffused)):
        for b in range(4):
            moved[pl.ds(32 * i, 32), pl.ds(128 * b, 128)] = part[b]
    sorted_rows = lax.dot_general(moved[...], hot[...], TRAILING, preferred_element_type=F32)
    columns = sorted_rows[0:32] + sorted_rows[32:64] + sorted_rows[64:96]
    for i in range(NY):
        amsg[i] = columns[:, 128 * i : 128 * i + 128]
    rep_x = []
    for k in (2, 1, 3):
        to = (y + k) % NY
        rep_x.append(copy(amsg.at[to], rf.at[y], REP_X + k, ys[k - 1]))
        rep_x[-1].start()
    rf[y] = amsg[y]
    for one in xc_p:
        one.wait_recv()
    at_lane = lax.broadcasted_iota(jnp.int32, (128, 128), 1).astype(F32)
    put[...] = jnp.where(pq[...].reshape(128, 128) == at_lane, 1.0, 0.0).astype(BF16)
    for one in rep_x:
        one.wait_recv()
    t2[...] = rf[...].reshape(128, 128).T.reshape(NZ, 8, 128)
    zx_start, zx_recv, zx_sent = over_z(t2, rz2, Z_X)
    lax.fori_loop(1, NZ, zx_start, 0)
    rz2[z] = t2[z]
    lax.fori_loop(1, NZ, zx_recv, 0)
    for i in range(8):
        rx[i] = rz2[:, i, :]
    xc_x = over_xc(rx, rq, XC_X)
    rq[mine_xc] = rx[mine_xc]
    for one in xc_x:
        one.wait_recv()
    copies += rep_x + xc_x
    lines = jnp.concatenate(split(rq[...].reshape(128, 128).T), axis=0)
    placed = jnp.dot(lines, put[...], preferred_element_type=F32)
    batch = placed[0:128] + placed[128:256] + placed[256:384]
    out_x[...] = batch

    x2[c] = batch
    ex_x = copy(x2.at[c], x2.at[c], EX_X, partner)
    ex_x.start()
    ex_c.wait_recv()
    for i in range(2):
        ct[pl.ds(128 * i, 128), :] = cot2[i].T.astype(BF16)
    ex_x.wait_recv()
    for i in range(2):
        xt[pl.ds(128 * i, 128), :] = x2[i].T.astype(BF16)

    for j in range(4):
        cols = pl.ds(256 * j, 256)
        pre = jnp.dot(xt[...], w_in_ref[:, cols], preferred_element_type=F32)
        g = sigmoid(pre)
        h1[:, cols] = (pre * g).astype(BF16)
        slope1[j] = g * (1.0 + pre * (1.0 - g))
    half = lanes(c, 512)
    pre_two = jnp.dot(h1[...], w_mid_ref[:, half], preferred_element_type=F32)
    g_two = sigmoid(pre_two)
    h2 = (pre_two * g_two).astype(BF16)
    back_two = jnp.dot(ct[...], wo[:, half], preferred_element_type=F32)
    d2[...] = (back_two * (g_two * (1.0 + pre_two * (1.0 - g_two)))).astype(BF16)

    send_b[...] = lax.dot_general(
        d2[...], w_mid_ref[lanes(1 - c, 512), half], TRAILING, preferred_element_type=F32
    )
    ex_b = copy(send_b, recv_b, EX_B, partner)
    ex_b.start()

    copies += [ex_x, ex_b]
    first_a = []
    for k in (2, 1, 3, 0):
        to = (x + k) % NX
        rows = lax.dot_general(
            h1[:, lanes(to, 256)], d2[...], LEADING, preferred_element_type=F32
        ).reshape(NZ, 2, 8, 512)
        mid[0, to] = rows[:, 0]
        mid[1, to] = rows[:, 1]
        if k:
            one = copy(mid.at[0, to], ra_mid.at[k - 1], A_MID + k - 1, xs[k - 1])
            one.start()
            first_a.append(one)
    first_b = []
    for k in (2, 1, 3):
        one = copy(
            mid.at[1, :, :, :, lanes((y + k) % NY, 128)], rb_mid.at[k - 1], B_MID + k - 1, ys[k - 1]
        )
        one.start()
        first_b.append(one)

    cot_rows = [cot2[i].astype(BF16) for i in range(2)]
    grad_out = jnp.dot(
        jnp.concatenate(cot_rows, axis=1), h2, preferred_element_type=F32
    ).reshape(24, 8, 512)
    own_back = lax.dot_general(
        d2[...], w_mid_ref[half, half], TRAILING, preferred_element_type=F32
    )
    ex_b.wait_recv()
    slope = jnp.concatenate([slope1[2 * c], slope1[2 * c + 1]], axis=1)
    delta_one = ((own_back + recv_b[...]) * slope).astype(BF16)
    x_rows = jnp.concatenate([x2[i].astype(BF16) for i in range(2)], axis=1)
    grad_in = jnp.dot(x_rows, delta_one, preferred_element_type=F32).reshape(16, 8, 512)
    io[0:16] = grad_in
    io[16:40] = grad_out
    for k in (2, 1, 3):
        to = (x + k) % NX
        one = copy(io.at[pl.ds(to * 5, 5)], ra_io.at[k - 1], A_IO + k - 1, xs[k - 1])
        one.start()
        first_a.append(one)
        one = copy(
            io.at[pl.ds(20, 20), :, lanes((y + k) % NY, 128)], rb_io.at[k - 1], B_IO + k - 1, ys[k - 1]
        )
        one.start()
        first_b.append(one)
    copies += first_a + first_b

    y_lane = lanes(y, 128)
    for one in first_a:
        one.wait_recv()
    sa[0:16] = mid[0, x] + ra_mid[0] + ra_mid[1] + ra_mid[2]
    sa[16:21] = io[pl.ds(x * 5, 5)] + ra_io[0] + ra_io[1] + ra_io[2]
    second = []
    for k in (2, 1, 3):
        one = copy(
            sa.at[:, :, lanes((y + k) % NY, 128)], r2a.at[k - 1], A_TWO + k - 1, ys[k - 1]
        )
        one.start()
        second.append(one)
    for one in first_b:
        one.wait_recv()
    for i in range(NX):
        sb[i, 0:16] = mid[1, i, :, :, y_lane] + rb_mid[0, i] + rb_mid[1, i] + rb_mid[2, i]
        at = pl.ds(5 * i, 5)
        sb[i, 16:21] = io[pl.ds(20 + 5 * i, 5), :, y_lane] + rb_io[0, at] + rb_io[1, at] + rb_io[2, at]
    for k in (2, 1, 3):
        one = copy(sb.at[(x + k) % NX], r2b.at[k - 1], B_TWO + k - 1, xs[k - 1])
        one.start()
        second.append(one)
    for one in second:
        one.wait_recv()
    copies += second
    sum_a = sa[:, :, y_lane] + r2a[0] + r2a[1] + r2a[2]
    sum_b = sb[x] + r2b[0] + r2b[1] + r2b[2]

    group, spot_z = z // 4, z % 4
    io_tiles = [sum_a[16 + t] for t in range(5)] + [sum_b[16 + t] for t in range(5)]
    io_tiles += [jnp.zeros((8, 128), F32)] * 2
    for i in range(4):
        for g in range(4):
            zs[i, g] = sum_a[4 * g + i]
            zs[i, 4 + g] = sum_b[4 * g + i]
        for t in range(3):
            zs[i, 8 + t] = io_tiles[4 * t + i]
    third = []
    for k in (2, 1, 3):
        to = (spot_z + k) % 4
        third.append(
            copy(zs.at[to], rz.at[k - 1], Z_ONE + k, place(x, y, group * 4 + to, c))
        )
        third[-1].start()
    for one in third:
        one.wait_recv()
    grouped = zs[spot_z] + rz[0] + rz[1] + rz[2]
    for g in range(4):
        zs_two[g, 0] = grouped[g]
        zs_two[g, 1] = grouped[4 + g]
        zs_two[g, 2:5] = grouped[8:11]
    across = []
    for k in (2, 1, 3):
        to = (group + k) % 4
        across.append(
            copy(zs_two.at[to], rz_two.at[group], Z_TWO + k, place(x, y, to * 4 + spot_z, c))
        )
        across[-1].start()
    rz_two[group] = zs_two[group]
    for one in across:
        one.wait_recv()
    copies += third + across
    mine[...] = ((rz_two[0] + rz_two[1]) + rz_two[2]) + rz_two[3]

    last = []
    for k in range(NY):
        if k:
            one = copy(mine.at[c], r4.at[c, y], MID_ALL + k, ys[k - 1])
            one.start()
            last.append(one)
        one = copy(
            mine.at[1 - c], r4.at[c, y], MID_ALL + 4 + k, yo[k - 1] if k else partner
        )
        one.start()
        last.append(one)
    r4[c, y] = mine[c]
    copies += last

    share = []
    for k in (2, 1, 3):
        share.append(
            copy(
                mine.at[pl.ds(2, 3)], ri.at[spot_z], Z_ALL + k,
                place(x, y, group * 4 + (spot_z + k) % 4, c),
            )
        )
        share[-1].start()
    ri[spot_z] = mine[2:5]
    for one in share:
        one.wait_recv()
    copies += share
    tile = lanes(c * NY + y, 128)
    rows_a, rows_b = pl.ds(x * 5, 5), pl.ds((NX + x) * 5, 5)
    for t in range(10):
        full[(t // 5 * NX + x) * 5 + t % 5, :, tile] = ri[t % 4, t // 4]
    third = []
    for k in (2, 1, 3):
        spot = full.at[rows_a, :, tile]
        third.append(copy(spot, spot, A_THREE + k - 1, ys[k - 1]))
        third[-1].start()
        spot = full.at[rows_b, :, tile]
        third.append(copy(spot, spot, B_THREE + k - 1, xs[k - 1]))
        third[-1].start()
    for one in third:
        one.wait_recv()
    fourth = []
    for k in (2, 1, 3):
        spot = full.at[rows_a, :, half]
        fourth.append(copy(spot, spot, A_FOUR + k - 1, xs[k - 1]))
        fourth[-1].start()
        spot = full.at[pl.ds(20, 20), :, tile]
        fourth.append(copy(spot, spot, B_FOUR + k - 1, ys[k - 1]))
        fourth[-1].start()
    for one in fourth:
        one.wait_recv()
    spot = full.at[:, :, half]
    pair = copy(spot, spot, PAIR, partner)
    pair.start()
    for one in last:
        one.wait_recv()
    for i in range(8):
        out_mid[:, pl.ds(128 * i, 128)] = r4[i // 4, i % 4]
    copies += third + fourth + [pair]
    pair.wait_recv()
    out_in[...] = full[0:16].reshape(128, 1024)
    out_out[...] = full[16:40].reshape(192, 1024)[0:172]

    lax.fori_loop(1, NZ, pz_sent, 0)
    lax.fori_loop(1, NZ, zx_sent, 0)
    for one in copies:
        one.wait_send()


def train(tile_row, tile_col, tile_count, features, tiles, dest, cotangent, w_in, w_mid, w_out):
    vmem = pl.BlockSpec(memory_space=pltpu.VMEM)
    hbm = pl.BlockSpec(memory_space=pltpu.HBM)
    buf = pltpu.VMEM
    return pl.pallas_call(
        train_kernel,
        out_shape=(
            jax.ShapeDtypeStruct((128, 128), F32),
            jax.ShapeDtypeStruct((128, 1024), F32),
            jax.ShapeDtypeStruct((8, 1024), F32),
            jax.ShapeDtypeStruct((172, 1024), F32),
        ),
        in_specs=[hbm] * 10,
        out_specs=(vmem,) * 4,
        scratch_shapes=[
            pltpu.SMEM((40,), jnp.int32),
            pltpu.SMEM((40,), jnp.int32),
            pltpu.SMEM((1,), jnp.int32),
            buf((32, 512), F32),
            buf((40, 128, 128), BF16),
            buf((4, 128), jnp.int32),
            buf((172, 128), BF16),
            buf((128, 1024), BF16),
            buf((1024, 1024), BF16),
            buf((172, 1024), BF16),
            buf((12, 32, 128), F32),
            buf((12, 32, 128), F32),
            buf((12, 96, 128), BF16),
            buf((512, 512), BF16),
            buf((96, 512), BF16),
            buf((128, 512), BF16),
            buf((NY, 32, 128), F32),
            buf((NY, 32, 128), F32),
            buf((NZ, 8, 128), F32),
            buf((NZ, 8, 128), F32),
            buf((8, NZ, 128), F32),
            buf((8, NZ, 128), F32),
            buf((NZ, 8, 128), F32),
            buf((NZ, 8, 128), F32),
            buf((8, NZ, 128), F32),
            buf((8, NZ, 128), F32),
            buf((128, 128), BF16),
            buf((2, 128, 128), F32),
            buf((2, 192, 128), F32),
            buf((256, 128), BF16),
            buf((256, 192), BF16),
            buf((192, 1024), BF16),
            buf((256, 1024), BF16),
            buf((4, 256, 256), F32),
            buf((256, 512), BF16),
            buf((256, 512), F32),
            buf((256, 512), F32),
            buf((2, NX, NZ, 8, 512), F32),
            buf((40, 8, 512), F32),
            buf((3, NZ, 8, 512), F32),
            buf((3, 5, 8, 512), F32),
            buf((3, NX, NZ, 8, 128), F32),
            buf((3, 20, 8, 128), F32),
            buf((21, 8, 512), F32),
            buf((NX, 21, 8, 128), F32),
            buf((3, 21, 8, 128), F32),
            buf((3, 21, 8, 128), F32),
            buf((4, 11, 8, 128), F32),
            buf((3, 11, 8, 128), F32),
            buf((4, 5, 8, 128), F32),
            buf((4, 5, 8, 128), F32),
            buf((5, 8, 128), F32),
            buf((4, 3, 8, 128), F32),
            buf((2, NY, 8, 128), F32),
            buf((40, 8, 1024), F32),
            pltpu.SemaphoreType.DMA((SEMS,)),
            pltpu.SemaphoreType.DMA((SEMS,)),
            pltpu.SemaphoreType.DMA((10,)),
        ],
        compiler_params=pltpu.CompilerParams(
            collective_id=0, has_side_effects=True, vmem_limit_bytes=60 * 1024 * 1024
        ),
    )(tile_row, tile_col, tile_count, features, tiles, dest, cotangent, w_in, w_mid, w_out)


def shards(
    features, tiles, tile_row, tile_col, tile_count, dest_slot, w_in, w_mid, w_out, cotangent
):
    dest = dest_slot.reshape(4, 128)
    return train(
        tile_row, tile_col, tile_count, features, tiles, dest, cotangent, w_in, w_mid, w_out
    )


def solution(mesh):
    in_specs = (
        P("rep", "dom"),
        P("dom", None, None),
        P("dom"),
        P("dom"),
        P("dom"),
        P("dom"),
        P(),
        P(),
        P(),
        P(None, ("dom", "rep")),
    )
    out_specs = (P(None, ("dom", "rep")), P(), P("dom", None), P())
    return jax.shard_map(shards, mesh=mesh, in_specs=in_specs, out_specs=out_specs, check_vma=False)
```

```python
import jax
import jax.numpy as jnp
from jax import lax
from jax.experimental import pallas as pl
from jax.experimental.pallas import tpu as pltpu
from jax.sharding import PartitionSpec as P

series_zero = 0.3085083
series_one = -0.4305395
series_two = 0.1864784
LEADING = (((0,), (0,)), ((), ()))
TRAILING = (((1,), (1,)), ((), ()))
MESH = pl.DeviceIdType.MESH
NX, NY, NZ = 4, 4, 16
F32 = jnp.float32
BF16 = jnp.bfloat16


EX_X, EX_C, EX_B = 0, 1, 2
A_MID, A_IO, B_MID, B_IO = 3, 6, 9, 12
A_TWO, B_TWO = 15, 18
Z_ONE, Z_TWO, Z_ALL = 21, 25, 29
MID_ALL = 53
A_THREE, B_THREE, A_FOUR, B_FOUR, PAIR = 61, 64, 67, 70, 73
HALO_ONE, HALO_TWO = 74, 76
REP_X, Z_X, XC_X = 78, 82, 98
Z_P, XC_P = 106, 122
A_TWO_IO, B_TWO_IO, Z_ONE_IO, Z_TWO_IO = 130, 133, 136, 140
SEMS = 144


def sigmoid(v):
    return 0.5 + 0.5 * jnp.tanh(0.5 * v)


def split(v):
    high = v.astype(BF16)
    rest = v - high.astype(F32)
    middle = rest.astype(BF16)
    low = (rest - middle.astype(F32)).astype(BF16)
    return high, middle, low


def train_kernel(
    count_ref, row_hbm, col_hbm, feat_hbm, tiles_hbm, dest_hbm, cot_hbm, w_in_hbm, w_mid_hbm, w_out_hbm,
    out_x, out_in, out_mid, out_out,
    row_ref, col_ref, feat, tiles, dest, cot, w_in_ref, w_mid_ref, w_out_ref,
    ext, ext_two, parts, hot, moved, within, amsg, rf, t2, rz2, rx, rq, p2, pz2, px, pq, put,
    x2, cot2, xt, ct, wo, h1, slope1, d2, send_b, recv_b,
    mid, io, ra_mid, ra_io, rb_mid, rb_io, sa, sb, r2a, r2b, zs, rz, zs_two, rz_two, mine, ri, r4, full,
    sai, sbi, r2ai, r2bi, zi, rzi, rzi_two, mine_io,
    ssem, rsem, lsem,
):
    loads = []
    for i, (src, dst) in enumerate((
        (feat_hbm, feat), (dest_hbm, dest), (cot_hbm, cot), (row_hbm, row_ref),
        (col_hbm, col_ref), (tiles_hbm, tiles),
        (w_in_hbm, w_in_ref), (w_out_hbm, w_out_ref), (w_mid_hbm, w_mid_ref),
    )):
        loads.append(pltpu.make_async_copy(src, dst, lsem.at[i]))
        loads[-1].start()
    d = lax.axis_index("dom")
    y = lax.axis_index("rep")
    c = d % 2
    z = (d // 2) % NZ
    x = d // (2 * NZ)

    def place(xx, yy, zz, cc):
        return ((xx * NZ + zz) * 2 + cc, yy)

    def copy(src, dst, slot, dev):
        return pltpu.make_async_remote_copy(
            src_ref=src, dst_ref=dst, send_sem=ssem.at[slot], recv_sem=rsem.at[slot],
            device_id=dev, device_id_type=MESH,
        )

    def lanes(index, width):
        return pl.ds(pl.multiple_of(index * width, width), width)

    partner = place(x, y, z, 1 - c)
    far = ((d + 2 * c - 1 + 2 * NX * NZ) % (2 * NX * NZ), y)
    xs = [place((x + k) % NX, y, z, c) for k in range(1, NX)]
    xo = [place((x + k) % NX, y, z, 1 - c) for k in range(1, NX)]
    ys = [place(x, (y + k) % NY, z, c) for k in range(1, NY)]
    yo = [place(x, (y + k) % NY, z, 1 - c) for k in range(1, NY)]
    barrier = pltpu.get_barrier_semaphore()
    for dev in [partner, far] + xs + xo + ys + yo:
        pl.semaphore_signal(barrier, inc=1, device_id=dev, device_id_type=MESH)

    def greet(k, carry):
        pl.semaphore_signal(
            barrier, inc=1, device_id=place(x, y, (z + k) % NZ, c), device_id_type=MESH
        )
        return carry

    lax.fori_loop(1, NZ, greet, 0)

    for one in loads[:3]:
        one.wait()
    own = jnp.stack([feat[:, pl.ds(128 * b, 128)] for b in range(4)])
    ext[4:8] = own
    for i, part in enumerate(split(own)):
        parts[4:8, pl.ds(32 * i, 32)] = part
    cot2[c] = jnp.zeros((192, 128), F32)
    cot2[c, 0:172] = cot[...].astype(F32)
    j = lax.broadcasted_iota(jnp.int32, (512, 128), 0)
    target = ((((j >> 1) & 3) * NZ + ((j >> 3) & 15)) * 2 + (j & 1)) * NY + (j >> 7)
    for b in range(4):
        line = dest[pl.ds(b, 1), :]
        hot[:, pl.ds(128 * b, 128)] = jnp.where(target == (line >> 7), 1.0, 0.0).astype(BF16)
        within[:, pl.ds(128 * b, 128)] = jnp.broadcast_to(
            (line & 127).astype(F32), (128, 128)
        ).astype(BF16)

    p2[...] = lax.dot_general(
        hot[lanes(y, 128), :], within[...], TRAILING, preferred_element_type=F32
    ).reshape(NZ, 8, 128)
    pl.semaphore_wait(barrier, 2 + 3 + 3 + 3 + 3 + NZ - 1)

    def halo(field, slot):
        one = copy(field.at[pl.ds(4, 4)], field.at[pl.ds(8 * c, 4)], slot, partner)
        two = copy(field.at[pl.ds(4, 4)], field.at[pl.ds(8 * (1 - c), 4)], slot + 1, far)
        two.start()
        one.start()
        return one, two

    near, wide = halo(ext, HALO_ONE)
    ex_c = copy(cot2.at[c], cot2.at[c], EX_C, partner)
    ex_c.start()
    copies = [near, wide, ex_c]
    mine_xc = x * 2 + c

    def over_z(src, dst, slot):
        def one(k):
            to = (z + k) % NZ
            return copy(src.at[to], dst.at[z], slot + k, place(x, y, to, c))

        def start(k, carry):
            one(k).start()
            return carry

        def recv(k, carry):
            one(k).wait_recv()
            return carry

        def sent(k, carry):
            one(k).wait_send()
            return carry

        return start, recv, sent

    def over_xc(src, dst, slot):
        made = []
        for k in (2, 1, 3, 0):
            to = (x + k) % NX
            if k:
                made.append(copy(src.at[to * 2 + c], dst.at[mine_xc], slot + k, xs[k - 1]))
                made[-1].start()
            dev = xo[k - 1] if k else partner
            made.append(copy(src.at[to * 2 + 1 - c], dst.at[mine_xc], slot + 4 + k, dev))
            made[-1].start()
        return made

    pz_start, pz_recv, pz_sent = over_z(p2, pz2, Z_P)
    lax.fori_loop(1, NZ, pz_start, 0)
    pz2[z] = p2[z]
    wo[...] = jnp.zeros((192, 1024), BF16)
    for one in loads[3:]:
        one.wait()
    wo[0:172, :] = w_out_ref[...]

    count = count_ref[0]

    def spread(field, near, wide):
        near.wait_recv()
        for i, part in enumerate(split(field[pl.ds(8 * (1 - c), 4)])):
            parts[pl.ds(8 * (1 - c), 4), pl.ds(32 * i, 32)] = part
        wide.wait_recv()
        for i, part in enumerate(split(field[pl.ds(8 * c, 4)])):
            parts[pl.ds(8 * c, 4), pl.ds(32 * i, 32)] = part

        def slots(i, sums):
            for u in range(5):
                s = i * 5 + u
                at = jnp.minimum((col_ref[s] - 4 * d + 4) & 511, 11)
                product = lax.dot_general(
                    parts[at], tiles[s], TRAILING, preferred_element_type=F32
                )
                total = product[0:32] + product[32:64] + product[64:96]
                row = jnp.where(s < count, row_ref[s], -1)
                sums = tuple(
                    v + jnp.where(row == b, 1.0, 0.0) * total for b, v in enumerate(sums)
                )
            return sums

        zero = jnp.zeros((32, 128), F32)
        return jnp.stack(lax.fori_loop(0, 8, slots, (zero,) * 4))

    first = spread(ext, near, wide)
    ext_two[4:8] = first
    near, wide = halo(ext_two, HALO_TWO)
    copies += [near, wide]
    for i, part in enumerate(split(first)):
        parts[4:8, pl.ds(32 * i, 32)] = part
    lax.fori_loop(1, NZ, pz_recv, 0)
    for i in range(8):
        px[i] = pz2[:, i, :]
    xc_p = over_xc(px, pq, XC_P)
    pq[mine_xc] = px[mine_xc]
    copies += xc_p
    second = spread(ext_two, near, wide)
    second = 2.0 * second - ext[4:8]
    diffused = series_zero * ext[4:8] + series_one * ext_two[4:8] + series_two * second

    for i, part in enumerate(split(diffused)):
        for b in range(4):
            moved[pl.ds(32 * i, 32), pl.ds(128 * b, 128)] = part[b]
    sorted_rows = lax.dot_general(moved[...], hot[...], TRAILING, preferred_element_type=F32)
    columns = sorted_rows[0:32] + sorted_rows[32:64] + sorted_rows[64:96]
    for i in range(NY):
        amsg[i] = columns[:, 128 * i : 128 * i + 128]
    rep_x = []
    for k in (2, 1, 3):
        to = (y + k) % NY
        rep_x.append(copy(amsg.at[to], rf.at[y], REP_X + k, ys[k - 1]))
        rep_x[-1].start()
    rf[y] = amsg[y]
    for one in xc_p:
        one.wait_recv()
    at_lane = lax.broadcasted_iota(jnp.int32, (128, 128), 1).astype(F32)
    put[...] = jnp.where(pq[...].reshape(128, 128) == at_lane, 1.0, 0.0).astype(BF16)
    for one in rep_x:
        one.wait_recv()
    t2[...] = rf[...].reshape(128, 128).T.reshape(NZ, 8, 128)
    zx_start, zx_recv, zx_sent = over_z(t2, rz2, Z_X)
    lax.fori_loop(1, NZ, zx_start, 0)
    rz2[z] = t2[z]
    lax.fori_loop(1, NZ, zx_recv, 0)
    for i in range(8):
        rx[i] = rz2[:, i, :]
    xc_x = over_xc(rx, rq, XC_X)
    rq[mine_xc] = rx[mine_xc]
    for one in xc_x:
        one.wait_recv()
    copies += rep_x + xc_x
    lines = jnp.concatenate(split(rq[...].reshape(128, 128).T), axis=0)
    placed = jnp.dot(lines, put[...], preferred_element_type=F32)
    batch = placed[0:128] + placed[128:256] + placed[256:384]
    out_x[...] = batch

    x2[c] = batch
    ex_x = copy(x2.at[c], x2.at[c], EX_X, partner)
    ex_x.start()
    ex_c.wait_recv()
    for i in range(2):
        ct[pl.ds(128 * i, 128), :] = cot2[i].T.astype(BF16)
    ex_x.wait_recv()
    for i in range(2):
        xt[pl.ds(128 * i, 128), :] = x2[i].T.astype(BF16)

    for j in range(4):
        cols = pl.ds(256 * j, 256)
        pre = jnp.dot(xt[...], w_in_ref[:, cols], preferred_element_type=F32)
        g = sigmoid(pre)
        h1[:, cols] = (pre * g).astype(BF16)
        slope1[j] = g * (1.0 + pre * (1.0 - g))
    half = lanes(c, 512)
    pre_two = jnp.dot(h1[...], w_mid_ref[:, half], preferred_element_type=F32)
    g_two = sigmoid(pre_two)
    h2 = (pre_two * g_two).astype(BF16)
    back_two = jnp.dot(ct[...], wo[:, half], preferred_element_type=F32)
    d2[...] = (back_two * (g_two * (1.0 + pre_two * (1.0 - g_two)))).astype(BF16)

    send_b[...] = lax.dot_general(
        d2[...], w_mid_ref[lanes(1 - c, 512), half], TRAILING, preferred_element_type=F32
    )
    ex_b = copy(send_b, recv_b, EX_B, partner)
    ex_b.start()

    copies += [ex_x, ex_b]
    cot_rows = [cot2[i].astype(BF16) for i in range(2)]
    grad_out = jnp.dot(
        jnp.concatenate(cot_rows, axis=1), h2, preferred_element_type=F32
    ).reshape(24, 8, 512)
    io[16:40] = grad_out
    own_back = lax.dot_general(
        d2[...], w_mid_ref[half, half], TRAILING, preferred_element_type=F32
    )
    ex_b.wait_recv()
    slope = jnp.concatenate([slope1[2 * c], slope1[2 * c + 1]], axis=1)
    delta_one = ((own_back + recv_b[...]) * slope).astype(BF16)
    x_rows = jnp.concatenate([x2[i].astype(BF16) for i in range(2)], axis=1)
    grad_in = jnp.dot(x_rows, delta_one, preferred_element_type=F32).reshape(16, 8, 512)
    io[0:16] = grad_in

    def send(src, dst, slot, dev):
        one = copy(src, dst, slot, dev)
        one.start()
        copies.append(one)
        return one

    def arrive(made):
        for one in made:
            one.wait_recv()

    first_a, first_b = [], []
    for k in (2, 1, 3):
        first_a.append(
            send(io.at[pl.ds((x + k) % NX * 5, 5)], ra_io.at[k - 1], A_IO + k - 1, xs[k - 1])
        )
        first_b.append(
            send(
                io.at[pl.ds(20, 20), :, lanes((y + k) % NY, 128)],
                rb_io.at[k - 1], B_IO + k - 1, ys[k - 1],
            )
        )

    mid_a, mid_b = [], []
    for k in (2, 1, 3, 0):
        to = (x + k) % NX
        rows = lax.dot_general(
            h1[:, lanes(to, 256)], d2[...], LEADING, preferred_element_type=F32
        ).reshape(NZ, 2, 8, 512)
        mid[0, to] = rows[:, 0]
        mid[1, to] = rows[:, 1]
        if k:
            mid_a.append(send(mid.at[0, to], ra_mid.at[k - 1], A_MID + k - 1, xs[k - 1]))
    for k in (2, 1, 3):
        mid_b.append(
            send(
                mid.at[1, :, :, :, lanes((y + k) % NY, 128)],
                rb_mid.at[k - 1], B_MID + k - 1, ys[k - 1],
            )
        )

    y_lane = lanes(y, 128)
    two_io = []
    arrive(first_a)
    sai[...] = io[pl.ds(x * 5, 5)] + ra_io[0] + ra_io[1] + ra_io[2]
    for k in (2, 1, 3):
        two_io.append(
            send(sai.at[:, :, lanes((y + k) % NY, 128)], r2ai.at[k - 1], A_TWO_IO + k - 1, ys[k - 1])
        )
    arrive(first_b)
    sbi[...] = io[20:40, :, y_lane] + rb_io[0] + rb_io[1] + rb_io[2]
    for k in (2, 1, 3):
        two_io.append(
            send(sbi.at[pl.ds((x + k) % NX * 5, 5)], r2bi.at[k - 1], B_TWO_IO + k - 1, xs[k - 1])
        )
    arrive(two_io)
    io_a = sai[:, :, y_lane] + r2ai[0] + r2ai[1] + r2ai[2]
    io_b = sbi[pl.ds(x * 5, 5)] + r2bi[0] + r2bi[1] + r2bi[2]

    group, spot_z = z // 4, z % 4
    tiles_io = [io_a[t] for t in range(5)] + [io_b[t] for t in range(5)]
    tiles_io += [jnp.zeros((8, 128), F32)] * 2
    for i in range(4):
        for t in range(3):
            zi[i, t] = tiles_io[4 * t + i]
    near_z = [place(x, y, group * 4 + (spot_z + k) % 4, c) for k in range(1, 4)]
    far_z = [place(x, y, (z + 4 * k) % NZ, c) for k in range(1, 4)]
    third_io = []
    for k in (2, 1, 3):
        third_io.append(
            send(zi.at[(spot_z + k) % 4], rzi.at[k - 1], Z_ONE_IO + k, near_z[k - 1])
        )
    arrive(third_io)
    rzi_two[group] = zi[spot_z] + rzi[0] + rzi[1] + rzi[2]
    across_io = []
    for k in (2, 1, 3):
        across_io.append(
            send(rzi_two.at[group], rzi_two.at[group], Z_TWO_IO + k, far_z[k - 1])
        )

    two = []
    arrive(mid_a)
    sa[...] = mid[0, x] + ra_mid[0] + ra_mid[1] + ra_mid[2]
    for k in (2, 1, 3):
        two.append(
            send(sa.at[:, :, lanes((y + k) % NY, 128)], r2a.at[k - 1], A_TWO + k - 1, ys[k - 1])
        )
    arrive(mid_b)
    for i in range(NX):
        sb[i] = mid[1, i, :, :, y_lane] + rb_mid[0, i] + rb_mid[1, i] + rb_mid[2, i]
    for k in (2, 1, 3):
        two.append(send(sb.at[(x + k) % NX], r2b.at[k - 1], B_TWO + k - 1, xs[k - 1]))

    arrive(across_io)
    mine_io[...] = ((rzi_two[0] + rzi_two[1]) + rzi_two[2]) + rzi_two[3]
    share = []
    for k in (2, 1, 3):
        share.append(send(mine_io, ri.at[spot_z], Z_ALL + k, near_z[k - 1]))
    ri[spot_z] = mine_io[...]

    arrive(two)
    sum_a = sa[:, :, y_lane] + r2a[0] + r2a[1] + r2a[2]
    sum_b = sb[x] + r2b[0] + r2b[1] + r2b[2]
    for i in range(4):
        for g in range(4):
            zs[i, g] = sum_a[4 * g + i]
            zs[i, 4 + g] = sum_b[4 * g + i]
    third = []
    for k in (2, 1, 3):
        third.append(send(zs.at[(spot_z + k) % 4], rz.at[k - 1], Z_ONE + k, near_z[k - 1]))

    arrive(share)
    tile = lanes(c * NY + y, 128)
    rows_a, rows_b = pl.ds(x * 5, 5), pl.ds((NX + x) * 5, 5)
    for t in range(10):
        full[(t // 5 * NX + x) * 5 + t % 5, :, tile] = ri[t % 4, t // 4]
    gather = []
    for k in (2, 1, 3):
        spot = full.at[rows_a, :, tile]
        gather.append(send(spot, spot, A_THREE + k - 1, ys[k - 1]))
        spot = full.at[rows_b, :, tile]
        gather.append(send(spot, spot, B_THREE + k - 1, xs[k - 1]))

    arrive(third)
    grouped = zs[spot_z] + rz[0] + rz[1] + rz[2]
    for g in range(4):
        zs_two[g, 0] = grouped[g]
        zs_two[g, 1] = grouped[4 + g]
    across = []
    for k in (2, 1, 3):
        across.append(
            send(zs_two.at[(group + k) % 4], rz_two.at[k - 1], Z_TWO + k, far_z[k - 1])
        )

    arrive(gather)
    fourth = []
    for k in (2, 1, 3):
        spot = full.at[rows_a, :, half]
        fourth.append(send(spot, spot, A_FOUR + k - 1, xs[k - 1]))
        spot = full.at[pl.ds(20, 20), :, tile]
        fourth.append(send(spot, spot, B_FOUR + k - 1, ys[k - 1]))
    arrive(fourth)
    spot = full.at[:, :, half]
    pair = send(spot, spot, PAIR, partner)

    arrive(across)
    mine[...] = zs_two[group] + rz_two[0] + rz_two[1] + rz_two[2]
    last = []
    for k in range(NY):
        if k:
            last.append(send(mine.at[c], r4.at[c, y], MID_ALL + k, ys[k - 1]))
        last.append(
            send(
                mine.at[1 - c], r4.at[c, y], MID_ALL + 4 + k, yo[k - 1] if k else partner
            )
        )
    r4[c, y] = mine[c]
    pair.wait_recv()
    out_in[...] = full[0:16].reshape(128, 1024)
    out_out[...] = full[16:40].reshape(192, 1024)[0:172]
    arrive(last)
    for i in range(8):
        out_mid[:, pl.ds(128 * i, 128)] = r4[i // 4, i % 4]

    lax.fori_loop(1, NZ, pz_sent, 0)
    lax.fori_loop(1, NZ, zx_sent, 0)
    for one in copies:
        one.wait_send()


def train(tile_row, tile_col, tile_count, features, tiles, dest, cotangent, w_in, w_mid, w_out):
    vmem = pl.BlockSpec(memory_space=pltpu.VMEM)
    hbm = pl.BlockSpec(memory_space=pltpu.HBM)
    buf = pltpu.VMEM
    return pl.pallas_call(
        train_kernel,
        out_shape=(
            jax.ShapeDtypeStruct((128, 128), F32),
            jax.ShapeDtypeStruct((128, 1024), F32),
            jax.ShapeDtypeStruct((8, 1024), F32),
            jax.ShapeDtypeStruct((172, 1024), F32),
        ),
        in_specs=[pl.BlockSpec(memory_space=pltpu.SMEM)] + [hbm] * 9,
        out_specs=(vmem,) * 4,
        scratch_shapes=[
            pltpu.SMEM((40,), jnp.int32),
            pltpu.SMEM((40,), jnp.int32),
            buf((32, 512), F32),
            buf((40, 128, 128), BF16),
            buf((4, 128), jnp.int32),
            buf((172, 128), BF16),
            buf((128, 1024), BF16),
            buf((1024, 1024), BF16),
            buf((172, 1024), BF16),
            buf((12, 32, 128), F32),
            buf((12, 32, 128), F32),
            buf((12, 96, 128), BF16),
            buf((512, 512), BF16),
            buf((96, 512), BF16),
            buf((128, 512), BF16),
            buf((NY, 32, 128), F32),
            buf((NY, 32, 128), F32),
            buf((NZ, 8, 128), F32),
            buf((NZ, 8, 128), F32),
            buf((8, NZ, 128), F32),
            buf((8, NZ, 128), F32),
            buf((NZ, 8, 128), F32),
            buf((NZ, 8, 128), F32),
            buf((8, NZ, 128), F32),
            buf((8, NZ, 128), F32),
            buf((128, 128), BF16),
            buf((2, 128, 128), F32),
            buf((2, 192, 128), F32),
            buf((256, 128), BF16),
            buf((256, 192), BF16),
            buf((192, 1024), BF16),
            buf((256, 1024), BF16),
            buf((4, 256, 256), F32),
            buf((256, 512), BF16),
            buf((256, 512), F32),
            buf((256, 512), F32),
            buf((2, NX, NZ, 8, 512), F32),
            buf((40, 8, 512), F32),
            buf((3, NZ, 8, 512), F32),
            buf((3, 5, 8, 512), F32),
            buf((3, NX, NZ, 8, 128), F32),
            buf((3, 20, 8, 128), F32),
            buf((NZ, 8, 512), F32),
            buf((NX, NZ, 8, 128), F32),
            buf((3, NZ, 8, 128), F32),
            buf((3, NZ, 8, 128), F32),
            buf((4, 8, 8, 128), F32),
            buf((3, 8, 8, 128), F32),
            buf((4, 2, 8, 128), F32),
            buf((3, 2, 8, 128), F32),
            buf((2, 8, 128), F32),
            buf((4, 3, 8, 128), F32),
            buf((2, NY, 8, 128), F32),
            buf((40, 8, 1024), F32),
            buf((5, 8, 512), F32),
            buf((20, 8, 128), F32),
            buf((3, 5, 8, 128), F32),
            buf((3, 5, 8, 128), F32),
            buf((4, 3, 8, 128), F32),
            buf((3, 3, 8, 128), F32),
            buf((4, 3, 8, 128), F32),
            buf((3, 8, 128), F32),
            pltpu.SemaphoreType.DMA((SEMS,)),
            pltpu.SemaphoreType.DMA((SEMS,)),
            pltpu.SemaphoreType.DMA((9,)),
        ],
        compiler_params=pltpu.CompilerParams(
            collective_id=0, has_side_effects=True, vmem_limit_bytes=46 * 1024 * 1024
        ),
    )(tile_count, *(pltpu.with_memory_space_constraint(v, pltpu.HBM) for v in (
        tile_row, tile_col, features, tiles, dest, cotangent, w_in, w_mid, w_out
    )))


def shards(
    features, tiles, tile_row, tile_col, tile_count, dest_slot, w_in, w_mid, w_out, cotangent
):
    dest = dest_slot.reshape(4, 128)
    return train(
        tile_row, tile_col, tile_count, features, tiles, dest, cotangent, w_in, w_mid, w_out
    )


def solution(mesh):
    in_specs = (
        P("rep", "dom"),
        P("dom", None, None),
        P("dom"),
        P("dom"),
        P("dom"),
        P("dom"),
        P(),
        P(),
        P(),
        P(None, ("dom", "rep")),
    )
    out_specs = (P(None, ("dom", "rep")), P(), P("dom", None), P())
    return jax.shard_map(shards, mesh=mesh, in_specs=in_specs, out_specs=out_specs, check_vma=False)
```

```python
import jax
import jax.numpy as jnp
from jax import lax
from jax.experimental import pallas as pl
from jax.experimental.pallas import tpu as pltpu
from jax.sharding import PartitionSpec as P

series_zero = 0.3085083
series_one = -0.4305395
series_two = 0.1864784
LEADING = (((0,), (0,)), ((), ()))
TRAILING = (((1,), (1,)), ((), ()))
MESH = pl.DeviceIdType.MESH
NX, NY, NZ = 4, 4, 16
F32 = jnp.float32
BF16 = jnp.bfloat16


EX_X, EX_C, EX_B = 0, 1, 2
A_IO, B_IO = 6, 12
A_TWO, B_TWO = 15, 18
Z_ONE, Z_TWO, Z_ALL = 21, 25, 29
MID_ALL = 53
A_THREE, B_THREE, A_FOUR, B_FOUR, PAIR = 61, 64, 67, 70, 73
HALO_ONE, HALO_TWO = 74, 76
REP_X, Z_X, XC_X = 78, 82, 98
Z_P, XC_P = 106, 122
A_TWO_IO, B_TWO_IO, Z_ONE_IO, Z_TWO_IO = 130, 133, 136, 140
MID_ONE = 144
SEMS = 154


def sigmoid(v):
    return 0.5 + 0.5 * jnp.tanh(0.5 * v)


def split(v):
    high = v.astype(BF16)
    rest = v - high.astype(F32)
    middle = rest.astype(BF16)
    low = (rest - middle.astype(F32)).astype(BF16)
    return high, middle, low


def train_kernel(
    count_ref, row_hbm, col_hbm, feat_hbm, tiles_hbm, dest_hbm, cot_hbm, w_in_hbm, w_mid_hbm, w_out_hbm,
    out_x, out_in, out_mid, out_out,
    row_ref, col_ref, feat, tiles, dest, cot, w_in_ref, w_mid_ref, w_out_ref,
    ext, ext_two, parts, hot, moved, within, amsg, rf, t2, rz2, rx, rq, p2, pz2, px, pq, put,
    x2, cot2, xt, ct, wo, h1, slope1, d2, send_b, recv_b,
    mid, io, ra_mid, ra_io, rb_mid, rb_io, sa, sb, r2a, r2b, zs, rz, zs_two, rz_two, mine, ri, r4, full,
    sai, sbi, r2ai, r2bi, zi, rzi, rzi_two, mine_io,
    ssem, rsem, lsem,
):
    loads = []
    for i, (src, dst) in enumerate((
        (feat_hbm, feat), (dest_hbm, dest), (cot_hbm, cot), (row_hbm, row_ref),
        (col_hbm, col_ref), (tiles_hbm, tiles),
        (w_in_hbm, w_in_ref), (w_out_hbm, w_out_ref), (w_mid_hbm, w_mid_ref),
    )):
        loads.append(pltpu.make_async_copy(src, dst, lsem.at[i]))
        loads[-1].start()
    d = lax.axis_index("dom")
    y = lax.axis_index("rep")
    c = d % 2
    z = (d // 2) % NZ
    x = d // (2 * NZ)

    def place(xx, yy, zz, cc):
        return ((xx * NZ + zz) * 2 + cc, yy)

    def copy(src, dst, slot, dev):
        return pltpu.make_async_remote_copy(
            src_ref=src, dst_ref=dst, send_sem=ssem.at[slot], recv_sem=rsem.at[slot],
            device_id=dev, device_id_type=MESH,
        )

    def lanes(index, width):
        return pl.ds(pl.multiple_of(index * width, width), width)

    partner = place(x, y, z, 1 - c)
    far = ((d + 2 * c - 1 + 2 * NX * NZ) % (2 * NX * NZ), y)
    xs = [place((x + k) % NX, y, z, c) for k in range(1, NX)]
    xo = [place((x + k) % NX, y, z, 1 - c) for k in range(1, NX)]
    ys = [place(x, (y + k) % NY, z, c) for k in range(1, NY)]
    yo = [place(x, (y + k) % NY, z, 1 - c) for k in range(1, NY)]
    barrier = pltpu.get_barrier_semaphore()
    for dev in [partner, far] + xs + xo + ys + yo:
        pl.semaphore_signal(barrier, inc=1, device_id=dev, device_id_type=MESH)

    def greet(k, carry):
        pl.semaphore_signal(
            barrier, inc=1, device_id=place(x, y, (z + k) % NZ, c), device_id_type=MESH
        )
        return carry

    lax.fori_loop(1, NZ, greet, 0)

    for one in loads[:3]:
        one.wait()
    own = jnp.stack([feat[:, pl.ds(128 * b, 128)] for b in range(4)])
    ext[4:8] = own
    for i, part in enumerate(split(own)):
        parts[4:8, pl.ds(32 * i, 32)] = part
    cot2[c] = jnp.zeros((192, 128), F32)
    cot2[c, 0:172] = cot[...].astype(F32)
    j = lax.broadcasted_iota(jnp.int32, (512, 128), 0)
    target = ((((j >> 1) & 3) * NZ + ((j >> 3) & 15)) * 2 + (j & 1)) * NY + (j >> 7)
    for b in range(4):
        line = dest[pl.ds(b, 1), :]
        hot[:, pl.ds(128 * b, 128)] = jnp.where(target == (line >> 7), 1.0, 0.0).astype(BF16)
        within[:, pl.ds(128 * b, 128)] = jnp.broadcast_to(
            (line & 127).astype(F32), (128, 128)
        ).astype(BF16)

    p2[...] = lax.dot_general(
        hot[lanes(y, 128), :], within[...], TRAILING, preferred_element_type=F32
    ).reshape(NZ, 8, 128)
    pl.semaphore_wait(barrier, 2 + 3 + 3 + 3 + 3 + NZ - 1)

    def halo(field, slot):
        one = copy(field.at[pl.ds(4, 4)], field.at[pl.ds(8 * c, 4)], slot, partner)
        two = copy(field.at[pl.ds(4, 4)], field.at[pl.ds(8 * (1 - c), 4)], slot + 1, far)
        two.start()
        one.start()
        return one, two

    near, wide = halo(ext, HALO_ONE)
    ex_c = copy(cot2.at[c], cot2.at[c], EX_C, partner)
    ex_c.start()
    copies = [near, wide, ex_c]
    mine_xc = x * 2 + c

    def over_z(src, dst, slot):
        def one(k):
            to = (z + k) % NZ
            return copy(src.at[to], dst.at[z], slot + k, place(x, y, to, c))

        def start(k, carry):
            one(k).start()
            return carry

        def recv(k, carry):
            one(k).wait_recv()
            return carry

        def sent(k, carry):
            one(k).wait_send()
            return carry

        return start, recv, sent

    def over_xc(src, dst, slot):
        made = []
        for k in (2, 1, 3, 0):
            to = (x + k) % NX
            if k:
                made.append(copy(src.at[to * 2 + c], dst.at[mine_xc], slot + k, xs[k - 1]))
                made[-1].start()
            dev = xo[k - 1] if k else partner
            made.append(copy(src.at[to * 2 + 1 - c], dst.at[mine_xc], slot + 4 + k, dev))
            made[-1].start()
        return made

    pz_start, pz_recv, pz_sent = over_z(p2, pz2, Z_P)
    lax.fori_loop(1, NZ, pz_start, 0)
    pz2[z] = p2[z]
    wo[...] = jnp.zeros((192, 1024), BF16)
    for one in loads[3:]:
        one.wait()
    wo[0:172, :] = w_out_ref[...]

    count = count_ref[0]

    def spread(field, near, wide):
        near.wait_recv()
        for i, part in enumerate(split(field[pl.ds(8 * (1 - c), 4)])):
            parts[pl.ds(8 * (1 - c), 4), pl.ds(32 * i, 32)] = part
        wide.wait_recv()
        for i, part in enumerate(split(field[pl.ds(8 * c, 4)])):
            parts[pl.ds(8 * c, 4), pl.ds(32 * i, 32)] = part

        def slots(i, sums):
            for u in range(5):
                s = i * 5 + u
                at = jnp.minimum((col_ref[s] - 4 * d + 4) & 511, 11)
                product = lax.dot_general(
                    parts[at], tiles[s], TRAILING, preferred_element_type=F32
                )
                total = product[0:32] + product[32:64] + product[64:96]
                row = jnp.where(s < count, row_ref[s], -1)
                sums = tuple(
                    v + jnp.where(row == b, 1.0, 0.0) * total for b, v in enumerate(sums)
                )
            return sums

        zero = jnp.zeros((32, 128), F32)
        return jnp.stack(lax.fori_loop(0, 8, slots, (zero,) * 4))

    first = spread(ext, near, wide)
    ext_two[4:8] = first
    near, wide = halo(ext_two, HALO_TWO)
    copies += [near, wide]
    for i, part in enumerate(split(first)):
        parts[4:8, pl.ds(32 * i, 32)] = part
    lax.fori_loop(1, NZ, pz_recv, 0)
    for i in range(8):
        px[i] = pz2[:, i, :]
    xc_p = over_xc(px, pq, XC_P)
    pq[mine_xc] = px[mine_xc]
    copies += xc_p
    second = spread(ext_two, near, wide)
    second = 2.0 * second - ext[4:8]
    diffused = series_zero * ext[4:8] + series_one * ext_two[4:8] + series_two * second

    for i, part in enumerate(split(diffused)):
        for b in range(4):
            moved[pl.ds(32 * i, 32), pl.ds(128 * b, 128)] = part[b]
    sorted_rows = lax.dot_general(moved[...], hot[...], TRAILING, preferred_element_type=F32)
    columns = sorted_rows[0:32] + sorted_rows[32:64] + sorted_rows[64:96]
    for i in range(NY):
        amsg[i] = columns[:, 128 * i : 128 * i + 128]
    rep_x = []
    for k in (2, 1, 3):
        to = (y + k) % NY
        rep_x.append(copy(amsg.at[to], rf.at[y], REP_X + k, ys[k - 1]))
        rep_x[-1].start()
    rf[y] = amsg[y]
    for one in xc_p:
        one.wait_recv()
    at_lane = lax.broadcasted_iota(jnp.int32, (128, 128), 1).astype(F32)
    put[...] = jnp.where(pq[...].reshape(128, 128) == at_lane, 1.0, 0.0).astype(BF16)
    for one in rep_x:
        one.wait_recv()
    t2[...] = rf[...].reshape(128, 128).T.reshape(NZ, 8, 128)
    zx_start, zx_recv, zx_sent = over_z(t2, rz2, Z_X)
    lax.fori_loop(1, NZ, zx_start, 0)
    rz2[z] = t2[z]
    lax.fori_loop(1, NZ, zx_recv, 0)
    for i in range(8):
        rx[i] = rz2[:, i, :]
    xc_x = over_xc(rx, rq, XC_X)
    rq[mine_xc] = rx[mine_xc]
    for one in xc_x:
        one.wait_recv()
    copies += rep_x + xc_x
    lines = jnp.concatenate(split(rq[...].reshape(128, 128).T), axis=0)
    placed = jnp.dot(lines, put[...], preferred_element_type=F32)
    batch = placed[0:128] + placed[128:256] + placed[256:384]
    out_x[...] = batch

    x2[c] = batch
    ex_x = copy(x2.at[c], x2.at[c], EX_X, partner)
    ex_x.start()
    ex_c.wait_recv()
    for i in range(2):
        ct[pl.ds(128 * i, 128), :] = cot2[i].T.astype(BF16)
    ex_x.wait_recv()
    for i in range(2):
        xt[pl.ds(128 * i, 128), :] = x2[i].T.astype(BF16)

    for j in range(4):
        cols = pl.ds(256 * j, 256)
        pre = jnp.dot(xt[...], w_in_ref[:, cols], preferred_element_type=F32)
        g = sigmoid(pre)
        h1[:, cols] = (pre * g).astype(BF16)
        slope1[j] = g * (1.0 + pre * (1.0 - g))
    half = lanes(c, 512)
    pre_two = jnp.dot(h1[...], w_mid_ref[:, half], preferred_element_type=F32)
    g_two = sigmoid(pre_two)
    h2 = (pre_two * g_two).astype(BF16)
    back_two = jnp.dot(ct[...], wo[:, half], preferred_element_type=F32)
    d2[...] = (back_two * (g_two * (1.0 + pre_two * (1.0 - g_two)))).astype(BF16)

    send_b[...] = lax.dot_general(
        d2[...], w_mid_ref[lanes(1 - c, 512), half], TRAILING, preferred_element_type=F32
    )
    ex_b = copy(send_b, recv_b, EX_B, partner)
    ex_b.start()

    copies += [ex_x, ex_b]
    cot_rows = [cot2[i].astype(BF16) for i in range(2)]
    grad_out = jnp.dot(
        jnp.concatenate(cot_rows, axis=1), h2, preferred_element_type=F32
    ).reshape(24, 8, 512)
    io[16:40] = grad_out
    own_back = lax.dot_general(
        d2[...], w_mid_ref[half, half], TRAILING, preferred_element_type=F32
    )
    ex_b.wait_recv()
    slope = jnp.concatenate([slope1[2 * c], slope1[2 * c + 1]], axis=1)
    delta_one = ((own_back + recv_b[...]) * slope).astype(BF16)
    x_rows = jnp.concatenate([x2[i].astype(BF16) for i in range(2)], axis=1)
    grad_in = jnp.dot(x_rows, delta_one, preferred_element_type=F32).reshape(16, 8, 512)
    io[0:16] = grad_in

    def send(src, dst, slot, dev):
        one = copy(src, dst, slot, dev)
        one.start()
        copies.append(one)
        return one

    def arrive(made):
        for one in made:
            one.wait_recv()

    first_a, first_b = [], []
    for k in (2, 1, 3):
        first_a.append(
            send(io.at[pl.ds((x + k) % NX * 5, 5)], ra_io.at[k - 1], A_IO + k - 1, xs[k - 1])
        )
        first_b.append(
            send(
                io.at[pl.ds(20, 20), :, lanes((y + k) % NY, 128)],
                rb_io.at[k - 1], B_IO + k - 1, ys[k - 1],
            )
        )

    mid_a, mid_b = [], []
    for k in (2, 1, 3, 0):
        to = (x + k) % NX
        rows = lax.dot_general(
            h1[:, lanes(to, 256)], d2[...], LEADING, preferred_element_type=F32
        ).reshape(NZ, 2, 8, 512)
        mid[0, to] = rows[:, 0]
        mid[1, to] = rows[:, 1]

    def send_mid(k, part, slot):
        rows = pl.ds(*part)
        mid_a.append(
            send(
                mid.at[0, (x + k) % NX, rows], ra_mid.at[k - 1, rows], slot, xs[k - 1]
            )
        )
        blocks = pl.ds(part[0] // 4, part[1] // 4)
        mid_b.append(
            send(
                mid.at[1, blocks, :, :, lanes((y + k) % NY, 128)],
                rb_mid.at[k - 1, blocks], slot + 1, ys[k - 1],
            )
        )

    send_mid(1, (0, 8), MID_ONE)
    send_mid(3, (0, 8), MID_ONE + 2)

    y_lane = lanes(y, 128)
    two_io = []
    arrive(first_a)
    sai[...] = io[pl.ds(x * 5, 5)] + ra_io[0] + ra_io[1] + ra_io[2]
    for k in (2, 1, 3):
        two_io.append(
            send(sai.at[:, :, lanes((y + k) % NY, 128)], r2ai.at[k - 1], A_TWO_IO + k - 1, ys[k - 1])
        )
    arrive(first_b)
    sbi[...] = io[20:40, :, y_lane] + rb_io[0] + rb_io[1] + rb_io[2]
    for k in (2, 1, 3):
        two_io.append(
            send(sbi.at[pl.ds((x + k) % NX * 5, 5)], r2bi.at[k - 1], B_TWO_IO + k - 1, xs[k - 1])
        )
    send_mid(2, (0, 16), MID_ONE + 4)
    send_mid(1, (8, 8), MID_ONE + 6)
    send_mid(3, (8, 8), MID_ONE + 8)
    arrive(two_io)
    io_a = sai[:, :, y_lane] + r2ai[0] + r2ai[1] + r2ai[2]
    io_b = sbi[pl.ds(x * 5, 5)] + r2bi[0] + r2bi[1] + r2bi[2]

    group, spot_z = z // 4, z % 4
    tiles_io = [io_a[t] for t in range(5)] + [io_b[t] for t in range(5)]
    tiles_io += [jnp.zeros((8, 128), F32)] * 2
    for i in range(4):
        for t in range(3):
            zi[i, t] = tiles_io[4 * t + i]
    near_z = [place(x, y, group * 4 + (spot_z + k) % 4, c) for k in range(1, 4)]
    far_z = [place(x, y, (z + 4 * k) % NZ, c) for k in range(1, 4)]
    third_io = []
    for k in (2, 1, 3):
        third_io.append(
            send(zi.at[(spot_z + k) % 4], rzi.at[k - 1], Z_ONE_IO + k, near_z[k - 1])
        )
    arrive(third_io)
    rzi_two[group] = zi[spot_z] + rzi[0] + rzi[1] + rzi[2]
    across_io = []
    for k in (2, 1, 3):
        across_io.append(
            send(rzi_two.at[group], rzi_two.at[group], Z_TWO_IO + k, far_z[k - 1])
        )

    two = []
    arrive(mid_a)
    sa[...] = mid[0, x] + ra_mid[0] + ra_mid[1] + ra_mid[2]
    for k in (2, 1, 3):
        two.append(
            send(sa.at[:, :, lanes((y + k) % NY, 128)], r2a.at[k - 1], A_TWO + k - 1, ys[k - 1])
        )
    arrive(mid_b)
    for i in range(NX):
        sb[i] = mid[1, i, :, :, y_lane] + rb_mid[0, i] + rb_mid[1, i] + rb_mid[2, i]
    for k in (2, 1, 3):
        two.append(send(sb.at[(x + k) % NX], r2b.at[k - 1], B_TWO + k - 1, xs[k - 1]))

    arrive(across_io)
    mine_io[...] = ((rzi_two[0] + rzi_two[1]) + rzi_two[2]) + rzi_two[3]
    share = []
    for k in (2, 1, 3):
        share.append(send(mine_io, ri.at[spot_z], Z_ALL + k, near_z[k - 1]))
    ri[spot_z] = mine_io[...]

    arrive(two)
    sum_a = sa[:, :, y_lane] + r2a[0] + r2a[1] + r2a[2]
    sum_b = sb[x] + r2b[0] + r2b[1] + r2b[2]
    for i in range(4):
        for g in range(4):
            zs[i, g] = sum_a[4 * g + i]
            zs[i, 4 + g] = sum_b[4 * g + i]
    third = []
    for k in (2, 1, 3):
        third.append(send(zs.at[(spot_z + k) % 4], rz.at[k - 1], Z_ONE + k, near_z[k - 1]))

    arrive(share)
    tile = lanes(c * NY + y, 128)
    rows_a, rows_b = pl.ds(x * 5, 5), pl.ds((NX + x) * 5, 5)
    for t in range(10):
        full[(t // 5 * NX + x) * 5 + t % 5, :, tile] = ri[t % 4, t // 4]
    gather = []
    for k in (2, 1, 3):
        spot = full.at[rows_a, :, tile]
        gather.append(send(spot, spot, A_THREE + k - 1, ys[k - 1]))
        spot = full.at[rows_b, :, tile]
        gather.append(send(spot, spot, B_THREE + k - 1, xs[k - 1]))

    arrive(third)
    grouped = zs[spot_z] + rz[0] + rz[1] + rz[2]
    for g in range(4):
        zs_two[g, 0] = grouped[g]
        zs_two[g, 1] = grouped[4 + g]
    across = []
    for k in (2, 1, 3):
        across.append(
            send(zs_two.at[(group + k) % 4], rz_two.at[k - 1], Z_TWO + k, far_z[k - 1])
        )

    arrive(gather)
    fourth = []
    for k in (2, 1, 3):
        spot = full.at[rows_a, :, half]
        fourth.append(send(spot, spot, A_FOUR + k - 1, xs[k - 1]))
        spot = full.at[pl.ds(20, 20), :, tile]
        fourth.append(send(spot, spot, B_FOUR + k - 1, ys[k - 1]))
    arrive(fourth)
    spot = full.at[:, :, half]
    pair = send(spot, spot, PAIR, partner)

    arrive(across)
    mine[...] = zs_two[group] + rz_two[0] + rz_two[1] + rz_two[2]
    last = []
    for k in range(NY):
        if k:
            last.append(send(mine.at[c], r4.at[c, y], MID_ALL + k, ys[k - 1]))
        last.append(
            send(
                mine.at[1 - c], r4.at[c, y], MID_ALL + 4 + k, yo[k - 1] if k else partner
            )
        )
    r4[c, y] = mine[c]
    pair.wait_recv()
    out_in[...] = full[0:16].reshape(128, 1024)
    out_out[...] = full[16:40].reshape(192, 1024)[0:172]
    arrive(last)
    for i in range(8):
        out_mid[:, pl.ds(128 * i, 128)] = r4[i // 4, i % 4]

    lax.fori_loop(1, NZ, pz_sent, 0)
    lax.fori_loop(1, NZ, zx_sent, 0)
    for one in copies:
        one.wait_send()


def write_kernel(*refs):
    writes = [
        pltpu.make_async_copy(refs[i], refs[4 + i], refs[8].at[i]) for i in range(4)
    ]
    for one in writes:
        one.start()
    for one in writes:
        one.wait()


def train(tile_row, tile_col, tile_count, features, tiles, dest, cotangent, w_in, w_mid, w_out):
    vmem = pl.BlockSpec(memory_space=pltpu.VMEM)
    hbm = pl.BlockSpec(memory_space=pltpu.HBM)
    buf = pltpu.VMEM
    return pl.pallas_call(
        train_kernel,
        out_shape=(
            jax.ShapeDtypeStruct((128, 128), F32),
            jax.ShapeDtypeStruct((128, 1024), F32),
            jax.ShapeDtypeStruct((8, 1024), F32),
            jax.ShapeDtypeStruct((172, 1024), F32),
        ),
        in_specs=[pl.BlockSpec(memory_space=pltpu.SMEM)] + [hbm] * 9,
        out_specs=(vmem,) * 4,
        scratch_shapes=[
            pltpu.SMEM((40,), jnp.int32),
            pltpu.SMEM((40,), jnp.int32),
            buf((32, 512), F32),
            buf((40, 128, 128), BF16),
            buf((4, 128), jnp.int32),
            buf((172, 128), BF16),
            buf((128, 1024), BF16),
            buf((1024, 1024), BF16),
            buf((172, 1024), BF16),
            buf((12, 32, 128), F32),
            buf((12, 32, 128), F32),
            buf((12, 96, 128), BF16),
            buf((512, 512), BF16),
            buf((96, 512), BF16),
            buf((128, 512), BF16),
            buf((NY, 32, 128), F32),
            buf((NY, 32, 128), F32),
            buf((NZ, 8, 128), F32),
            buf((NZ, 8, 128), F32),
            buf((8, NZ, 128), F32),
            buf((8, NZ, 128), F32),
            buf((NZ, 8, 128), F32),
            buf((NZ, 8, 128), F32),
            buf((8, NZ, 128), F32),
            buf((8, NZ, 128), F32),
            buf((128, 128), BF16),
            buf((2, 128, 128), F32),
            buf((2, 192, 128), F32),
            buf((256, 128), BF16),
            buf((256, 192), BF16),
            buf((192, 1024), BF16),
            buf((256, 1024), BF16),
            buf((4, 256, 256), F32),
            buf((256, 512), BF16),
            buf((256, 512), F32),
            buf((256, 512), F32),
            buf((2, NX, NZ, 8, 512), F32),
            buf((40, 8, 512), F32),
            buf((3, NZ, 8, 512), F32),
            buf((3, 5, 8, 512), F32),
            buf((3, NX, NZ, 8, 128), F32),
            buf((3, 20, 8, 128), F32),
            buf((NZ, 8, 512), F32),
            buf((NX, NZ, 8, 128), F32),
            buf((3, NZ, 8, 128), F32),
            buf((3, NZ, 8, 128), F32),
            buf((4, 8, 8, 128), F32),
            buf((3, 8, 8, 128), F32),
            buf((4, 2, 8, 128), F32),
            buf((3, 2, 8, 128), F32),
            buf((2, 8, 128), F32),
            buf((4, 3, 8, 128), F32),
            buf((2, NY, 8, 128), F32),
            buf((40, 8, 1024), F32),
            buf((5, 8, 512), F32),
            buf((20, 8, 128), F32),
            buf((3, 5, 8, 128), F32),
            buf((3, 5, 8, 128), F32),
            buf((4, 3, 8, 128), F32),
            buf((3, 3, 8, 128), F32),
            buf((4, 3, 8, 128), F32),
            buf((3, 8, 128), F32),
            pltpu.SemaphoreType.DMA((SEMS,)),
            pltpu.SemaphoreType.DMA((SEMS,)),
            pltpu.SemaphoreType.DMA((9,)),
        ],
        compiler_params=pltpu.CompilerParams(
            collective_id=0, has_side_effects=True, vmem_limit_bytes=46 * 1024 * 1024
        ),
    )(tile_count, *(pltpu.with_memory_space_constraint(v, pltpu.HBM) for v in (
        tile_row, tile_col, features, tiles, dest, cotangent, w_in, w_mid, w_out
    )))


def shards(
    features, tiles, tile_row, tile_col, tile_count, dest_slot, w_in, w_mid, w_out, cotangent
):
    dest = dest_slot.reshape(4, 128)
    results = train(
        tile_row, tile_col, tile_count, features, tiles, dest, cotangent, w_in, w_mid, w_out
    )
    return pl.pallas_call(
        write_kernel,
        out_shape=tuple(jax.ShapeDtypeStruct(v.shape, v.dtype) for v in results),
        in_specs=[pl.BlockSpec(memory_space=pltpu.VMEM)] * 4,
        out_specs=(pl.BlockSpec(memory_space=pltpu.HBM),) * 4,
        scratch_shapes=[pltpu.SemaphoreType.DMA((4,))],
    )(*(pltpu.with_memory_space_constraint(v, pltpu.VMEM) for v in results))


def solution(mesh):
    in_specs = (
        P("rep", "dom"),
        P("dom", None, None),
        P("dom"),
        P("dom"),
        P("dom"),
        P("dom"),
        P(),
        P(),
        P(),
        P(None, ("dom", "rep")),
    )
    out_specs = (P(None, ("dom", "rep")), P(), P("dom", None), P())
    return jax.shard_map(shards, mesh=mesh, in_specs=in_specs, out_specs=out_specs, check_vma=False)
```

```python
import jax
import jax.numpy as jnp
from jax import lax
from jax.experimental import pallas as pl
from jax.experimental.pallas import tpu as pltpu
from jax.sharding import PartitionSpec as P

series_zero = 0.3085083
series_one = -0.4305395
series_two = 0.1864784
LEADING = (((0,), (0,)), ((), ()))
TRAILING = (((1,), (1,)), ((), ()))
MESH = pl.DeviceIdType.MESH
NX, NY, NZ = 4, 4, 16
F32 = jnp.float32
BF16 = jnp.bfloat16


EX_X, EX_C, EX_B = 0, 1, 2
A_IO, B_IO = 6, 12
A_TWO, B_TWO = 15, 18
Z_ONE, Z_TWO, Z_ALL = 21, 25, 29
MID_ALL = 53
A_THREE, B_THREE, A_FOUR, B_FOUR, PAIR = 61, 64, 67, 70, 73
HALO_ONE, HALO_TWO = 74, 76
REP_X, Z_X, XC_X = 78, 82, 98
Z_P, XC_P = 106, 122
A_TWO_IO, B_TWO_IO, Z_ONE_IO, Z_TWO_IO = 130, 133, 136, 140
MID_ONE = 144
SEMS = 154


def sigmoid(v):
    return 0.5 + 0.5 * jnp.tanh(0.5 * v)


def split(v):
    high = v.astype(BF16)
    rest = v - high.astype(F32)
    middle = rest.astype(BF16)
    low = (rest - middle.astype(F32)).astype(BF16)
    return high, middle, low


def train_kernel(
    count_ref, row_hbm, col_hbm, feat_hbm, tiles_hbm, dest_hbm, cot_hbm, w_in_hbm, w_mid_hbm, w_out_hbm,
    out_x, out_in, out_mid, out_out,
    row_ref, col_ref, feat, tiles, dest, cot, w_in_ref, w_mid_ref, w_out_ref,
    ext, ext_two, parts, hot, moved, within, amsg, rf, t2, rz2, rx, rq, p2, pz2, px, pq, put,
    x2, cot2, xt, ct, wo, h1, slope1, d2, send_b, recv_b,
    mid, io, ra_mid, ra_io, rb_mid, rb_io, sa, sb, r2a, r2b, zs, rz, zs_two, rz_two, mine, ri, r4, full,
    sai, sbi, r2ai, r2bi, zi, rzi, rzi_two, mine_io,
    ssem, rsem, lsem,
):
    loads = []
    for i, (src, dst) in enumerate((
        (feat_hbm, feat), (dest_hbm, dest), (cot_hbm, cot), (row_hbm, row_ref),
        (col_hbm, col_ref), (tiles_hbm, tiles),
        (w_in_hbm, w_in_ref), (w_out_hbm, w_out_ref), (w_mid_hbm, w_mid_ref),
    )):
        loads.append(pltpu.make_async_copy(src, dst, lsem.at[i]))
        loads[-1].start()
    d = lax.axis_index("dom")
    y = lax.axis_index("rep")
    c = d % 2
    z = (d // 2) % NZ
    x = d // (2 * NZ)

    def place(xx, yy, zz, cc):
        return ((xx * NZ + zz) * 2 + cc, yy)

    def copy(src, dst, slot, dev):
        return pltpu.make_async_remote_copy(
            src_ref=src, dst_ref=dst, send_sem=ssem.at[slot], recv_sem=rsem.at[slot],
            device_id=dev, device_id_type=MESH,
        )

    def lanes(index, width):
        return pl.ds(pl.multiple_of(index * width, width), width)

    partner = place(x, y, z, 1 - c)
    far = ((d + 2 * c - 1 + 2 * NX * NZ) % (2 * NX * NZ), y)
    xs = [place((x + k) % NX, y, z, c) for k in range(1, NX)]
    xo = [place((x + k) % NX, y, z, 1 - c) for k in range(1, NX)]
    ys = [place(x, (y + k) % NY, z, c) for k in range(1, NY)]
    yo = [place(x, (y + k) % NY, z, 1 - c) for k in range(1, NY)]
    barrier = pltpu.get_barrier_semaphore()
    for dev in [partner, far] + xs + xo + ys + yo:
        pl.semaphore_signal(barrier, inc=1, device_id=dev, device_id_type=MESH)

    def greet(k, carry):
        pl.semaphore_signal(
            barrier, inc=1, device_id=place(x, y, (z + k) % NZ, c), device_id_type=MESH
        )
        return carry

    lax.fori_loop(1, NZ, greet, 0)

    for one in loads[:3]:
        one.wait()
    own = jnp.stack([feat[:, pl.ds(128 * b, 128)] for b in range(4)])
    ext[4:8] = own
    for i, part in enumerate(split(own)):
        parts[4:8, pl.ds(32 * i, 32)] = part
    cot2[c] = jnp.zeros((192, 128), F32)
    cot2[c, 0:172] = cot[...].astype(F32)
    j = lax.broadcasted_iota(jnp.int32, (512, 128), 0)
    target = ((((j >> 1) & 3) * NZ + ((j >> 3) & 15)) * 2 + (j & 1)) * NY + (j >> 7)
    for b in range(4):
        line = dest[pl.ds(b, 1), :]
        hot[:, pl.ds(128 * b, 128)] = jnp.where(target == (line >> 7), 1.0, 0.0).astype(BF16)
        within[:, pl.ds(128 * b, 128)] = jnp.broadcast_to(
            (line & 127).astype(F32), (128, 128)
        ).astype(BF16)

    p2[...] = lax.dot_general(
        hot[lanes(y, 128), :], within[...], TRAILING, preferred_element_type=F32
    ).reshape(NZ, 8, 128)
    pl.semaphore_wait(barrier, 2 + 3 + 3 + 3 + 3 + NZ - 1)

    def halo(field, slot):
        one = copy(field.at[pl.ds(4, 4)], field.at[pl.ds(8 * c, 4)], slot, partner)
        two = copy(field.at[pl.ds(4, 4)], field.at[pl.ds(8 * (1 - c), 4)], slot + 1, far)
        two.start()
        one.start()
        return one, two

    near, wide = halo(ext, HALO_ONE)
    ex_c = copy(cot2.at[c], cot2.at[c], EX_C, partner)
    ex_c.start()
    copies = [near, wide, ex_c]
    mine_xc = x * 2 + c

    def over_z(src, dst, slot):
        def one(k):
            to = (z + k) % NZ
            return copy(src.at[to], dst.at[z], slot + k, place(x, y, to, c))

        def start(k, carry):
            one(k).start()
            return carry

        def recv(k, carry):
            one(k).wait_recv()
            return carry

        def sent(k, carry):
            one(k).wait_send()
            return carry

        return start, recv, sent

    def over_xc(src, dst, slot):
        made = []
        for k in (2, 1, 3, 0):
            to = (x + k) % NX
            if k:
                made.append(copy(src.at[to * 2 + c], dst.at[mine_xc], slot + k, xs[k - 1]))
                made[-1].start()
            dev = xo[k - 1] if k else partner
            made.append(copy(src.at[to * 2 + 1 - c], dst.at[mine_xc], slot + 4 + k, dev))
            made[-1].start()
        return made

    pz_start, pz_recv, pz_sent = over_z(p2, pz2, Z_P)
    lax.fori_loop(1, NZ, pz_start, 0, unroll=True)
    pz2[z] = p2[z]
    wo[...] = jnp.zeros((192, 1024), BF16)
    for one in loads[3:]:
        one.wait()
    wo[0:172, :] = w_out_ref[...]

    count = count_ref[0]

    def spread(field, near, wide):
        near.wait_recv()
        for i, part in enumerate(split(field[pl.ds(8 * (1 - c), 4)])):
            parts[pl.ds(8 * (1 - c), 4), pl.ds(32 * i, 32)] = part
        wide.wait_recv()
        for i, part in enumerate(split(field[pl.ds(8 * c, 4)])):
            parts[pl.ds(8 * c, 4), pl.ds(32 * i, 32)] = part

        def slots(i, sums):
            for u in range(5):
                s = i * 5 + u
                at = jnp.minimum((col_ref[s] - 4 * d + 4) & 511, 11)
                product = lax.dot_general(
                    parts[at], tiles[s], TRAILING, preferred_element_type=F32
                )
                total = product[0:32] + product[32:64] + product[64:96]
                row = jnp.where(s < count, row_ref[s], -1)
                sums = tuple(
                    v + jnp.where(row == b, 1.0, 0.0) * total for b, v in enumerate(sums)
                )
            return sums

        zero = jnp.zeros((32, 128), F32)
        return jnp.stack(lax.fori_loop(0, 8, slots, (zero,) * 4))

    first = spread(ext, near, wide)
    ext_two[4:8] = first
    near, wide = halo(ext_two, HALO_TWO)
    copies += [near, wide]
    for i, part in enumerate(split(first)):
        parts[4:8, pl.ds(32 * i, 32)] = part
    lax.fori_loop(1, NZ, pz_recv, 0)
    for i in range(8):
        px[i] = pz2[:, i, :]
    xc_p = over_xc(px, pq, XC_P)
    pq[mine_xc] = px[mine_xc]
    copies += xc_p
    second = spread(ext_two, near, wide)
    second = 2.0 * second - ext[4:8]
    diffused = series_zero * ext[4:8] + series_one * ext_two[4:8] + series_two * second

    for i, part in enumerate(split(diffused)):
        for b in range(4):
            moved[pl.ds(32 * i, 32), pl.ds(128 * b, 128)] = part[b]
    sorted_rows = lax.dot_general(moved[...], hot[...], TRAILING, preferred_element_type=F32)
    columns = sorted_rows[0:32] + sorted_rows[32:64] + sorted_rows[64:96]
    for i in range(NY):
        amsg[i] = columns[:, 128 * i : 128 * i + 128]
    rep_x = []
    for k in (2, 1, 3):
        to = (y + k) % NY
        rep_x.append(copy(amsg.at[to], rf.at[y], REP_X + k, ys[k - 1]))
        rep_x[-1].start()
    rf[y] = amsg[y]
    for one in xc_p:
        one.wait_recv()
    at_lane = lax.broadcasted_iota(jnp.int32, (128, 128), 1).astype(F32)
    put[...] = jnp.where(pq[...].reshape(128, 128) == at_lane, 1.0, 0.0).astype(BF16)
    for one in rep_x:
        one.wait_recv()
    t2[...] = rf[...].reshape(128, 128).T.reshape(NZ, 8, 128)
    zx_start, zx_recv, zx_sent = over_z(t2, rz2, Z_X)
    lax.fori_loop(1, NZ, zx_start, 0, unroll=True)
    rz2[z] = t2[z]
    lax.fori_loop(1, NZ, zx_recv, 0, unroll=True)
    for i in range(8):
        rx[i] = rz2[:, i, :]
    xc_x = over_xc(rx, rq, XC_X)
    rq[mine_xc] = rx[mine_xc]
    for one in xc_x:
        one.wait_recv()
    copies += rep_x + xc_x
    lines = jnp.concatenate(split(rq[...].reshape(128, 128).T), axis=0)
    placed = jnp.dot(lines, put[...], preferred_element_type=F32)
    batch = placed[0:128] + placed[128:256] + placed[256:384]
    out_x[...] = batch

    x2[c] = batch
    ex_x = copy(x2.at[c], x2.at[c], EX_X, partner)
    ex_x.start()
    ex_c.wait_recv()
    for i in range(2):
        ct[pl.ds(128 * i, 128), :] = cot2[i].T.astype(BF16)
    ex_x.wait_recv()
    for i in range(2):
        xt[pl.ds(128 * i, 128), :] = x2[i].T.astype(BF16)

    for j in range(4):
        cols = pl.ds(256 * j, 256)
        pre = jnp.dot(xt[...], w_in_ref[:, cols], preferred_element_type=F32)
        g = sigmoid(pre)
        h1[:, cols] = (pre * g).astype(BF16)
        slope1[j] = g * (1.0 + pre * (1.0 - g))
    half = lanes(c, 512)
    pre_two = jnp.dot(h1[...], w_mid_ref[:, half], preferred_element_type=F32)
    g_two = sigmoid(pre_two)
    h2 = (pre_two * g_two).astype(BF16)
    back_two = jnp.dot(ct[...], wo[:, half], preferred_element_type=F32)
    d2[...] = (back_two * (g_two * (1.0 + pre_two * (1.0 - g_two)))).astype(BF16)

    send_b[...] = lax.dot_general(
        d2[...], w_mid_ref[lanes(1 - c, 512), half], TRAILING, preferred_element_type=F32
    )
    ex_b = copy(send_b, recv_b, EX_B, partner)
    ex_b.start()

    def send(src, dst, slot, dev):
        one = copy(src, dst, slot, dev)
        one.start()
        copies.append(one)
        return one

    def arrive(made):
        for one in made:
            one.wait_recv()

    copies += [ex_x, ex_b]
    mid_a, mid_b = [], []
    for k in (2, 1, 3, 0):
        to = (x + k) % NX
        rows = lax.dot_general(
            h1[:, lanes(to, 256)], d2[...], LEADING, preferred_element_type=F32
        ).reshape(NZ, 2, 8, 512)
        mid[0, to] = rows[:, 0]
        mid[1, to] = rows[:, 1]

    def send_mid(k, part, slot):
        rows = pl.ds(*part)
        mid_a.append(
            send(
                mid.at[0, (x + k) % NX, rows], ra_mid.at[k - 1, rows], slot, xs[k - 1]
            )
        )
        blocks = pl.ds(part[0] // 4, part[1] // 4)
        mid_b.append(
            send(
                mid.at[1, blocks, :, :, lanes((y + k) % NY, 128)],
                rb_mid.at[k - 1, blocks], slot + 1, ys[k - 1],
            )
        )

    send_mid(1, (0, 8), MID_ONE)
    send_mid(3, (0, 8), MID_ONE + 2)

    cot_rows = [cot2[i].astype(BF16) for i in range(2)]
    grad_out = jnp.dot(
        jnp.concatenate(cot_rows, axis=1), h2, preferred_element_type=F32
    ).reshape(24, 8, 512)
    io[16:40] = grad_out
    own_back = lax.dot_general(
        d2[...], w_mid_ref[half, half], TRAILING, preferred_element_type=F32
    )
    ex_b.wait_recv()
    slope = jnp.concatenate([slope1[2 * c], slope1[2 * c + 1]], axis=1)
    delta_one = ((own_back + recv_b[...]) * slope).astype(BF16)
    x_rows = jnp.concatenate([x2[i].astype(BF16) for i in range(2)], axis=1)
    grad_in = jnp.dot(x_rows, delta_one, preferred_element_type=F32).reshape(16, 8, 512)
    io[0:16] = grad_in

    first_a, first_b = [], []
    for k in (2, 1, 3):
        first_a.append(
            send(io.at[pl.ds((x + k) % NX * 5, 5)], ra_io.at[k - 1], A_IO + k - 1, xs[k - 1])
        )
        first_b.append(
            send(
                io.at[pl.ds(20, 20), :, lanes((y + k) % NY, 128)],
                rb_io.at[k - 1], B_IO + k - 1, ys[k - 1],
            )
        )
    send_mid(1, (8, 8), MID_ONE + 6)
    send_mid(3, (8, 8), MID_ONE + 8)

    y_lane = lanes(y, 128)
    two_io = []
    arrive(first_a)
    sai[...] = io[pl.ds(x * 5, 5)] + ra_io[0] + ra_io[1] + ra_io[2]
    for k in (2, 1, 3):
        two_io.append(
            send(sai.at[:, :, lanes((y + k) % NY, 128)], r2ai.at[k - 1], A_TWO_IO + k - 1, ys[k - 1])
        )
    arrive(first_b)
    sbi[...] = io[20:40, :, y_lane] + rb_io[0] + rb_io[1] + rb_io[2]
    for k in (2, 1, 3):
        two_io.append(
            send(sbi.at[pl.ds((x + k) % NX * 5, 5)], r2bi.at[k - 1], B_TWO_IO + k - 1, xs[k - 1])
        )
    send_mid(2, (0, 16), MID_ONE + 4)
    arrive(two_io)
    io_a = sai[:, :, y_lane] + r2ai[0] + r2ai[1] + r2ai[2]
    io_b = sbi[pl.ds(x * 5, 5)] + r2bi[0] + r2bi[1] + r2bi[2]

    group, spot_z = z // 4, z % 4
    tiles_io = [io_a[t] for t in range(5)] + [io_b[t] for t in range(5)]
    tiles_io += [jnp.zeros((8, 128), F32)] * 2
    for i in range(4):
        for t in range(3):
            zi[i, t] = tiles_io[4 * t + i]
    near_z = [place(x, y, group * 4 + (spot_z + k) % 4, c) for k in range(1, 4)]
    far_z = [place(x, y, (z + 4 * k) % NZ, c) for k in range(1, 4)]
    third_io = []
    for k in (2, 1, 3):
        third_io.append(
            send(zi.at[(spot_z + k) % 4], rzi.at[k - 1], Z_ONE_IO + k, near_z[k - 1])
        )
    arrive(third_io)
    rzi_two[group] = zi[spot_z] + rzi[0] + rzi[1] + rzi[2]
    across_io = []
    for k in (2, 1, 3):
        across_io.append(
            send(rzi_two.at[group], rzi_two.at[group], Z_TWO_IO + k, far_z[k - 1])
        )

    two = []
    arrive(mid_a)
    sa[...] = mid[0, x] + ra_mid[0] + ra_mid[1] + ra_mid[2]
    for k in (2, 1, 3):
        two.append(
            send(sa.at[:, :, lanes((y + k) % NY, 128)], r2a.at[k - 1], A_TWO + k - 1, ys[k - 1])
        )
    arrive(mid_b)
    for i in range(NX):
        sb[i] = mid[1, i, :, :, y_lane] + rb_mid[0, i] + rb_mid[1, i] + rb_mid[2, i]
    for k in (2, 1, 3):
        two.append(send(sb.at[(x + k) % NX], r2b.at[k - 1], B_TWO + k - 1, xs[k - 1]))

    arrive(across_io)
    mine_io[...] = ((rzi_two[0] + rzi_two[1]) + rzi_two[2]) + rzi_two[3]
    share = []
    for k in (2, 1, 3):
        share.append(send(mine_io, ri.at[spot_z], Z_ALL + k, near_z[k - 1]))
    ri[spot_z] = mine_io[...]

    arrive(two)
    sum_a = sa[:, :, y_lane] + r2a[0] + r2a[1] + r2a[2]
    sum_b = sb[x] + r2b[0] + r2b[1] + r2b[2]
    for i in range(4):
        for g in range(4):
            zs[i, g] = sum_a[4 * g + i]
            zs[i, 4 + g] = sum_b[4 * g + i]
    third = []
    for k in (2, 1, 3):
        third.append(send(zs.at[(spot_z + k) % 4], rz.at[k - 1], Z_ONE + k, near_z[k - 1]))

    arrive(share)
    tile = lanes(c * NY + y, 128)
    rows_a, rows_b = pl.ds(x * 5, 5), pl.ds((NX + x) * 5, 5)
    for t in range(10):
        full[(t // 5 * NX + x) * 5 + t % 5, :, tile] = ri[t % 4, t // 4]
    gather = []
    for k in (2, 1, 3):
        spot = full.at[rows_a, :, tile]
        gather.append(send(spot, spot, A_THREE + k - 1, ys[k - 1]))
        spot = full.at[rows_b, :, tile]
        gather.append(send(spot, spot, B_THREE + k - 1, xs[k - 1]))

    arrive(third)
    grouped = zs[spot_z] + rz[0] + rz[1] + rz[2]
    for g in range(4):
        zs_two[g, 0] = grouped[g]
        zs_two[g, 1] = grouped[4 + g]
    across = []
    for k in (2, 1, 3):
        across.append(
            send(zs_two.at[(group + k) % 4], rz_two.at[k - 1], Z_TWO + k, far_z[k - 1])
        )

    arrive(gather)
    fourth = []
    for k in (2, 1, 3):
        spot = full.at[rows_a, :, half]
        fourth.append(send(spot, spot, A_FOUR + k - 1, xs[k - 1]))
        spot = full.at[pl.ds(20, 20), :, tile]
        fourth.append(send(spot, spot, B_FOUR + k - 1, ys[k - 1]))
    arrive(fourth)
    spot = full.at[:, :, half]
    pair = send(spot, spot, PAIR, partner)

    arrive(across)
    mine[...] = zs_two[group] + rz_two[0] + rz_two[1] + rz_two[2]
    last = []
    for k in range(NY):
        if k:
            last.append(send(mine.at[c], r4.at[c, y], MID_ALL + k, ys[k - 1]))
        last.append(
            send(
                mine.at[1 - c], r4.at[c, y], MID_ALL + 4 + k, yo[k - 1] if k else partner
            )
        )
    r4[c, y] = mine[c]
    pair.wait_recv()
    out_in[...] = full[0:16].reshape(128, 1024)
    out_out[...] = full[16:40].reshape(192, 1024)[0:172]
    arrive(last)
    for i in range(8):
        out_mid[:, pl.ds(128 * i, 128)] = r4[i // 4, i % 4]

    lax.fori_loop(1, NZ, pz_sent, 0)
    lax.fori_loop(1, NZ, zx_sent, 0)
    for one in copies:
        one.wait_send()


def write_kernel(*refs):
    writes = [
        pltpu.make_async_copy(refs[i], refs[4 + i], refs[8].at[i]) for i in range(4)
    ]
    for one in writes:
        one.start()
    for one in writes:
        one.wait()


def train(tile_row, tile_col, tile_count, features, tiles, dest, cotangent, w_in, w_mid, w_out):
    vmem = pl.BlockSpec(memory_space=pltpu.VMEM)
    hbm = pl.BlockSpec(memory_space=pltpu.HBM)
    buf = pltpu.VMEM
    return pl.pallas_call(
        train_kernel,
        out_shape=(
            jax.ShapeDtypeStruct((128, 128), F32),
            jax.ShapeDtypeStruct((128, 1024), F32),
            jax.ShapeDtypeStruct((8, 1024), F32),
            jax.ShapeDtypeStruct((172, 1024), F32),
        ),
        in_specs=[pl.BlockSpec(memory_space=pltpu.SMEM)] + [hbm] * 9,
        out_specs=(vmem,) * 4,
        scratch_shapes=[
            pltpu.SMEM((40,), jnp.int32),
            pltpu.SMEM((40,), jnp.int32),
            buf((32, 512), F32),
            buf((40, 128, 128), BF16),
            buf((4, 128), jnp.int32),
            buf((172, 128), BF16),
            buf((128, 1024), BF16),
            buf((1024, 1024), BF16),
            buf((172, 1024), BF16),
            buf((12, 32, 128), F32),
            buf((12, 32, 128), F32),
            buf((12, 96, 128), BF16),
            buf((512, 512), BF16),
            buf((96, 512), BF16),
            buf((128, 512), BF16),
            buf((NY, 32, 128), F32),
            buf((NY, 32, 128), F32),
            buf((NZ, 8, 128), F32),
            buf((NZ, 8, 128), F32),
            buf((8, NZ, 128), F32),
            buf((8, NZ, 128), F32),
            buf((NZ, 8, 128), F32),
            buf((NZ, 8, 128), F32),
            buf((8, NZ, 128), F32),
            buf((8, NZ, 128), F32),
            buf((128, 128), BF16),
            buf((2, 128, 128), F32),
            buf((2, 192, 128), F32),
            buf((256, 128), BF16),
            buf((256, 192), BF16),
            buf((192, 1024), BF16),
            buf((256, 1024), BF16),
            buf((4, 256, 256), F32),
            buf((256, 512), BF16),
            buf((256, 512), F32),
            buf((256, 512), F32),
            buf((2, NX, NZ, 8, 512), F32),
            buf((40, 8, 512), F32),
            buf((3, NZ, 8, 512), F32),
            buf((3, 5, 8, 512), F32),
            buf((3, NX, NZ, 8, 128), F32),
            buf((3, 20, 8, 128), F32),
            buf((NZ, 8, 512), F32),
            buf((NX, NZ, 8, 128), F32),
            buf((3, NZ, 8, 128), F32),
            buf((3, NZ, 8, 128), F32),
            buf((4, 8, 8, 128), F32),
            buf((3, 8, 8, 128), F32),
            buf((4, 2, 8, 128), F32),
            buf((3, 2, 8, 128), F32),
            buf((2, 8, 128), F32),
            buf((4, 3, 8, 128), F32),
            buf((2, NY, 8, 128), F32),
            buf((40, 8, 1024), F32),
            buf((5, 8, 512), F32),
            buf((20, 8, 128), F32),
            buf((3, 5, 8, 128), F32),
            buf((3, 5, 8, 128), F32),
            buf((4, 3, 8, 128), F32),
            buf((3, 3, 8, 128), F32),
            buf((4, 3, 8, 128), F32),
            buf((3, 8, 128), F32),
            pltpu.SemaphoreType.DMA((SEMS,)),
            pltpu.SemaphoreType.DMA((SEMS,)),
            pltpu.SemaphoreType.DMA((9,)),
        ],
        compiler_params=pltpu.CompilerParams(
            collective_id=0, has_side_effects=True, vmem_limit_bytes=46 * 1024 * 1024
        ),
    )(tile_count, *(pltpu.with_memory_space_constraint(v, pltpu.HBM) for v in (
        tile_row, tile_col, features, tiles, dest, cotangent, w_in, w_mid, w_out
    )))


def shards(
    features, tiles, tile_row, tile_col, tile_count, dest_slot, w_in, w_mid, w_out, cotangent
):
    dest = dest_slot.reshape(4, 128)
    results = train(
        tile_row, tile_col, tile_count, features, tiles, dest, cotangent, w_in, w_mid, w_out
    )
    return pl.pallas_call(
        write_kernel,
        out_shape=tuple(jax.ShapeDtypeStruct(v.shape, v.dtype) for v in results),
        in_specs=[pl.BlockSpec(memory_space=pltpu.VMEM)] * 4,
        out_specs=(pl.BlockSpec(memory_space=pltpu.HBM),) * 4,
        scratch_shapes=[pltpu.SemaphoreType.DMA((4,))],
    )(*(pltpu.with_memory_space_constraint(v, pltpu.VMEM) for v in results))


def solution(mesh):
    in_specs = (
        P("rep", "dom"),
        P("dom", None, None),
        P("dom"),
        P("dom"),
        P("dom"),
        P("dom"),
        P(),
        P(),
        P(),
        P(None, ("dom", "rep")),
    )
    out_specs = (P(None, ("dom", "rep")), P(), P("dom", None), P())
    return jax.shard_map(shards, mesh=mesh, in_specs=in_specs, out_specs=out_specs, check_vma=False)
```

```python
import jax
import jax.numpy as jnp
from jax import lax
from jax.experimental import pallas as pl
from jax.experimental.pallas import tpu as pltpu
from jax.sharding import PartitionSpec as P

series_zero = 0.3085083
series_one = -0.4305395
series_two = 0.1864784
LEADING = (((0,), (0,)), ((), ()))
TRAILING = (((1,), (1,)), ((), ()))
MESH = pl.DeviceIdType.MESH
NX, NY, NZ = 4, 4, 16
F32 = jnp.float32
BF16 = jnp.bfloat16


EX_X, EX_C, EX_B = 0, 1, 2
A_IO, B_IO = 6, 12
A_TWO, B_TWO = 15, 18
Z_ONE, Z_TWO, Z_ALL = 21, 25, 29
MID_ALL = 53
A_THREE, B_THREE, A_FOUR, B_FOUR, PAIR = 61, 64, 67, 70, 73
HALO_ONE, HALO_TWO = 74, 76
REP_X, Z_X, XC_X = 78, 82, 98
Z_P, XC_P = 106, 122
A_TWO_IO, B_TWO_IO, Z_ONE_IO, Z_TWO_IO = 130, 133, 136, 140
MID_ONE = 144
SEMS = 154


def sigmoid(v):
    return 0.5 + 0.5 * jnp.tanh(0.5 * v)


def split(v):
    high = v.astype(BF16)
    rest = v - high.astype(F32)
    middle = rest.astype(BF16)
    low = (rest - middle.astype(F32)).astype(BF16)
    return high, middle, low


def train_kernel(
    count_ref, row_hbm, col_hbm, feat_hbm, tiles_hbm, dest_hbm, cot_hbm, w_in_hbm, w_mid_hbm, w_out_hbm,
    out_x, out_in, out_mid, out_out,
    row_ref, col_ref, feat, tiles, dest, cot, w_in_ref, w_mid_ref, w_out_ref,
    ext, ext_two, parts, hot, moved, within, amsg, rf, t2, rz2, rx, rq, p2, pz2, px, pq, put,
    x2, cot2, xt, ct, wo, h1, slope1, d2, send_b, recv_b,
    mid, io, ra_mid, ra_io, rb_mid, rb_io, sa, sb, r2a, r2b, zs, rz, zs_two, rz_two, mine, ri, r4, full,
    sai, sbi, r2ai, r2bi, zi, rzi, rzi_two, mine_io,
    ssem, rsem, lsem, relay,
):
    loads = []
    for i, (src, dst) in enumerate((
        (feat_hbm, feat), (dest_hbm, dest), (cot_hbm, cot), (row_hbm, row_ref),
        (col_hbm, col_ref), (tiles_hbm, tiles),
        (w_in_hbm, w_in_ref), (w_out_hbm, w_out_ref), (w_mid_hbm, w_mid_ref),
    )):
        loads.append(pltpu.make_async_copy(src, dst, lsem.at[i]))
        loads[-1].start()
    d = lax.axis_index("dom")
    y = lax.axis_index("rep")
    c = d % 2
    z = (d // 2) % NZ
    x = d // (2 * NZ)

    def place(xx, yy, zz, cc):
        return ((xx * NZ + zz) * 2 + cc, yy)

    def copy(src, dst, slot, dev):
        return pltpu.make_async_remote_copy(
            src_ref=src, dst_ref=dst, send_sem=ssem.at[slot], recv_sem=rsem.at[slot],
            device_id=dev, device_id_type=MESH,
        )

    def lanes(index, width):
        return pl.ds(pl.multiple_of(index * width, width), width)

    partner = place(x, y, z, 1 - c)
    far = ((d + 2 * c - 1 + 2 * NX * NZ) % (2 * NX * NZ), y)
    xs = [place((x + k) % NX, y, z, c) for k in range(1, NX)]
    xo = [place((x + k) % NX, y, z, 1 - c) for k in range(1, NX)]
    ys = [place(x, (y + k) % NY, z, c) for k in range(1, NY)]
    yo = [place(x, (y + k) % NY, z, 1 - c) for k in range(1, NY)]
    barrier = pltpu.get_barrier_semaphore()
    zs_at = lambda k: place(x, y, (z + k) % NZ, c)
    greeted = [partner, far] + xs + xo + ys + yo + [zs_at(1), zs_at(NZ - 1)]
    for dev in greeted:
        pl.semaphore_signal(barrier, inc=1, device_id=dev, device_id_type=MESH)

    def tell(turn):
        for k in (1 << turn, NZ - (1 << turn)):
            pl.semaphore_signal(
                relay.at[turn], inc=1, device_id=zs_at(k), device_id_type=MESH
            )

    for one in loads[:3]:
        one.wait()
    own = jnp.stack([feat[:, pl.ds(128 * b, 128)] for b in range(4)])
    ext[4:8] = own
    for i, part in enumerate(split(own)):
        parts[4:8, pl.ds(32 * i, 32)] = part
    cot2[c] = jnp.zeros((192, 128), F32)
    cot2[c, 0:172] = cot[...].astype(F32)
    j = lax.broadcasted_iota(jnp.int32, (512, 128), 0)
    target = ((((j >> 1) & 3) * NZ + ((j >> 3) & 15)) * 2 + (j & 1)) * NY + (j >> 7)
    for b in range(4):
        line = dest[pl.ds(b, 1), :]
        hot[:, pl.ds(128 * b, 128)] = jnp.where(target == (line >> 7), 1.0, 0.0).astype(BF16)
        within[:, pl.ds(128 * b, 128)] = jnp.broadcast_to(
            (line & 127).astype(F32), (128, 128)
        ).astype(BF16)

    p2[...] = lax.dot_general(
        hot[lanes(y, 128), :], within[...], TRAILING, preferred_element_type=F32
    ).reshape(NZ, 8, 128)
    pl.semaphore_wait(barrier, len(greeted))
    tell(0)

    def halo(field, slot):
        one = copy(field.at[pl.ds(4, 4)], field.at[pl.ds(8 * c, 4)], slot, partner)
        two = copy(field.at[pl.ds(4, 4)], field.at[pl.ds(8 * (1 - c), 4)], slot + 1, far)
        two.start()
        one.start()
        return one, two

    near, wide = halo(ext, HALO_ONE)
    ex_c = copy(cot2.at[c], cot2.at[c], EX_C, partner)
    ex_c.start()
    copies = [near, wide, ex_c]
    mine_xc = x * 2 + c

    def over_z(src, dst, slot):
        def one(k):
            to = (z + k) % NZ
            return copy(src.at[to], dst.at[z], slot + k, place(x, y, to, c))

        def start(k, carry):
            one(k).start()
            return carry

        def recv(k, carry):
            one(k).wait_recv()
            return carry

        def sent(k, carry):
            one(k).wait_send()
            return carry

        return start, recv, sent

    def over_xc(src, dst, slot):
        made = []
        for k in (2, 1, 3, 0):
            to = (x + k) % NX
            if k:
                made.append(copy(src.at[to * 2 + c], dst.at[mine_xc], slot + k, xs[k - 1]))
                made[-1].start()
            dev = xo[k - 1] if k else partner
            made.append(copy(src.at[to * 2 + 1 - c], dst.at[mine_xc], slot + 4 + k, dev))
            made[-1].start()
        return made

    wo[...] = jnp.zeros((192, 1024), BF16)
    for one in loads[3:]:
        one.wait()
    wo[0:172, :] = w_out_ref[...]
    pl.semaphore_wait(relay.at[0], 2)
    tell(1)

    count = count_ref[0]

    def spread(field, near, wide, then=None):
        near.wait_recv()
        for i, part in enumerate(split(field[pl.ds(8 * (1 - c), 4)])):
            parts[pl.ds(8 * (1 - c), 4), pl.ds(32 * i, 32)] = part
        wide.wait_recv()
        for i, part in enumerate(split(field[pl.ds(8 * c, 4)])):
            parts[pl.ds(8 * c, 4), pl.ds(32 * i, 32)] = part
        if then is not None:
            then()

        def slots(i, sums):
            for u in range(5):
                s = i * 5 + u
                at = jnp.minimum((col_ref[s] - 4 * d + 4) & 511, 11)
                product = lax.dot_general(
                    parts[at], tiles[s], TRAILING, preferred_element_type=F32
                )
                total = product[0:32] + product[32:64] + product[64:96]
                row = jnp.where(s < count, row_ref[s], -1)
                sums = tuple(
                    v + jnp.where(row == b, 1.0, 0.0) * total for b, v in enumerate(sums)
                )
            return sums

        zero = jnp.zeros((32, 128), F32)
        return jnp.stack(lax.fori_loop(0, 8, slots, (zero,) * 4))

    first = spread(ext, near, wide)
    ext_two[4:8] = first
    near, wide = halo(ext_two, HALO_TWO)
    copies += [near, wide]
    for i, part in enumerate(split(first)):
        parts[4:8, pl.ds(32 * i, 32)] = part
    pl.semaphore_wait(relay.at[1], 2)
    tell(2)
    pz_start, pz_recv, pz_sent = over_z(p2, pz2, Z_P)

    def positions():
        pl.semaphore_wait(relay.at[2], 2)
        lax.fori_loop(1, NZ, pz_start, 0, unroll=True)
        pz2[z] = p2[z]

    second = spread(ext_two, near, wide, positions)
    second = 2.0 * second - ext[4:8]
    diffused = series_zero * ext[4:8] + series_one * ext_two[4:8] + series_two * second

    for i, part in enumerate(split(diffused)):
        for b in range(4):
            moved[pl.ds(32 * i, 32), pl.ds(128 * b, 128)] = part[b]
    sorted_rows = lax.dot_general(moved[...], hot[...], TRAILING, preferred_element_type=F32)
    columns = sorted_rows[0:32] + sorted_rows[32:64] + sorted_rows[64:96]
    for i in range(NY):
        amsg[i] = columns[:, 128 * i : 128 * i + 128]
    rep_x = []
    for k in (2, 1, 3):
        to = (y + k) % NY
        rep_x.append(copy(amsg.at[to], rf.at[y], REP_X + k, ys[k - 1]))
        rep_x[-1].start()
    rf[y] = amsg[y]
    for one in rep_x:
        one.wait_recv()
    t2[...] = rf[...].reshape(128, 128).T.reshape(NZ, 8, 128)
    zx_start, zx_recv, zx_sent = over_z(t2, rz2, Z_X)
    lax.fori_loop(1, NZ, zx_start, 0, unroll=True)
    rz2[z] = t2[z]
    lax.fori_loop(1, NZ, pz_recv, 0)
    for i in range(8):
        px[i] = pz2[:, i, :]
    xc_p = over_xc(px, pq, XC_P)
    pq[mine_xc] = px[mine_xc]
    copies += xc_p
    lax.fori_loop(1, NZ, zx_recv, 0, unroll=True)
    for i in range(8):
        rx[i] = rz2[:, i, :]
    xc_x = over_xc(rx, rq, XC_X)
    rq[mine_xc] = rx[mine_xc]
    for one in xc_p:
        one.wait_recv()
    at_lane = lax.broadcasted_iota(jnp.int32, (128, 128), 1).astype(F32)
    put[...] = jnp.where(pq[...].reshape(128, 128) == at_lane, 1.0, 0.0).astype(BF16)
    for one in xc_x:
        one.wait_recv()
    copies += rep_x + xc_x
    lines = jnp.concatenate(split(rq[...].reshape(128, 128).T), axis=0)
    placed = jnp.dot(lines, put[...], preferred_element_type=F32)
    batch = placed[0:128] + placed[128:256] + placed[256:384]
    out_x[...] = batch

    x2[c] = batch
    ex_x = copy(x2.at[c], x2.at[c], EX_X, partner)
    ex_x.start()
    ex_c.wait_recv()
    for i in range(2):
        ct[pl.ds(128 * i, 128), :] = cot2[i].T.astype(BF16)

    for side in (c, 1 - c):
        rows = lanes(side, 128)
        if side is not c:
            ex_x.wait_recv()
        xt[rows, :] = x2[side].T.astype(BF16)
        for j in range(4):
            cols = pl.ds(256 * j, 256)
            pre = jnp.dot(xt[rows, :], w_in_ref[:, cols], preferred_element_type=F32)
            g = sigmoid(pre)
            h1[rows, cols] = (pre * g).astype(BF16)
            slope1[j, rows] = g * (1.0 + pre * (1.0 - g))
    half = lanes(c, 512)
    pre_two = jnp.dot(h1[...], w_mid_ref[:, half], preferred_element_type=F32)
    g_two = sigmoid(pre_two)
    h2 = (pre_two * g_two).astype(BF16)
    back_two = jnp.dot(ct[...], wo[:, half], preferred_element_type=F32)
    d2[...] = (back_two * (g_two * (1.0 + pre_two * (1.0 - g_two)))).astype(BF16)

    send_b[...] = lax.dot_general(
        d2[...], w_mid_ref[lanes(1 - c, 512), half], TRAILING, preferred_element_type=F32
    )
    ex_b = copy(send_b, recv_b, EX_B, partner)
    ex_b.start()

    def send(src, dst, slot, dev):
        one = copy(src, dst, slot, dev)
        one.start()
        copies.append(one)
        return one

    def arrive(made):
        for one in made:
            one.wait_recv()

    copies += [ex_x, ex_b]
    mid_a, mid_b = [], []
    for k in (2, 1, 3, 0):
        to = (x + k) % NX
        rows = lax.dot_general(
            h1[:, lanes(to, 256)], d2[...], LEADING, preferred_element_type=F32
        ).reshape(NZ, 2, 8, 512)
        mid[0, to] = rows[:, 0]
        mid[1, to] = rows[:, 1]

    def send_mid(k, part, slot):
        rows = pl.ds(*part)
        mid_a.append(
            send(
                mid.at[0, (x + k) % NX, rows], ra_mid.at[k - 1, rows], slot, xs[k - 1]
            )
        )
        blocks = pl.ds(part[0] // 4, part[1] // 4)
        mid_b.append(
            send(
                mid.at[1, blocks, :, :, lanes((y + k) % NY, 128)],
                rb_mid.at[k - 1, blocks], slot + 1, ys[k - 1],
            )
        )

    send_mid(1, (0, 8), MID_ONE)
    send_mid(3, (0, 8), MID_ONE + 2)

    cot_rows = [cot2[i].astype(BF16) for i in range(2)]
    grad_out = jnp.dot(
        jnp.concatenate(cot_rows, axis=1), h2, preferred_element_type=F32
    ).reshape(24, 8, 512)
    io[16:40] = grad_out
    own_back = lax.dot_general(
        d2[...], w_mid_ref[half, half], TRAILING, preferred_element_type=F32
    )
    ex_b.wait_recv()
    slope = jnp.concatenate([slope1[2 * c], slope1[2 * c + 1]], axis=1)
    delta_one = ((own_back + recv_b[...]) * slope).astype(BF16)
    x_rows = jnp.concatenate([x2[i].astype(BF16) for i in range(2)], axis=1)
    grad_in = jnp.dot(x_rows, delta_one, preferred_element_type=F32).reshape(16, 8, 512)
    io[0:16] = grad_in

    first_a, first_b = [], []
    for k in (2, 1, 3):
        first_a.append(
            send(io.at[pl.ds((x + k) % NX * 5, 5)], ra_io.at[k - 1], A_IO + k - 1, xs[k - 1])
        )
        first_b.append(
            send(
                io.at[pl.ds(20, 20), :, lanes((y + k) % NY, 128)],
                rb_io.at[k - 1], B_IO + k - 1, ys[k - 1],
            )
        )
    send_mid(1, (8, 8), MID_ONE + 6)
    send_mid(3, (8, 8), MID_ONE + 8)

    y_lane = lanes(y, 128)
    two_io = []
    arrive(first_a)
    sai[...] = io[pl.ds(x * 5, 5)] + ra_io[0] + ra_io[1] + ra_io[2]
    for k in (2, 1, 3):
        two_io.append(
            send(sai.at[:, :, lanes((y + k) % NY, 128)], r2ai.at[k - 1], A_TWO_IO + k - 1, ys[k - 1])
        )
    arrive(first_b)
    sbi[...] = io[20:40, :, y_lane] + rb_io[0] + rb_io[1] + rb_io[2]
    for k in (2, 1, 3):
        two_io.append(
            send(sbi.at[pl.ds((x + k) % NX * 5, 5)], r2bi.at[k - 1], B_TWO_IO + k - 1, xs[k - 1])
        )
    send_mid(2, (0, 16), MID_ONE + 4)
    arrive(two_io)
    io_a = sai[:, :, y_lane] + r2ai[0] + r2ai[1] + r2ai[2]
    io_b = sbi[pl.ds(x * 5, 5)] + r2bi[0] + r2bi[1] + r2bi[2]

    group, spot_z = z // 4, z % 4
    tiles_io = [io_a[t] for t in range(5)] + [io_b[t] for t in range(5)]
    tiles_io += [jnp.zeros((8, 128), F32)] * 2
    for i in range(4):
        for t in range(3):
            zi[i, t] = tiles_io[4 * t + i]
    near_z = [place(x, y, group * 4 + (spot_z + k) % 4, c) for k in range(1, 4)]
    far_z = [place(x, y, (z + 4 * k) % NZ, c) for k in range(1, 4)]
    third_io = []
    for k in (2, 1, 3):
        third_io.append(
            send(zi.at[(spot_z + k) % 4], rzi.at[k - 1], Z_ONE_IO + k, near_z[k - 1])
        )
    arrive(third_io)
    rzi_two[group] = zi[spot_z] + rzi[0] + rzi[1] + rzi[2]
    across_io = []
    for k in (2, 1, 3):
        across_io.append(
            send(rzi_two.at[group], rzi_two.at[group], Z_TWO_IO + k, far_z[k - 1])
        )

    two = []
    arrive(mid_a)
    sa[...] = mid[0, x] + ra_mid[0] + ra_mid[1] + ra_mid[2]
    for k in (2, 1, 3):
        two.append(
            send(sa.at[:, :, lanes((y + k) % NY, 128)], r2a.at[k - 1], A_TWO + k - 1, ys[k - 1])
        )
    arrive(mid_b)
    for i in range(NX):
        sb[i] = mid[1, i, :, :, y_lane] + rb_mid[0, i] + rb_mid[1, i] + rb_mid[2, i]
    for k in (2, 1, 3):
        two.append(send(sb.at[(x + k) % NX], r2b.at[k - 1], B_TWO + k - 1, xs[k - 1]))

    arrive(across_io)
    mine_io[...] = ((rzi_two[0] + rzi_two[1]) + rzi_two[2]) + rzi_two[3]
    share = []
    for k in (2, 1, 3):
        share.append(send(mine_io, ri.at[spot_z], Z_ALL + k, near_z[k - 1]))
    ri[spot_z] = mine_io[...]

    arrive(two)
    sum_a = sa[:, :, y_lane] + r2a[0] + r2a[1] + r2a[2]
    sum_b = sb[x] + r2b[0] + r2b[1] + r2b[2]
    for i in range(4):
        for g in range(4):
            zs[i, g] = sum_a[4 * g + i]
            zs[i, 4 + g] = sum_b[4 * g + i]
    third = []
    for k in (2, 1, 3):
        third.append(send(zs.at[(spot_z + k) % 4], rz.at[k - 1], Z_ONE + k, near_z[k - 1]))

    arrive(share)
    tile = lanes(c * NY + y, 128)
    rows_a, rows_b = pl.ds(x * 5, 5), pl.ds((NX + x) * 5, 5)
    for t in range(10):
        full[(t // 5 * NX + x) * 5 + t % 5, :, tile] = ri[t % 4, t // 4]
    gather = []
    for k in (2, 1, 3):
        spot = full.at[rows_a, :, tile]
        gather.append(send(spot, spot, A_THREE + k - 1, ys[k - 1]))
        spot = full.at[rows_b, :, tile]
        gather.append(send(spot, spot, B_THREE + k - 1, xs[k - 1]))

    arrive(third)
    grouped = zs[spot_z] + rz[0] + rz[1] + rz[2]
    for g in range(4):
        zs_two[g, 0] = grouped[g]
        zs_two[g, 1] = grouped[4 + g]
    across = []
    for k in (2, 1, 3):
        across.append(
            send(zs_two.at[(group + k) % 4], rz_two.at[k - 1], Z_TWO + k, far_z[k - 1])
        )

    arrive(gather)
    fourth = []
    for k in (2, 1, 3):
        spot = full.at[rows_a, :, half]
        fourth.append(send(spot, spot, A_FOUR + k - 1, xs[k - 1]))
        spot = full.at[pl.ds(20, 20), :, tile]
        fourth.append(send(spot, spot, B_FOUR + k - 1, ys[k - 1]))
    arrive(fourth)
    spot = full.at[:, :, half]
    pair = send(spot, spot, PAIR, partner)

    arrive(across)
    mine[...] = zs_two[group] + rz_two[0] + rz_two[1] + rz_two[2]
    last = []
    for k in range(NY):
        if k:
            last.append(send(mine.at[c], r4.at[c, y], MID_ALL + k, ys[k - 1]))
        last.append(
            send(
                mine.at[1 - c], r4.at[c, y], MID_ALL + 4 + k, yo[k - 1] if k else partner
            )
        )
    r4[c, y] = mine[c]
    pair.wait_recv()
    out_in[...] = full[0:16].reshape(128, 1024)
    out_out[...] = full[16:40].reshape(192, 1024)[0:172]
    arrive(last)
    for i in range(8):
        out_mid[:, pl.ds(128 * i, 128)] = r4[i // 4, i % 4]

    lax.fori_loop(1, NZ, pz_sent, 0)
    lax.fori_loop(1, NZ, zx_sent, 0)
    for one in copies:
        one.wait_send()


def write_kernel(*refs):
    writes = [
        pltpu.make_async_copy(refs[i], refs[4 + i], refs[8].at[i]) for i in range(4)
    ]
    for one in writes:
        one.start()
    for one in writes:
        one.wait()


def train(tile_row, tile_col, tile_count, features, tiles, dest, cotangent, w_in, w_mid, w_out):
    vmem = pl.BlockSpec(memory_space=pltpu.VMEM)
    hbm = pl.BlockSpec(memory_space=pltpu.HBM)
    buf = pltpu.VMEM
    return pl.pallas_call(
        train_kernel,
        out_shape=(
            jax.ShapeDtypeStruct((128, 128), F32),
            jax.ShapeDtypeStruct((128, 1024), F32),
            jax.ShapeDtypeStruct((8, 1024), F32),
            jax.ShapeDtypeStruct((172, 1024), F32),
        ),
        in_specs=[pl.BlockSpec(memory_space=pltpu.SMEM)] + [hbm] * 9,
        out_specs=(vmem,) * 4,
        scratch_shapes=[
            pltpu.SMEM((40,), jnp.int32),
            pltpu.SMEM((40,), jnp.int32),
            buf((32, 512), F32),
            buf((40, 128, 128), BF16),
            buf((4, 128), jnp.int32),
            buf((172, 128), BF16),
            buf((128, 1024), BF16),
            buf((1024, 1024), BF16),
            buf((172, 1024), BF16),
            buf((12, 32, 128), F32),
            buf((12, 32, 128), F32),
            buf((12, 96, 128), BF16),
            buf((512, 512), BF16),
            buf((96, 512), BF16),
            buf((128, 512), BF16),
            buf((NY, 32, 128), F32),
            buf((NY, 32, 128), F32),
            buf((NZ, 8, 128), F32),
            buf((NZ, 8, 128), F32),
            buf((8, NZ, 128), F32),
            buf((8, NZ, 128), F32),
            buf((NZ, 8, 128), F32),
            buf((NZ, 8, 128), F32),
            buf((8, NZ, 128), F32),
            buf((8, NZ, 128), F32),
            buf((128, 128), BF16),
            buf((2, 128, 128), F32),
            buf((2, 192, 128), F32),
            buf((256, 128), BF16),
            buf((256, 192), BF16),
            buf((192, 1024), BF16),
            buf((256, 1024), BF16),
            buf((4, 256, 256), F32),
            buf((256, 512), BF16),
            buf((256, 512), F32),
            buf((256, 512), F32),
            buf((2, NX, NZ, 8, 512), F32),
            buf((40, 8, 512), F32),
            buf((3, NZ, 8, 512), F32),
            buf((3, 5, 8, 512), F32),
            buf((3, NX, NZ, 8, 128), F32),
            buf((3, 20, 8, 128), F32),
            buf((NZ, 8, 512), F32),
            buf((NX, NZ, 8, 128), F32),
            buf((3, NZ, 8, 128), F32),
            buf((3, NZ, 8, 128), F32),
            buf((4, 8, 8, 128), F32),
            buf((3, 8, 8, 128), F32),
            buf((4, 2, 8, 128), F32),
            buf((3, 2, 8, 128), F32),
            buf((2, 8, 128), F32),
            buf((4, 3, 8, 128), F32),
            buf((2, NY, 8, 128), F32),
            buf((40, 8, 1024), F32),
            buf((5, 8, 512), F32),
            buf((20, 8, 128), F32),
            buf((3, 5, 8, 128), F32),
            buf((3, 5, 8, 128), F32),
            buf((4, 3, 8, 128), F32),
            buf((3, 3, 8, 128), F32),
            buf((4, 3, 8, 128), F32),
            buf((3, 8, 128), F32),
            pltpu.SemaphoreType.DMA((SEMS,)),
            pltpu.SemaphoreType.DMA((SEMS,)),
            pltpu.SemaphoreType.DMA((9,)),
            pltpu.SemaphoreType.REGULAR((3,)),
        ],
        compiler_params=pltpu.CompilerParams(
            collective_id=0, has_side_effects=True, vmem_limit_bytes=46 * 1024 * 1024
        ),
    )(tile_count, *(pltpu.with_memory_space_constraint(v, pltpu.HBM) for v in (
        tile_row, tile_col, features, tiles, dest, cotangent, w_in, w_mid, w_out
    )))


def shards(
    features, tiles, tile_row, tile_col, tile_count, dest_slot, w_in, w_mid, w_out, cotangent
):
    dest = dest_slot.reshape(4, 128)
    results = train(
        tile_row, tile_col, tile_count, features, tiles, dest, cotangent, w_in, w_mid, w_out
    )
    return pl.pallas_call(
        write_kernel,
        out_shape=tuple(jax.ShapeDtypeStruct(v.shape, v.dtype) for v in results),
        in_specs=[pl.BlockSpec(memory_space=pltpu.VMEM)] * 4,
        out_specs=(pl.BlockSpec(memory_space=pltpu.HBM),) * 4,
        scratch_shapes=[pltpu.SemaphoreType.DMA((4,))],
    )(*(pltpu.with_memory_space_constraint(v, pltpu.VMEM) for v in results))


def solution(mesh):
    in_specs = (
        P("rep", "dom"),
        P("dom", None, None),
        P("dom"),
        P("dom"),
        P("dom"),
        P("dom"),
        P(),
        P(),
        P(),
        P(None, ("dom", "rep")),
    )
    out_specs = (P(None, ("dom", "rep")), P(), P("dom", None), P())
    return jax.shard_map(shards, mesh=mesh, in_specs=in_specs, out_specs=out_specs, check_vma=False)
```

```python
import jax
import jax.numpy as jnp
from jax import lax
from jax.experimental import pallas as pl
from jax.experimental.pallas import tpu as pltpu
from jax.sharding import PartitionSpec as P

series_zero = 0.3085083
series_one = -0.4305395
series_two = 0.1864784
LEADING = (((0,), (0,)), ((), ()))
TRAILING = (((1,), (1,)), ((), ()))
MESH = pl.DeviceIdType.MESH
NX, NY, NZ = 4, 4, 16
F32 = jnp.float32
BF16 = jnp.bfloat16


EX_X, EX_C, EX_B = 0, 1, 2
A_IO, B_IO = 6, 12
A_TWO, B_TWO = 15, 18
Z_ONE, Z_TWO, Z_ALL = 21, 25, 29
MID_ALL = 53
A_THREE, B_THREE, A_FOUR, B_FOUR, PAIR = 61, 64, 67, 70, 73
HALO_ONE, HALO_TWO = 74, 76
REP_X, Z_X, XC_X = 78, 82, 98
Z_P, XC_P = 106, 122
A_TWO_IO, B_TWO_IO, Z_ONE_IO, Z_TWO_IO = 130, 133, 136, 140
MID_ONE = 144
SEMS = 154


def sigmoid(v):
    return 0.5 + 0.5 * jnp.tanh(0.5 * v)


def split(v):
    high = v.astype(BF16)
    rest = v - high.astype(F32)
    middle = rest.astype(BF16)
    low = (rest - middle.astype(F32)).astype(BF16)
    return high, middle, low


def train_kernel(
    count_ref, row_hbm, col_hbm, feat_hbm, tiles_hbm, dest_hbm, cot_hbm, w_in_hbm, w_mid_hbm, w_out_hbm,
    out_x, out_in, out_mid, out_out,
    row_ref, col_ref, feat, tiles, dest, cot, w_in_ref, w_mid_ref, w_out_ref,
    ext, ext_two, parts, hot, moved, within, amsg, rf, t2, rz2, rx, rq, p2, pz2, px, pq, put,
    x2, cot2, xt, ct, wo, h1, slope1, d2, send_b, recv_b,
    mid, io, ra_mid, ra_io, rb_mid, rb_io, sa, sb, r2a, r2b, zs, rz, zs_two, rz_two, mine, ri, r4, full,
    sai, sbi, r2ai, r2bi, zi, rzi, rzi_two, mine_io,
    ssem, rsem, lsem, relay,
):
    d = lax.axis_index("dom")
    y = lax.axis_index("rep")
    c = d % 2
    z = (d // 2) % NZ
    x = d // (2 * NZ)

    def place(xx, yy, zz, cc):
        return ((xx * NZ + zz) * 2 + cc, yy)

    def copy(src, dst, slot, dev):
        return pltpu.make_async_remote_copy(
            src_ref=src, dst_ref=dst, send_sem=ssem.at[slot], recv_sem=rsem.at[slot],
            device_id=dev, device_id_type=MESH,
        )

    def lanes(index, width):
        return pl.ds(pl.multiple_of(index * width, width), width)

    partner = place(x, y, z, 1 - c)
    far = ((d + 2 * c - 1 + 2 * NX * NZ) % (2 * NX * NZ), y)
    xs = [place((x + k) % NX, y, z, c) for k in range(1, NX)]
    xo = [place((x + k) % NX, y, z, 1 - c) for k in range(1, NX)]
    ys = [place(x, (y + k) % NY, z, c) for k in range(1, NY)]
    yo = [place(x, (y + k) % NY, z, 1 - c) for k in range(1, NY)]
    barrier = pltpu.get_barrier_semaphore()
    zs_at = lambda k: place(x, y, (z + k) % NZ, c)
    greeted = [partner, far] + xs + xo + ys + yo + [zs_at(1), zs_at(NZ - 1)]
    for dev in greeted:
        pl.semaphore_signal(barrier, inc=1, device_id=dev, device_id_type=MESH)

    def tell(turn):
        for k in (1 << turn, NZ - (1 << turn)):
            pl.semaphore_signal(
                relay.at[turn], inc=1, device_id=zs_at(k), device_id_type=MESH
            )

    loads = []
    for i, (src, dst) in enumerate((
        (feat_hbm, feat), (dest_hbm, dest), (cot_hbm, cot), (row_hbm, row_ref),
        (col_hbm, col_ref), (tiles_hbm, tiles),
        (w_in_hbm, w_in_ref), (w_out_hbm, w_out_ref), (w_mid_hbm, w_mid_ref),
    )):
        loads.append(pltpu.make_async_copy(src, dst, lsem.at[i]))
        loads[-1].start()
    pl.semaphore_wait(barrier, len(greeted))

    def halo(src, field, slot):
        one = copy(src, field.at[2 * c], slot, partner)
        two = copy(src, field.at[2 * (1 - c)], slot + 1, far)
        two.start()
        one.start()
        return one, two

    def keep_parts(value, slot):
        for i, part in enumerate(split(value)):
            for b in range(4):
                parts[slot * 4 + b, pl.ds(32 * i, 32)] = part[:, 128 * b : 128 * b + 128]

    near, wide = halo(feat_hbm, ext, HALO_ONE)
    tell(0)
    for one in loads[:3]:
        one.wait()
    cot2[c] = jnp.zeros((192, 128), F32)
    cot2[c, 0:172] = cot[...].astype(F32)
    ex_c = copy(cot2.at[c], cot2.at[c], EX_C, partner)
    ex_c.start()
    copies = [near, wide, ex_c]
    keep_parts(feat[...], 1)

    j = lax.broadcasted_iota(jnp.int32, (512, 128), 0)
    target = ((((j >> 1) & 3) * NZ + ((j >> 3) & 15)) * 2 + (j & 1)) * NY + (j >> 7)
    for b in range(4):
        line = dest[pl.ds(b, 1), :]
        hot[:, pl.ds(128 * b, 128)] = jnp.where(target == (line >> 7), 1.0, 0.0).astype(BF16)
        within[:, pl.ds(128 * b, 128)] = jnp.broadcast_to(
            (line & 127).astype(F32), (128, 128)
        ).astype(BF16)

    p2[...] = lax.dot_general(
        hot[lanes(y, 128), :], within[...], TRAILING, preferred_element_type=F32
    ).reshape(NZ, 8, 128)
    pl.semaphore_wait(relay.at[0], 2)
    tell(1)
    mine_xc = x * 2 + c

    def over_z(src, dst, slot):
        def one(k):
            to = (z + k) % NZ
            return copy(src.at[to], dst.at[z], slot + k, place(x, y, to, c))

        def start(k, carry):
            one(k).start()
            return carry

        def recv(k, carry):
            one(k).wait_recv()
            return carry

        def sent(k, carry):
            one(k).wait_send()
            return carry

        return start, recv, sent

    def over_xc(src, dst, slot):
        made = []
        for k in (2, 1, 3, 0):
            to = (x + k) % NX
            if k:
                made.append(copy(src.at[to * 2 + c], dst.at[mine_xc], slot + k, xs[k - 1]))
                made[-1].start()
            dev = xo[k - 1] if k else partner
            made.append(copy(src.at[to * 2 + 1 - c], dst.at[mine_xc], slot + 4 + k, dev))
            made[-1].start()
        return made

    wo[...] = jnp.zeros((192, 1024), BF16)
    for one in loads[3:]:
        one.wait()
    wo[0:172, :] = w_out_ref[...]
    count = count_ref[0]

    def spread(field, near, wide, then=None):
        near.wait_recv()
        keep_parts(field[2 * (1 - c)], 2 * (1 - c))
        wide.wait_recv()
        keep_parts(field[2 * c], 2 * c)
        if then is not None:
            then()

        def slots(i, sums):
            for u in range(5):
                s = i * 5 + u
                at = jnp.minimum((col_ref[s] - 4 * d + 4) & 511, 11)
                product = lax.dot_general(
                    parts[at], tiles[s], TRAILING, preferred_element_type=F32
                )
                total = product[0:32] + product[32:64] + product[64:96]
                row = jnp.where(s < count, row_ref[s], -1)
                sums = tuple(
                    v + jnp.where(row == b, 1.0, 0.0) * total for b, v in enumerate(sums)
                )
            return sums

        zero = jnp.zeros((32, 128), F32)
        return jnp.concatenate(lax.fori_loop(0, 8, slots, (zero,) * 4), axis=1)

    first = spread(ext, near, wide)
    ext_two[1] = first
    near, wide = halo(ext_two.at[1], ext_two, HALO_TWO)
    copies += [near, wide]
    keep_parts(first, 1)
    pl.semaphore_wait(relay.at[1], 2)
    tell(2)
    pz_start, pz_recv, pz_sent = over_z(p2, pz2, Z_P)

    def positions():
        pl.semaphore_wait(relay.at[2], 2)
        lax.fori_loop(1, NZ, pz_start, 0, unroll=True)
        pz2[z] = p2[z]

    second = spread(ext_two, near, wide, positions)
    second = 2.0 * second - feat[...]
    diffused = series_zero * feat[...] + series_one * ext_two[1] + series_two * second

    for i, part in enumerate(split(diffused)):
        moved[pl.ds(32 * i, 32), :] = part
    sorted_rows = lax.dot_general(moved[...], hot[...], TRAILING, preferred_element_type=F32)
    columns = sorted_rows[0:32] + sorted_rows[32:64] + sorted_rows[64:96]
    for i in range(NY):
        amsg[i] = columns[:, 128 * i : 128 * i + 128]
    rep_x = []
    for k in (2, 1, 3):
        to = (y + k) % NY
        rep_x.append(copy(amsg.at[to], rf.at[y], REP_X + k, ys[k - 1]))
        rep_x[-1].start()
    rf[y] = amsg[y]
    for one in rep_x:
        one.wait_recv()
    t2[...] = rf[...].reshape(128, 128).T.reshape(NZ, 8, 128)
    zx_start, zx_recv, zx_sent = over_z(t2, rz2, Z_X)
    lax.fori_loop(1, NZ, zx_start, 0, unroll=True)
    rz2[z] = t2[z]
    lax.fori_loop(1, NZ, pz_recv, 0)
    for i in range(8):
        px[i] = pz2[:, i, :]
    xc_p = over_xc(px, pq, XC_P)
    pq[mine_xc] = px[mine_xc]
    copies += xc_p
    lax.fori_loop(1, NZ, zx_recv, 0, unroll=True)
    for i in range(8):
        rx[i] = rz2[:, i, :]
    xc_x = over_xc(rx, rq, XC_X)
    rq[mine_xc] = rx[mine_xc]
    for one in xc_p:
        one.wait_recv()
    at_lane = lax.broadcasted_iota(jnp.int32, (128, 128), 1).astype(F32)
    put[...] = jnp.where(pq[...].reshape(128, 128) == at_lane, 1.0, 0.0).astype(BF16)
    for one in xc_x:
        one.wait_recv()
    copies += rep_x + xc_x
    lines = jnp.concatenate(split(rq[...].reshape(128, 128).T), axis=0)
    placed = jnp.dot(lines, put[...], preferred_element_type=F32)
    batch = placed[0:128] + placed[128:256] + placed[256:384]
    out_x[...] = batch

    x2[c] = batch
    ex_x = copy(x2.at[c], x2.at[c], EX_X, partner)
    ex_x.start()
    ex_c.wait_recv()
    for i in range(2):
        ct[pl.ds(128 * i, 128), :] = cot2[i].T.astype(BF16)

    for side in (c, 1 - c):
        rows = lanes(side, 128)
        if side is not c:
            ex_x.wait_recv()
        xt[rows, :] = x2[side].T.astype(BF16)
        for j in range(4):
            cols = pl.ds(256 * j, 256)
            pre = jnp.dot(xt[rows, :], w_in_ref[:, cols], preferred_element_type=F32)
            g = sigmoid(pre)
            h1[rows, cols] = (pre * g).astype(BF16)
            slope1[j, rows] = g * (1.0 + pre * (1.0 - g))
    half = lanes(c, 512)
    pre_two = jnp.dot(h1[...], w_mid_ref[:, half], preferred_element_type=F32)
    g_two = sigmoid(pre_two)
    h2 = (pre_two * g_two).astype(BF16)
    back_two = jnp.dot(ct[...], wo[:, half], preferred_element_type=F32)
    d2[...] = (back_two * (g_two * (1.0 + pre_two * (1.0 - g_two)))).astype(BF16)

    send_b[...] = lax.dot_general(
        d2[...], w_mid_ref[lanes(1 - c, 512), half], TRAILING, preferred_element_type=F32
    )
    ex_b = copy(send_b, recv_b, EX_B, partner)
    ex_b.start()

    def send(src, dst, slot, dev):
        one = copy(src, dst, slot, dev)
        one.start()
        copies.append(one)
        return one

    def arrive(made):
        for one in made:
            one.wait_recv()

    copies += [ex_x, ex_b]
    mid_a, mid_b = [], []
    for k in (2, 1, 3, 0):
        to = (x + k) % NX
        rows = lax.dot_general(
            h1[:, lanes(to, 256)], d2[...], LEADING, preferred_element_type=F32
        ).reshape(NZ, 2, 8, 512)
        mid[0, to] = rows[:, 0]
        mid[1, to] = rows[:, 1]

    def send_mid(k, part, slot):
        rows = pl.ds(*part)
        mid_a.append(
            send(
                mid.at[0, (x + k) % NX, rows], ra_mid.at[k - 1, rows], slot, xs[k - 1]
            )
        )
        blocks = pl.ds(part[0] // 4, part[1] // 4)
        mid_b.append(
            send(
                mid.at[1, blocks, :, :, lanes((y + k) % NY, 128)],
                rb_mid.at[k - 1, blocks], slot + 1, ys[k - 1],
            )
        )

    send_mid(1, (0, 8), MID_ONE)
    send_mid(3, (0, 8), MID_ONE + 2)

    cot_rows = [cot2[i].astype(BF16) for i in range(2)]
    grad_out = jnp.dot(
        jnp.concatenate(cot_rows, axis=1), h2, preferred_element_type=F32
    ).reshape(24, 8, 512)
    io[16:40] = grad_out
    own_back = lax.dot_general(
        d2[...], w_mid_ref[half, half], TRAILING, preferred_element_type=F32
    )
    ex_b.wait_recv()
    slope = jnp.concatenate([slope1[2 * c], slope1[2 * c + 1]], axis=1)
    delta_one = ((own_back + recv_b[...]) * slope).astype(BF16)
    x_rows = jnp.concatenate([x2[i].astype(BF16) for i in range(2)], axis=1)
    grad_in = jnp.dot(x_rows, delta_one, preferred_element_type=F32).reshape(16, 8, 512)
    io[0:16] = grad_in

    first_a, first_b = [], []
    for k in (2, 1, 3):
        first_a.append(
            send(io.at[pl.ds((x + k) % NX * 5, 5)], ra_io.at[k - 1], A_IO + k - 1, xs[k - 1])
        )
        first_b.append(
            send(
                io.at[pl.ds(20, 20), :, lanes((y + k) % NY, 128)],
                rb_io.at[k - 1], B_IO + k - 1, ys[k - 1],
            )
        )
    send_mid(1, (8, 8), MID_ONE + 6)
    send_mid(3, (8, 8), MID_ONE + 8)

    y_lane = lanes(y, 128)
    two_io = []
    arrive(first_a)
    sai[...] = io[pl.ds(x * 5, 5)] + ra_io[0] + ra_io[1] + ra_io[2]
    for k in (2, 1, 3):
        two_io.append(
            send(sai.at[:, :, lanes((y + k) % NY, 128)], r2ai.at[k - 1], A_TWO_IO + k - 1, ys[k - 1])
        )
    arrive(first_b)
    sbi[...] = io[20:40, :, y_lane] + rb_io[0] + rb_io[1] + rb_io[2]
    for k in (2, 1, 3):
        two_io.append(
            send(sbi.at[pl.ds((x + k) % NX * 5, 5)], r2bi.at[k - 1], B_TWO_IO + k - 1, xs[k - 1])
        )
    send_mid(2, (0, 16), MID_ONE + 4)
    arrive(two_io)
    io_a = sai[:, :, y_lane] + r2ai[0] + r2ai[1] + r2ai[2]
    io_b = sbi[pl.ds(x * 5, 5)] + r2bi[0] + r2bi[1] + r2bi[2]

    group, spot_z = z // 4, z % 4
    tiles_io = [io_a[t] for t in range(5)] + [io_b[t] for t in range(5)]
    tiles_io += [jnp.zeros((8, 128), F32)] * 2
    for i in range(4):
        for t in range(3):
            zi[i, t] = tiles_io[4 * t + i]
    near_z = [place(x, y, group * 4 + (spot_z + k) % 4, c) for k in range(1, 4)]
    far_z = [place(x, y, (z + 4 * k) % NZ, c) for k in range(1, 4)]
    third_io = []
    for k in (2, 1, 3):
        third_io.append(
            send(zi.at[(spot_z + k) % 4], rzi.at[k - 1], Z_ONE_IO + k, near_z[k - 1])
        )
    arrive(third_io)
    rzi_two[group] = zi[spot_z] + rzi[0] + rzi[1] + rzi[2]
    across_io = []
    for k in (2, 1, 3):
        across_io.append(
            send(rzi_two.at[group], rzi_two.at[group], Z_TWO_IO + k, far_z[k - 1])
        )

    two = []
    arrive(mid_a)
    sa[...] = mid[0, x] + ra_mid[0] + ra_mid[1] + ra_mid[2]
    for k in (2, 1, 3):
        two.append(
            send(sa.at[:, :, lanes((y + k) % NY, 128)], r2a.at[k - 1], A_TWO + k - 1, ys[k - 1])
        )
    arrive(mid_b)
    for i in range(NX):
        sb[i] = mid[1, i, :, :, y_lane] + rb_mid[0, i] + rb_mid[1, i] + rb_mid[2, i]
    for k in (2, 1, 3):
        two.append(send(sb.at[(x + k) % NX], r2b.at[k - 1], B_TWO + k - 1, xs[k - 1]))

    arrive(across_io)
    mine_io[...] = ((rzi_two[0] + rzi_two[1]) + rzi_two[2]) + rzi_two[3]
    share = []
    for k in (2, 1, 3):
        share.append(send(mine_io, ri.at[spot_z], Z_ALL + k, near_z[k - 1]))
    ri[spot_z] = mine_io[...]

    arrive(two)
    sum_a = sa[:, :, y_lane] + r2a[0] + r2a[1] + r2a[2]
    sum_b = sb[x] + r2b[0] + r2b[1] + r2b[2]
    for i in range(4):
        for g in range(4):
            zs[i, g] = sum_a[4 * g + i]
            zs[i, 4 + g] = sum_b[4 * g + i]
    third = []
    for k in (2, 1, 3):
        third.append(send(zs.at[(spot_z + k) % 4], rz.at[k - 1], Z_ONE + k, near_z[k - 1]))

    arrive(share)
    tile = lanes(c * NY + y, 128)
    rows_a, rows_b = pl.ds(x * 5, 5), pl.ds((NX + x) * 5, 5)
    for t in range(10):
        full[(t // 5 * NX + x) * 5 + t % 5, :, tile] = ri[t % 4, t // 4]
    gather = []
    for k in (2, 1, 3):
        spot = full.at[rows_a, :, tile]
        gather.append(send(spot, spot, A_THREE + k - 1, ys[k - 1]))
        spot = full.at[rows_b, :, tile]
        gather.append(send(spot, spot, B_THREE + k - 1, xs[k - 1]))

    arrive(third)
    grouped = zs[spot_z] + rz[0] + rz[1] + rz[2]
    for g in range(4):
        zs_two[g, 0] = grouped[g]
        zs_two[g, 1] = grouped[4 + g]
    across = []
    for k in (2, 1, 3):
        across.append(
            send(zs_two.at[(group + k) % 4], rz_two.at[k - 1], Z_TWO + k, far_z[k - 1])
        )

    arrive(gather)
    fourth = []
    for k in (2, 1, 3):
        spot = full.at[rows_a, :, half]
        fourth.append(send(spot, spot, A_FOUR + k - 1, xs[k - 1]))
        spot = full.at[pl.ds(20, 20), :, tile]
        fourth.append(send(spot, spot, B_FOUR + k - 1, ys[k - 1]))
    arrive(fourth)
    spot = full.at[:, :, half]
    pair = send(spot, spot, PAIR, partner)

    arrive(across)
    mine[...] = zs_two[group] + rz_two[0] + rz_two[1] + rz_two[2]
    last = []
    for k in range(NY):
        if k:
            last.append(send(mine.at[c], r4.at[c, y], MID_ALL + k, ys[k - 1]))
        last.append(
            send(
                mine.at[1 - c], r4.at[c, y], MID_ALL + 4 + k, yo[k - 1] if k else partner
            )
        )
    r4[c, y] = mine[c]
    pair.wait_recv()
    out_in[...] = full[0:16].reshape(128, 1024)
    out_out[...] = full[16:40].reshape(192, 1024)[0:172]
    arrive(last)
    for i in range(8):
        out_mid[:, pl.ds(128 * i, 128)] = r4[i // 4, i % 4]

    lax.fori_loop(1, NZ, pz_sent, 0)
    lax.fori_loop(1, NZ, zx_sent, 0)
    for one in copies:
        one.wait_send()


def write_kernel(*refs):
    writes = [
        pltpu.make_async_copy(refs[i], refs[4 + i], refs[8].at[i]) for i in range(4)
    ]
    for one in writes:
        one.start()
    for one in writes:
        one.wait()


def train(tile_row, tile_col, tile_count, features, tiles, dest, cotangent, w_in, w_mid, w_out):
    vmem = pl.BlockSpec(memory_space=pltpu.VMEM)
    hbm = pl.BlockSpec(memory_space=pltpu.HBM)
    buf = pltpu.VMEM
    return pl.pallas_call(
        train_kernel,
        out_shape=(
            jax.ShapeDtypeStruct((128, 128), F32),
            jax.ShapeDtypeStruct((128, 1024), F32),
            jax.ShapeDtypeStruct((8, 1024), F32),
            jax.ShapeDtypeStruct((172, 1024), F32),
        ),
        in_specs=[pl.BlockSpec(memory_space=pltpu.SMEM)] + [hbm] * 9,
        out_specs=(vmem,) * 4,
        scratch_shapes=[
            pltpu.SMEM((40,), jnp.int32),
            pltpu.SMEM((40,), jnp.int32),
            buf((32, 512), F32),
            buf((40, 128, 128), BF16),
            buf((4, 128), jnp.int32),
            buf((172, 128), BF16),
            buf((128, 1024), BF16),
            buf((1024, 1024), BF16),
            buf((172, 1024), BF16),
            buf((3, 32, 512), F32),
            buf((3, 32, 512), F32),
            buf((12, 96, 128), BF16),
            buf((512, 512), BF16),
            buf((96, 512), BF16),
            buf((128, 512), BF16),
            buf((NY, 32, 128), F32),
            buf((NY, 32, 128), F32),
            buf((NZ, 8, 128), F32),
            buf((NZ, 8, 128), F32),
            buf((8, NZ, 128), F32),
            buf((8, NZ, 128), F32),
            buf((NZ, 8, 128), F32),
            buf((NZ, 8, 128), F32),
            buf((8, NZ, 128), F32),
            buf((8, NZ, 128), F32),
            buf((128, 128), BF16),
            buf((2, 128, 128), F32),
            buf((2, 192, 128), F32),
            buf((256, 128), BF16),
            buf((256, 192), BF16),
            buf((192, 1024), BF16),
            buf((256, 1024), BF16),
            buf((4, 256, 256), F32),
            buf((256, 512), BF16),
            buf((256, 512), F32),
            buf((256, 512), F32),
            buf((2, NX, NZ, 8, 512), F32),
            buf((40, 8, 512), F32),
            buf((3, NZ, 8, 512), F32),
            buf((3, 5, 8, 512), F32),
            buf((3, NX, NZ, 8, 128), F32),
            buf((3, 20, 8, 128), F32),
            buf((NZ, 8, 512), F32),
            buf((NX, NZ, 8, 128), F32),
            buf((3, NZ, 8, 128), F32),
            buf((3, NZ, 8, 128), F32),
            buf((4, 8, 8, 128), F32),
            buf((3, 8, 8, 128), F32),
            buf((4, 2, 8, 128), F32),
            buf((3, 2, 8, 128), F32),
            buf((2, 8, 128), F32),
            buf((4, 3, 8, 128), F32),
            buf((2, NY, 8, 128), F32),
            buf((40, 8, 1024), F32),
            buf((5, 8, 512), F32),
            buf((20, 8, 128), F32),
            buf((3, 5, 8, 128), F32),
            buf((3, 5, 8, 128), F32),
            buf((4, 3, 8, 128), F32),
            buf((3, 3, 8, 128), F32),
            buf((4, 3, 8, 128), F32),
            buf((3, 8, 128), F32),
            pltpu.SemaphoreType.DMA((SEMS,)),
            pltpu.SemaphoreType.DMA((SEMS,)),
            pltpu.SemaphoreType.DMA((9,)),
            pltpu.SemaphoreType.REGULAR((3,)),
        ],
        compiler_params=pltpu.CompilerParams(
            collective_id=0, has_side_effects=True, vmem_limit_bytes=46 * 1024 * 1024
        ),
    )(tile_count, *(pltpu.with_memory_space_constraint(v, pltpu.HBM) for v in (
        tile_row, tile_col, features, tiles, dest, cotangent, w_in, w_mid, w_out
    )))


def shards(
    features, tiles, tile_row, tile_col, tile_count, dest_slot, w_in, w_mid, w_out, cotangent
):
    dest = dest_slot.reshape(4, 128)
    results = train(
        tile_row, tile_col, tile_count, features, tiles, dest, cotangent, w_in, w_mid, w_out
    )
    return pl.pallas_call(
        write_kernel,
        out_shape=tuple(jax.ShapeDtypeStruct(v.shape, v.dtype) for v in results),
        in_specs=[pl.BlockSpec(memory_space=pltpu.VMEM)] * 4,
        out_specs=(pl.BlockSpec(memory_space=pltpu.HBM),) * 4,
        scratch_shapes=[pltpu.SemaphoreType.DMA((4,))],
    )(*(pltpu.with_memory_space_constraint(v, pltpu.VMEM) for v in results))


def solution(mesh):
    in_specs = (
        P("rep", "dom"),
        P("dom", None, None),
        P("dom"),
        P("dom"),
        P("dom"),
        P("dom"),
        P(),
        P(),
        P(),
        P(None, ("dom", "rep")),
    )
    out_specs = (P(None, ("dom", "rep")), P(), P("dom", None), P())
    return jax.shard_map(shards, mesh=mesh, in_specs=in_specs, out_specs=out_specs, check_vma=False)
```

```python
import jax
import jax.numpy as jnp
from jax import lax
from jax.experimental import pallas as pl
from jax.experimental.pallas import tpu as pltpu
from jax.sharding import PartitionSpec as P

series_zero = 0.3085083
series_one = -0.4305395
series_two = 0.1864784
LEADING = (((0,), (0,)), ((), ()))
TRAILING = (((1,), (1,)), ((), ()))
MESH = pl.DeviceIdType.MESH
NX, NY, NZ = 4, 4, 16
F32 = jnp.float32
BF16 = jnp.bfloat16


EX_X, EX_C, EX_B = 0, 1, 2
A_IO, B_IO = 6, 12
A_TWO, B_TWO = 15, 18
Z_ONE, Z_TWO, Z_ALL = 21, 25, 29
MID_ALL = 53
A_THREE, B_THREE, A_FOUR, B_FOUR, PAIR = 61, 64, 67, 70, 73
HALO_ONE, HALO_TWO = 74, 76
REP_X, Z_X, XC_X = 78, 82, 98
Z_P, XC_P = 106, 122
A_TWO_IO, B_TWO_IO, Z_ONE_IO, Z_TWO_IO = 130, 133, 136, 140
MID_ONE = 144
SEMS = 154


def sigmoid(v):
    return 0.5 + 0.5 * jnp.tanh(0.5 * v)


def split(v):
    high = v.astype(BF16)
    rest = v - high.astype(F32)
    middle = rest.astype(BF16)
    low = (rest - middle.astype(F32)).astype(BF16)
    return high, middle, low


def train_kernel(
    count_ref, row_hbm, col_hbm, feat_hbm, tiles_hbm, dest_hbm, cot_hbm, w_in_hbm, w_mid_hbm, w_out_hbm,
    out_x, out_in, out_mid, out_out,
    row_ref, col_ref, feat, tiles, dest, cot, w_in_ref, w_mid_ref, w_out_ref,
    ext, ext_two, parts, hot, moved, within, amsg, rf, t2, rz2, rx, rq, p2, pz2, px, pq, put,
    x2, cot2, xt, ct, wo, h1, slope1, d2, send_b, recv_b,
    mid, io, ra_mid, ra_io, rb_mid, rb_io, sa, sb, r2a, r2b, zs, rz, zs_two, rz_two, mine, ri, r4, full,
    sai, sbi, r2ai, r2bi, zi, rzi, rzi_two, mine_io,
    ssem, rsem, lsem, relay,
):
    d = lax.axis_index("dom")
    y = lax.axis_index("rep")
    c = d % 2
    z = (d // 2) % NZ
    x = d // (2 * NZ)

    def place(xx, yy, zz, cc):
        return ((xx * NZ + zz) * 2 + cc, yy)

    def copy(src, dst, slot, dev):
        return pltpu.make_async_remote_copy(
            src_ref=src, dst_ref=dst, send_sem=ssem.at[slot], recv_sem=rsem.at[slot],
            device_id=dev, device_id_type=MESH,
        )

    def lanes(index, width):
        return pl.ds(pl.multiple_of(index * width, width), width)

    partner = place(x, y, z, 1 - c)
    far = ((d + 2 * c - 1 + 2 * NX * NZ) % (2 * NX * NZ), y)
    xs = [place((x + k) % NX, y, z, c) for k in range(1, NX)]
    xo = [place((x + k) % NX, y, z, 1 - c) for k in range(1, NX)]
    ys = [place(x, (y + k) % NY, z, c) for k in range(1, NY)]
    yo = [place(x, (y + k) % NY, z, 1 - c) for k in range(1, NY)]
    barrier = pltpu.get_barrier_semaphore()
    zs_at = lambda k: place(x, y, (z + k) % NZ, c)
    greeted = [partner, far] + xs + xo + ys + yo + [zs_at(1), zs_at(NZ - 1)]
    for dev in greeted:
        pl.semaphore_signal(barrier, inc=1, device_id=dev, device_id_type=MESH)

    def tell(turn):
        for k in (1 << turn, NZ - (1 << turn)):
            pl.semaphore_signal(
                relay.at[turn], inc=1, device_id=zs_at(k), device_id_type=MESH
            )

    loads = []
    for i, (src, dst) in enumerate((
        (feat_hbm, feat), (dest_hbm, dest), (cot_hbm, cot), (row_hbm, row_ref),
        (col_hbm, col_ref), (tiles_hbm, tiles),
        (w_in_hbm, w_in_ref), (w_out_hbm, w_out_ref), (w_mid_hbm, w_mid_ref),
    )):
        loads.append(pltpu.make_async_copy(src, dst, lsem.at[i]))
        loads[-1].start()
    pl.semaphore_wait(barrier, len(greeted))

    def halo(src, field, slot):
        one = copy(src, field.at[2 * c], slot, partner)
        two = copy(src, field.at[2 * (1 - c)], slot + 1, far)
        two.start()
        one.start()
        return one, two

    def keep_parts(value, slot):
        for i, part in enumerate(split(value)):
            for b in range(4):
                parts[slot * 4 + b, pl.ds(32 * i, 32)] = part[:, 128 * b : 128 * b + 128]

    near, wide = halo(feat_hbm, ext, HALO_ONE)
    tell(0)
    for one in loads[:3]:
        one.wait()
    cot2[c] = jnp.zeros((192, 128), F32)
    cot2[c, 0:172] = cot[...].astype(F32)
    ex_c = copy(cot2.at[c], cot2.at[c], EX_C, partner)
    ex_c.start()
    copies = [near, wide, ex_c]
    keep_parts(feat[...], 1)

    j = lax.broadcasted_iota(jnp.int32, (512, 128), 0)
    target = ((((j >> 1) & 3) * NZ + ((j >> 3) & 15)) * 2 + (j & 1)) * NY + (j >> 7)
    for b in range(4):
        line = dest[pl.ds(b, 1), :]
        hot[:, pl.ds(128 * b, 128)] = jnp.where(target == (line >> 7), 1.0, 0.0).astype(BF16)
        within[:, pl.ds(128 * b, 128)] = jnp.broadcast_to(
            (line & 127).astype(F32), (128, 128)
        ).astype(BF16)

    p2[...] = lax.dot_general(
        hot[lanes(y, 128), :], within[...], TRAILING, preferred_element_type=F32
    ).reshape(NZ, 8, 128)
    pl.semaphore_wait(relay.at[0], 2)
    tell(1)
    mine_xc = x * 2 + c

    def over_z(src, dst, slot):
        def one(k):
            to = (z + k) % NZ
            return copy(src.at[to], dst.at[z], slot + k, place(x, y, to, c))

        def start(k, carry):
            one(k).start()
            return carry

        def recv(k, carry):
            one(k).wait_recv()
            return carry

        def sent(k, carry):
            one(k).wait_send()
            return carry

        return start, recv, sent

    def over_xc(src, dst, slot):
        made = []
        for k in (2, 1, 3, 0):
            to = (x + k) % NX
            if k:
                made.append(copy(src.at[to * 2 + c], dst.at[mine_xc], slot + k, xs[k - 1]))
                made[-1].start()
            dev = xo[k - 1] if k else partner
            made.append(copy(src.at[to * 2 + 1 - c], dst.at[mine_xc], slot + 4 + k, dev))
            made[-1].start()
        return made

    wo[...] = jnp.zeros((192, 1024), BF16)
    for one in loads[3:]:
        one.wait()
    wo[0:172, :] = w_out_ref[...]
    count = count_ref[0]

    def spread(field, near, wide):
        near.wait_recv()
        keep_parts(field[2 * (1 - c)], 2 * (1 - c))
        wide.wait_recv()
        keep_parts(field[2 * c], 2 * c)

        def slots(i, sums):
            for u in range(5):
                s = i * 5 + u
                at = jnp.minimum((col_ref[s] - 4 * d + 4) & 511, 11)
                product = lax.dot_general(
                    parts[at], tiles[s], TRAILING, preferred_element_type=F32
                )
                total = product[0:32] + product[32:64] + product[64:96]
                row = jnp.where(s < count, row_ref[s], -1)
                sums = tuple(
                    v + jnp.where(row == b, 1.0, 0.0) * total for b, v in enumerate(sums)
                )
            return sums

        zero = jnp.zeros((32, 128), F32)
        return jnp.concatenate(lax.fori_loop(0, 8, slots, (zero,) * 4), axis=1)

    first = spread(ext, near, wide)
    ext_two[1] = first
    near, wide = halo(ext_two.at[1], ext_two, HALO_TWO)
    copies += [near, wide]
    keep_parts(first, 1)
    pl.semaphore_wait(relay.at[1], 2)
    tell(2)
    pz_start, pz_recv, pz_sent = over_z(p2, pz2, Z_P)
    second = spread(ext_two, near, wide)
    second = 2.0 * second - feat[...]
    diffused = series_zero * feat[...] + series_one * ext_two[1] + series_two * second

    for i, part in enumerate(split(diffused)):
        moved[pl.ds(32 * i, 32), :] = part
    sorted_rows = lax.dot_general(moved[...], hot[...], TRAILING, preferred_element_type=F32)
    columns = sorted_rows[0:32] + sorted_rows[32:64] + sorted_rows[64:96]
    for i in range(NY):
        amsg[i] = columns[:, 128 * i : 128 * i + 128]
    rep_x = []
    for k in (2, 1, 3):
        to = (y + k) % NY
        rep_x.append(copy(amsg.at[to], rf.at[y], REP_X + k, ys[k - 1]))
        rep_x[-1].start()
    rf[y] = amsg[y]
    pl.semaphore_wait(relay.at[2], 2)
    lax.fori_loop(1, NZ, pz_start, 0, unroll=True)
    pz2[z] = p2[z]
    for one in rep_x:
        one.wait_recv()
    t2[...] = rf[...].reshape(128, 128).T.reshape(NZ, 8, 128)
    zx_start, zx_recv, zx_sent = over_z(t2, rz2, Z_X)
    lax.fori_loop(1, NZ, zx_start, 0, unroll=True)
    rz2[z] = t2[z]
    lax.fori_loop(1, NZ, pz_recv, 0)
    for i in range(8):
        px[i] = pz2[:, i, :]
    xc_p = over_xc(px, pq, XC_P)
    pq[mine_xc] = px[mine_xc]
    copies += xc_p
    lax.fori_loop(1, NZ, zx_recv, 0, unroll=True)
    for i in range(8):
        rx[i] = rz2[:, i, :]
    xc_x = over_xc(rx, rq, XC_X)
    rq[mine_xc] = rx[mine_xc]
    for one in xc_p:
        one.wait_recv()
    at_lane = lax.broadcasted_iota(jnp.int32, (128, 128), 1).astype(F32)
    put[...] = jnp.where(pq[...].reshape(128, 128) == at_lane, 1.0, 0.0).astype(BF16)
    for one in xc_x:
        one.wait_recv()
    copies += rep_x + xc_x
    lines = jnp.concatenate(split(rq[...].reshape(128, 128).T), axis=0)
    placed = jnp.dot(lines, put[...], preferred_element_type=F32)
    batch = placed[0:128] + placed[128:256] + placed[256:384]
    out_x[...] = batch

    x2[c] = batch
    ex_x = copy(x2.at[c], x2.at[c], EX_X, partner)
    ex_x.start()
    ex_c.wait_recv()
    for i in range(2):
        ct[pl.ds(128 * i, 128), :] = cot2[i].T.astype(BF16)

    for side in (c, 1 - c):
        rows = lanes(side, 128)
        if side is not c:
            ex_x.wait_recv()
        xt[rows, :] = x2[side].T.astype(BF16)
        for j in range(4):
            cols = pl.ds(256 * j, 256)
            pre = jnp.dot(xt[rows, :], w_in_ref[:, cols], preferred_element_type=F32)
            g = sigmoid(pre)
            h1[rows, cols] = (pre * g).astype(BF16)
            slope1[j, rows] = g * (1.0 + pre * (1.0 - g))
    half = lanes(c, 512)
    pre_two = jnp.dot(h1[...], w_mid_ref[:, half], preferred_element_type=F32)
    g_two = sigmoid(pre_two)
    h2 = (pre_two * g_two).astype(BF16)
    back_two = jnp.dot(ct[...], wo[:, half], preferred_element_type=F32)
    d2[...] = (back_two * (g_two * (1.0 + pre_two * (1.0 - g_two)))).astype(BF16)

    send_b[...] = lax.dot_general(
        d2[...], w_mid_ref[lanes(1 - c, 512), half], TRAILING, preferred_element_type=F32
    )
    ex_b = copy(send_b, recv_b, EX_B, partner)
    ex_b.start()

    def send(src, dst, slot, dev):
        one = copy(src, dst, slot, dev)
        one.start()
        copies.append(one)
        return one

    def arrive(made):
        for one in made:
            one.wait_recv()

    def drain(made):
        for one in made:
            one.wait_send()

    early, copies = copies + [ex_x, ex_b], []
    mid_a, mid_b = [], []
    for k in (2, 1, 3, 0):
        to = (x + k) % NX
        rows = lax.dot_general(
            h1[:, lanes(to, 256)], d2[...], LEADING, preferred_element_type=F32
        ).reshape(NZ, 2, 8, 512)
        mid[0, to] = rows[:, 0]
        mid[1, to] = rows[:, 1]

    def send_mid(k, part, slot):
        rows = pl.ds(*part)
        mid_a.append(
            send(
                mid.at[0, (x + k) % NX, rows], ra_mid.at[k - 1, rows], slot, xs[k - 1]
            )
        )
        blocks = pl.ds(part[0] // 4, part[1] // 4)
        mid_b.append(
            send(
                mid.at[1, blocks, :, :, lanes((y + k) % NY, 128)],
                rb_mid.at[k - 1, blocks], slot + 1, ys[k - 1],
            )
        )

    send_mid(1, (0, 8), MID_ONE)
    send_mid(3, (0, 8), MID_ONE + 2)

    cot_rows = [cot2[i].astype(BF16) for i in range(2)]
    grad_out = jnp.dot(
        jnp.concatenate(cot_rows, axis=1), h2, preferred_element_type=F32
    ).reshape(24, 8, 512)
    io[16:40] = grad_out
    own_back = lax.dot_general(
        d2[...], w_mid_ref[half, half], TRAILING, preferred_element_type=F32
    )
    ex_b.wait_recv()
    slope = jnp.concatenate([slope1[2 * c], slope1[2 * c + 1]], axis=1)
    delta_one = ((own_back + recv_b[...]) * slope).astype(BF16)
    x_rows = jnp.concatenate([x2[i].astype(BF16) for i in range(2)], axis=1)
    grad_in = jnp.dot(x_rows, delta_one, preferred_element_type=F32).reshape(16, 8, 512)
    io[0:16] = grad_in

    first_a, first_b = [], []
    for k in (2, 1, 3):
        first_a.append(
            send(io.at[pl.ds((x + k) % NX * 5, 5)], ra_io.at[k - 1], A_IO + k - 1, xs[k - 1])
        )
        first_b.append(
            send(
                io.at[pl.ds(20, 20), :, lanes((y + k) % NY, 128)],
                rb_io.at[k - 1], B_IO + k - 1, ys[k - 1],
            )
        )
    send_mid(1, (8, 8), MID_ONE + 6)
    send_mid(3, (8, 8), MID_ONE + 8)

    y_lane = lanes(y, 128)
    two_io = []
    arrive(first_a)
    sai[...] = io[pl.ds(x * 5, 5)] + ra_io[0] + ra_io[1] + ra_io[2]
    for k in (2, 1, 3):
        two_io.append(
            send(sai.at[:, :, lanes((y + k) % NY, 128)], r2ai.at[k - 1], A_TWO_IO + k - 1, ys[k - 1])
        )
    arrive(first_b)
    sbi[...] = io[20:40, :, y_lane] + rb_io[0] + rb_io[1] + rb_io[2]
    for k in (2, 1, 3):
        two_io.append(
            send(sbi.at[pl.ds((x + k) % NX * 5, 5)], r2bi.at[k - 1], B_TWO_IO + k - 1, xs[k - 1])
        )
    send_mid(2, (0, 16), MID_ONE + 4)
    drain(early)
    lax.fori_loop(1, NZ, pz_sent, 0)
    lax.fori_loop(1, NZ, zx_sent, 0)
    arrive(two_io)
    io_a = sai[:, :, y_lane] + r2ai[0] + r2ai[1] + r2ai[2]
    io_b = sbi[pl.ds(x * 5, 5)] + r2bi[0] + r2bi[1] + r2bi[2]

    group, spot_z = z // 4, z % 4
    tiles_io = [io_a[t] for t in range(5)] + [io_b[t] for t in range(5)]
    tiles_io += [jnp.zeros((8, 128), F32)] * 2
    for i in range(4):
        for t in range(3):
            zi[i, t] = tiles_io[4 * t + i]
    near_z = [place(x, y, group * 4 + (spot_z + k) % 4, c) for k in range(1, 4)]
    far_z = [place(x, y, (z + 4 * k) % NZ, c) for k in range(1, 4)]
    third_io = []
    for k in (2, 1, 3):
        third_io.append(
            send(zi.at[(spot_z + k) % 4], rzi.at[k - 1], Z_ONE_IO + k, near_z[k - 1])
        )
    arrive(third_io)
    rzi_two[group] = zi[spot_z] + rzi[0] + rzi[1] + rzi[2]
    across_io = []
    for k in (2, 1, 3):
        across_io.append(
            send(rzi_two.at[group], rzi_two.at[group], Z_TWO_IO + k, far_z[k - 1])
        )

    two = []
    arrive(mid_a)
    sa[...] = mid[0, x] + ra_mid[0] + ra_mid[1] + ra_mid[2]
    for k in (2, 1, 3):
        two.append(
            send(sa.at[:, :, lanes((y + k) % NY, 128)], r2a.at[k - 1], A_TWO + k - 1, ys[k - 1])
        )
    arrive(mid_b)
    for i in range(NX):
        sb[i] = mid[1, i, :, :, y_lane] + rb_mid[0, i] + rb_mid[1, i] + rb_mid[2, i]
    for k in (2, 1, 3):
        two.append(send(sb.at[(x + k) % NX], r2b.at[k - 1], B_TWO + k - 1, xs[k - 1]))

    arrive(across_io)
    mine_io[...] = ((rzi_two[0] + rzi_two[1]) + rzi_two[2]) + rzi_two[3]
    share = []
    for k in (2, 1, 3):
        share.append(send(mine_io, ri.at[spot_z], Z_ALL + k, near_z[k - 1]))
    ri[spot_z] = mine_io[...]

    arrive(two)
    sum_a = sa[:, :, y_lane] + r2a[0] + r2a[1] + r2a[2]
    sum_b = sb[x] + r2b[0] + r2b[1] + r2b[2]
    for i in range(4):
        for g in range(4):
            zs[i, g] = sum_a[4 * g + i]
            zs[i, 4 + g] = sum_b[4 * g + i]
    third = []
    for k in (2, 1, 3):
        third.append(send(zs.at[(spot_z + k) % 4], rz.at[k - 1], Z_ONE + k, near_z[k - 1]))

    arrive(share)
    tile = lanes(c * NY + y, 128)
    rows_a, rows_b = pl.ds(x * 5, 5), pl.ds((NX + x) * 5, 5)
    for t in range(10):
        full[(t // 5 * NX + x) * 5 + t % 5, :, tile] = ri[t % 4, t // 4]
    gather = []
    for k in (2, 1, 3):
        spot = full.at[rows_a, :, tile]
        gather.append(send(spot, spot, A_THREE + k - 1, ys[k - 1]))
        spot = full.at[rows_b, :, tile]
        gather.append(send(spot, spot, B_THREE + k - 1, xs[k - 1]))

    arrive(third)
    grouped = zs[spot_z] + rz[0] + rz[1] + rz[2]
    for g in range(4):
        zs_two[g, 0] = grouped[g]
        zs_two[g, 1] = grouped[4 + g]
    across = []
    for k in (2, 1, 3):
        across.append(
            send(zs_two.at[(group + k) % 4], rz_two.at[k - 1], Z_TWO + k, far_z[k - 1])
        )

    arrive(gather)
    fourth = []
    middle, copies = copies, []
    for k in (2, 1, 3):
        spot = full.at[rows_a, :, half]
        fourth.append(send(spot, spot, A_FOUR + k - 1, xs[k - 1]))
        spot = full.at[pl.ds(20, 20), :, tile]
        fourth.append(send(spot, spot, B_FOUR + k - 1, ys[k - 1]))
    drain(middle)
    arrive(fourth)
    spot = full.at[:, :, half]
    pair = send(spot, spot, PAIR, partner)

    arrive(across)
    mine[...] = zs_two[group] + rz_two[0] + rz_two[1] + rz_two[2]
    last = []
    for k in range(NY):
        if k:
            last.append(send(mine.at[c], r4.at[c, y], MID_ALL + k, ys[k - 1]))
        last.append(
            send(
                mine.at[1 - c], r4.at[c, y], MID_ALL + 4 + k, yo[k - 1] if k else partner
            )
        )
    r4[c, y] = mine[c]
    pair.wait_recv()
    out_in[...] = full[0:16].reshape(128, 1024)
    out_out[...] = full[16:40].reshape(192, 1024)[0:172]
    arrive(last)
    for i in range(8):
        out_mid[:, pl.ds(128 * i, 128)] = r4[i // 4, i % 4]

    drain(copies)


def write_kernel(*refs):
    writes = [
        pltpu.make_async_copy(refs[i], refs[4 + i], refs[8].at[i]) for i in range(4)
    ]
    for one in writes:
        one.start()
    for one in writes:
        one.wait()


def train(tile_row, tile_col, tile_count, features, tiles, dest, cotangent, w_in, w_mid, w_out):
    vmem = pl.BlockSpec(memory_space=pltpu.VMEM)
    hbm = pl.BlockSpec(memory_space=pltpu.HBM)
    buf = pltpu.VMEM
    return pl.pallas_call(
        train_kernel,
        out_shape=(
            jax.ShapeDtypeStruct((128, 128), F32),
            jax.ShapeDtypeStruct((128, 1024), F32),
            jax.ShapeDtypeStruct((8, 1024), F32),
            jax.ShapeDtypeStruct((172, 1024), F32),
        ),
        in_specs=[pl.BlockSpec(memory_space=pltpu.SMEM)] + [hbm] * 9,
        out_specs=(vmem,) * 4,
        scratch_shapes=[
            pltpu.SMEM((40,), jnp.int32),
            pltpu.SMEM((40,), jnp.int32),
            buf((32, 512), F32),
            buf((40, 128, 128), BF16),
            buf((4, 128), jnp.int32),
            buf((172, 128), BF16),
            buf((128, 1024), BF16),
            buf((1024, 1024), BF16),
            buf((172, 1024), BF16),
            buf((3, 32, 512), F32),
            buf((3, 32, 512), F32),
            buf((12, 96, 128), BF16),
            buf((512, 512), BF16),
            buf((96, 512), BF16),
            buf((128, 512), BF16),
            buf((NY, 32, 128), F32),
            buf((NY, 32, 128), F32),
            buf((NZ, 8, 128), F32),
            buf((NZ, 8, 128), F32),
            buf((8, NZ, 128), F32),
            buf((8, NZ, 128), F32),
            buf((NZ, 8, 128), F32),
            buf((NZ, 8, 128), F32),
            buf((8, NZ, 128), F32),
            buf((8, NZ, 128), F32),
            buf((128, 128), BF16),
            buf((2, 128, 128), F32),
            buf((2, 192, 128), F32),
            buf((256, 128), BF16),
            buf((256, 192), BF16),
            buf((192, 1024), BF16),
            buf((256, 1024), BF16),
            buf((4, 256, 256), F32),
            buf((256, 512), BF16),
            buf((256, 512), F32),
            buf((256, 512), F32),
            buf((2, NX, NZ, 8, 512), F32),
            buf((40, 8, 512), F32),
            buf((3, NZ, 8, 512), F32),
            buf((3, 5, 8, 512), F32),
            buf((3, NX, NZ, 8, 128), F32),
            buf((3, 20, 8, 128), F32),
            buf((NZ, 8, 512), F32),
            buf((NX, NZ, 8, 128), F32),
            buf((3, NZ, 8, 128), F32),
            buf((3, NZ, 8, 128), F32),
            buf((4, 8, 8, 128), F32),
            buf((3, 8, 8, 128), F32),
            buf((4, 2, 8, 128), F32),
            buf((3, 2, 8, 128), F32),
            buf((2, 8, 128), F32),
            buf((4, 3, 8, 128), F32),
            buf((2, NY, 8, 128), F32),
            buf((40, 8, 1024), F32),
            buf((5, 8, 512), F32),
            buf((20, 8, 128), F32),
            buf((3, 5, 8, 128), F32),
            buf((3, 5, 8, 128), F32),
            buf((4, 3, 8, 128), F32),
            buf((3, 3, 8, 128), F32),
            buf((4, 3, 8, 128), F32),
            buf((3, 8, 128), F32),
            pltpu.SemaphoreType.DMA((SEMS,)),
            pltpu.SemaphoreType.DMA((SEMS,)),
            pltpu.SemaphoreType.DMA((9,)),
            pltpu.SemaphoreType.REGULAR((3,)),
        ],
        compiler_params=pltpu.CompilerParams(
            collective_id=0, has_side_effects=True, vmem_limit_bytes=46 * 1024 * 1024
        ),
    )(tile_count, *(pltpu.with_memory_space_constraint(v, pltpu.HBM) for v in (
        tile_row, tile_col, features, tiles, dest, cotangent, w_in, w_mid, w_out
    )))


def shards(
    features, tiles, tile_row, tile_col, tile_count, dest_slot, w_in, w_mid, w_out, cotangent
):
    dest = dest_slot.reshape(4, 128)
    results = train(
        tile_row, tile_col, tile_count, features, tiles, dest, cotangent, w_in, w_mid, w_out
    )
    return pl.pallas_call(
        write_kernel,
        out_shape=tuple(jax.ShapeDtypeStruct(v.shape, v.dtype) for v in results),
        in_specs=[pl.BlockSpec(memory_space=pltpu.VMEM)] * 4,
        out_specs=(pl.BlockSpec(memory_space=pltpu.HBM),) * 4,
        scratch_shapes=[pltpu.SemaphoreType.DMA((4,))],
    )(*(pltpu.with_memory_space_constraint(v, pltpu.VMEM) for v in results))


def solution(mesh):
    in_specs = (
        P("rep", "dom"),
        P("dom", None, None),
        P("dom"),
        P("dom"),
        P("dom"),
        P("dom"),
        P(),
        P(),
        P(),
        P(None, ("dom", "rep")),
    )
    out_specs = (P(None, ("dom", "rep")), P(), P("dom", None), P())
    return jax.shard_map(shards, mesh=mesh, in_specs=in_specs, out_specs=out_specs, check_vma=False)
```

```python
import jax
import jax.numpy as jnp
from jax import lax
from jax.experimental import pallas as pl
from jax.experimental.pallas import tpu as pltpu
from jax.sharding import PartitionSpec as P

series_zero = 0.3085083
series_one = -0.4305395
series_two = 0.1864784
LEADING = (((0,), (0,)), ((), ()))
TRAILING = (((1,), (1,)), ((), ()))
MESH = pl.DeviceIdType.MESH
NX, NY, NZ = 4, 4, 16
F32 = jnp.float32
BF16 = jnp.bfloat16


EX_X, EX_C, EX_B = 0, 1, 2
A_IO, B_IO = 6, 12
A_TWO, B_TWO = 15, 18
Z_ONE, Z_TWO, Z_ALL = 21, 25, 29
MID_ALL = 53
A_THREE, B_THREE, A_FOUR, B_FOUR, PAIR = 61, 64, 67, 70, 73
HALO_ONE, HALO_TWO = 74, 76
REP_X, Z_X, XC_X = 78, 82, 98
Z_P, XC_P = 106, 122
A_TWO_IO, B_TWO_IO, Z_ONE_IO, Z_TWO_IO = 130, 133, 136, 140
MID_ONE = 144
SEMS = 154


def sigmoid(v):
    return 0.5 + 0.5 * jnp.tanh(0.5 * v)


def split(v):
    high = v.astype(BF16)
    rest = v - high.astype(F32)
    middle = rest.astype(BF16)
    low = (rest - middle.astype(F32)).astype(BF16)
    return high, middle, low


def train_kernel(
    count_ref, row_hbm, col_hbm, feat_hbm, tiles_hbm, dest_hbm, cot_hbm, w_in_hbm, w_mid_hbm, w_out_hbm,
    out_x, out_in, out_mid, out_out,
    row_ref, col_ref, feat, tiles, dest, cot, w_in_ref, w_mid_ref, w_out_ref,
    ext, ext_two, parts, hot, moved, within, amsg, rf, t2, rz2, rx, rq, p2, pz2, px, pq, put,
    x2, cot2, xt, ct, wo, h1, slope1, d2, send_b, recv_b,
    mid, io, ra_mid, ra_io, rb_mid, rb_io, sa, sb, r2a, r2b, zs, rz, zs_two, rz_two, mine, ri, r4, full,
    sai, sbi, r2ai, r2bi, zi, rzi, rzi_two, mine_io,
    ssem, rsem, lsem, relay,
):
    d = lax.axis_index("dom")
    y = lax.axis_index("rep")
    c = d % 2
    z = (d // 2) % NZ
    x = d // (2 * NZ)

    def place(xx, yy, zz, cc):
        return ((xx * NZ + zz) * 2 + cc, yy)

    def copy(src, dst, slot, dev):
        return pltpu.make_async_remote_copy(
            src_ref=src, dst_ref=dst, send_sem=ssem.at[slot], recv_sem=rsem.at[slot],
            device_id=dev, device_id_type=MESH,
        )

    def lanes(index, width):
        return pl.ds(pl.multiple_of(index * width, width), width)

    partner = place(x, y, z, 1 - c)
    far = ((d + 2 * c - 1 + 2 * NX * NZ) % (2 * NX * NZ), y)
    xs = [place((x + k) % NX, y, z, c) for k in range(1, NX)]
    xo = [place((x + k) % NX, y, z, 1 - c) for k in range(1, NX)]
    ys = [place(x, (y + k) % NY, z, c) for k in range(1, NY)]
    yo = [place(x, (y + k) % NY, z, 1 - c) for k in range(1, NY)]
    barrier = pltpu.get_barrier_semaphore()
    zs_at = lambda k: place(x, y, (z + k) % NZ, c)
    greeted = [partner, far] + xs + xo + ys + yo + [zs_at(1), zs_at(NZ - 1)]
    for dev in greeted:
        pl.semaphore_signal(barrier, inc=1, device_id=dev, device_id_type=MESH)

    def tell(turn):
        for k in (1 << turn, NZ - (1 << turn)):
            pl.semaphore_signal(
                relay.at[turn], inc=1, device_id=zs_at(k), device_id_type=MESH
            )

    loads = []
    for i, (src, dst) in enumerate((
        (feat_hbm, feat), (dest_hbm, dest), (cot_hbm, cot), (row_hbm, row_ref),
        (col_hbm, col_ref), (tiles_hbm, tiles),
        (w_in_hbm, w_in_ref), (w_out_hbm, w_out_ref), (w_mid_hbm, w_mid_ref),
    )):
        loads.append(pltpu.make_async_copy(src, dst, lsem.at[i]))
        loads[-1].start()
    pl.semaphore_wait(barrier, len(greeted))

    def halo(src, field, slot):
        one = copy(src, field.at[2 * c], slot, partner)
        two = copy(src, field.at[2 * (1 - c)], slot + 1, far)
        two.start()
        one.start()
        return one, two

    def keep_parts(value, slot):
        for i, part in enumerate(split(value)):
            for b in range(4):
                parts[slot * 4 + b, pl.ds(32 * i, 32)] = part[:, 128 * b : 128 * b + 128]

    near, wide = halo(feat_hbm, ext, HALO_ONE)
    tell(0)
    for one in loads[:3]:
        one.wait()
    cot2[c] = jnp.zeros((192, 128), F32)
    cot2[c, 0:172] = cot[...].astype(F32)
    ex_c = copy(cot2.at[c], cot2.at[c], EX_C, partner)
    ex_c.start()
    copies = [near, wide, ex_c]
    keep_parts(feat[...], 1)

    j = lax.broadcasted_iota(jnp.int32, (512, 128), 0)
    target = ((((j >> 1) & 3) * NZ + ((j >> 3) & 15)) * 2 + (j & 1)) * NY + (j >> 7)
    for b in range(4):
        line = dest[pl.ds(b, 1), :]
        hot[:, pl.ds(128 * b, 128)] = jnp.where(target == (line >> 7), 1.0, 0.0).astype(BF16)
        within[:, pl.ds(128 * b, 128)] = jnp.broadcast_to(
            (line & 127).astype(F32), (128, 128)
        ).astype(BF16)

    p2[...] = lax.dot_general(
        hot[lanes(y, 128), :], within[...], TRAILING, preferred_element_type=F32
    ).reshape(NZ, 8, 128)
    pl.semaphore_wait(relay.at[0], 2)
    tell(1)
    mine_xc = x * 2 + c

    def over_z(src, dst, slot):
        def one(k):
            to = (z + k) % NZ
            return copy(src.at[to], dst.at[z], slot + k, place(x, y, to, c))

        def start(k, carry):
            one(k).start()
            return carry

        def recv(k, carry):
            one(k).wait_recv()
            return carry

        def sent(k, carry):
            one(k).wait_send()
            return carry

        return start, recv, sent

    def over_xc(src, dst, slot):
        made = []
        for k in (2, 1, 3, 0):
            to = (x + k) % NX
            if k:
                made.append(copy(src.at[to * 2 + c], dst.at[mine_xc], slot + k, xs[k - 1]))
                made[-1].start()
            dev = xo[k - 1] if k else partner
            made.append(copy(src.at[to * 2 + 1 - c], dst.at[mine_xc], slot + 4 + k, dev))
            made[-1].start()
        return made

    wo[...] = jnp.zeros((192, 1024), BF16)
    for one in loads[3:]:
        one.wait()
    wo[0:172, :] = w_out_ref[...]
    count = count_ref[0]

    def spread(field, near, wide, then=None):
        near.wait_recv()
        keep_parts(field[2 * (1 - c)], 2 * (1 - c))
        if then is not None:
            then()
        wide.wait_recv()
        keep_parts(field[2 * c], 2 * c)

        def slots(i, sums):
            for u in range(5):
                s = i * 5 + u
                at = jnp.minimum((col_ref[s] - 4 * d + 4) & 511, 11)
                product = lax.dot_general(
                    parts[at], tiles[s], TRAILING, preferred_element_type=F32
                )
                total = product[0:32] + product[32:64] + product[64:96]
                row = jnp.where(s < count, row_ref[s], -1)
                sums = tuple(
                    v + jnp.where(row == b, 1.0, 0.0) * total for b, v in enumerate(sums)
                )
            return sums

        zero = jnp.zeros((32, 128), F32)
        return jnp.concatenate(lax.fori_loop(0, 8, slots, (zero,) * 4), axis=1)

    first = spread(ext, near, wide)
    ext_two[1] = first
    near, wide = halo(ext_two.at[1], ext_two, HALO_TWO)
    copies += [near, wide]
    keep_parts(first, 1)
    pl.semaphore_wait(relay.at[1], 2)
    tell(2)
    pz_start, pz_recv, pz_sent = over_z(p2, pz2, Z_P)

    def positions():
        pl.semaphore_wait(relay.at[2], 2)
        lax.fori_loop(1, NZ, pz_start, 0, unroll=True)
        pz2[z] = p2[z]

    second = spread(ext_two, near, wide, positions)
    second = 2.0 * second - feat[...]
    diffused = series_zero * feat[...] + series_one * ext_two[1] + series_two * second

    for i, part in enumerate(split(diffused)):
        moved[pl.ds(32 * i, 32), :] = part
    sorted_rows = lax.dot_general(moved[...], hot[...], TRAILING, preferred_element_type=F32)
    columns = sorted_rows[0:32] + sorted_rows[32:64] + sorted_rows[64:96]
    for i in range(NY):
        amsg[i] = columns[:, 128 * i : 128 * i + 128]
    rep_x = []
    for k in (2, 1, 3):
        to = (y + k) % NY
        rep_x.append(copy(amsg.at[to], rf.at[y], REP_X + k, ys[k - 1]))
        rep_x[-1].start()
    rf[y] = amsg[y]
    for one in rep_x:
        one.wait_recv()
    t2[...] = rf[...].reshape(128, 128).T.reshape(NZ, 8, 128)
    zx_start, zx_recv, zx_sent = over_z(t2, rz2, Z_X)
    lax.fori_loop(1, NZ, zx_start, 0, unroll=True)
    rz2[z] = t2[z]
    lax.fori_loop(1, NZ, pz_recv, 0)
    for i in range(8):
        px[i] = pz2[:, i, :]
    xc_p = over_xc(px, pq, XC_P)
    pq[mine_xc] = px[mine_xc]
    copies += xc_p
    lax.fori_loop(1, NZ, zx_recv, 0, unroll=True)
    for i in range(8):
        rx[i] = rz2[:, i, :]
    xc_x = over_xc(rx, rq, XC_X)
    rq[mine_xc] = rx[mine_xc]
    for one in xc_p:
        one.wait_recv()
    at_lane = lax.broadcasted_iota(jnp.int32, (128, 128), 1).astype(F32)
    put[...] = jnp.where(pq[...].reshape(128, 128) == at_lane, 1.0, 0.0).astype(BF16)
    for one in xc_x:
        one.wait_recv()
    copies += rep_x + xc_x
    lines = jnp.concatenate(split(rq[...].reshape(128, 128).T), axis=0)
    placed = jnp.dot(lines, put[...], preferred_element_type=F32)
    batch = placed[0:128] + placed[128:256] + placed[256:384]
    out_x[...] = batch

    x2[c] = batch
    ex_x = copy(x2.at[c], x2.at[c], EX_X, partner)
    ex_x.start()
    ex_c.wait_recv()
    for i in range(2):
        ct[pl.ds(128 * i, 128), :] = cot2[i].T.astype(BF16)

    for side in (c, 1 - c):
        rows = lanes(side, 128)
        if side is not c:
            ex_x.wait_recv()
        xt[rows, :] = x2[side].T.astype(BF16)
        for j in range(4):
            cols = pl.ds(256 * j, 256)
            pre = jnp.dot(xt[rows, :], w_in_ref[:, cols], preferred_element_type=F32)
            g = sigmoid(pre)
            h1[rows, cols] = (pre * g).astype(BF16)
            slope1[j, rows] = g * (1.0 + pre * (1.0 - g))
    half = lanes(c, 512)
    pre_two = jnp.dot(h1[...], w_mid_ref[:, half], preferred_element_type=F32)
    g_two = sigmoid(pre_two)
    h2 = (pre_two * g_two).astype(BF16)
    back_two = jnp.dot(ct[...], wo[:, half], preferred_element_type=F32)
    d2[...] = (back_two * (g_two * (1.0 + pre_two * (1.0 - g_two)))).astype(BF16)

    send_b[...] = lax.dot_general(
        d2[...], w_mid_ref[lanes(1 - c, 512), half], TRAILING, preferred_element_type=F32
    )
    ex_b = copy(send_b, recv_b, EX_B, partner)
    ex_b.start()

    def send(src, dst, slot, dev):
        one = copy(src, dst, slot, dev)
        one.start()
        copies.append(one)
        return one

    def arrive(made):
        for one in made:
            one.wait_recv()

    def drain(made):
        for one in made:
            one.wait_send()

    early, copies = copies + [ex_x, ex_b], []
    mid_a, mid_b = [], []
    for k in (2, 1, 3, 0):
        to = (x + k) % NX
        rows = lax.dot_general(
            h1[:, lanes(to, 256)], d2[...], LEADING, preferred_element_type=F32
        ).reshape(NZ, 2, 8, 512)
        mid[0, to] = rows[:, 0]
        mid[1, to] = rows[:, 1]

    def send_mid(k, part, slot):
        rows = pl.ds(*part)
        mid_a.append(
            send(
                mid.at[0, (x + k) % NX, rows], ra_mid.at[k - 1, rows], slot, xs[k - 1]
            )
        )
        blocks = pl.ds(part[0] // 4, part[1] // 4)
        mid_b.append(
            send(
                mid.at[1, blocks, :, :, lanes((y + k) % NY, 128)],
                rb_mid.at[k - 1, blocks], slot + 1, ys[k - 1],
            )
        )

    send_mid(1, (0, 8), MID_ONE)
    send_mid(3, (0, 8), MID_ONE + 2)

    cot_rows = [cot2[i].astype(BF16) for i in range(2)]
    grad_out = jnp.dot(
        jnp.concatenate(cot_rows, axis=1), h2, preferred_element_type=F32
    ).reshape(24, 8, 512)
    io[16:40] = grad_out
    own_back = lax.dot_general(
        d2[...], w_mid_ref[half, half], TRAILING, preferred_element_type=F32
    )
    ex_b.wait_recv()
    slope = jnp.concatenate([slope1[2 * c], slope1[2 * c + 1]], axis=1)
    delta_one = ((own_back + recv_b[...]) * slope).astype(BF16)
    x_rows = jnp.concatenate([x2[i].astype(BF16) for i in range(2)], axis=1)
    grad_in = jnp.dot(x_rows, delta_one, preferred_element_type=F32).reshape(16, 8, 512)
    io[0:16] = grad_in

    first_a, first_b = [], []
    for k in (2, 1, 3):
        first_a.append(
            send(io.at[pl.ds((x + k) % NX * 5, 5)], ra_io.at[k - 1], A_IO + k - 1, xs[k - 1])
        )
        first_b.append(
            send(
                io.at[pl.ds(20, 20), :, lanes((y + k) % NY, 128)],
                rb_io.at[k - 1], B_IO + k - 1, ys[k - 1],
            )
        )
    send_mid(1, (8, 8), MID_ONE + 6)
    send_mid(3, (8, 8), MID_ONE + 8)

    y_lane = lanes(y, 128)
    two_io = []
    arrive(first_a)
    sai[...] = io[pl.ds(x * 5, 5)] + ra_io[0] + ra_io[1] + ra_io[2]
    for k in (2, 1, 3):
        two_io.append(
            send(sai.at[:, :, lanes((y + k) % NY, 128)], r2ai.at[k - 1], A_TWO_IO + k - 1, ys[k - 1])
        )
    arrive(first_b)
    sbi[...] = io[20:40, :, y_lane] + rb_io[0] + rb_io[1] + rb_io[2]
    for k in (2, 1, 3):
        two_io.append(
            send(sbi.at[pl.ds((x + k) % NX * 5, 5)], r2bi.at[k - 1], B_TWO_IO + k - 1, xs[k - 1])
        )
    send_mid(2, (0, 16), MID_ONE + 4)
    drain(early)
    lax.fori_loop(1, NZ, pz_sent, 0)
    lax.fori_loop(1, NZ, zx_sent, 0)
    arrive(two_io)
    io_a = sai[:, :, y_lane] + r2ai[0] + r2ai[1] + r2ai[2]
    io_b = sbi[pl.ds(x * 5, 5)] + r2bi[0] + r2bi[1] + r2bi[2]

    group, spot_z = z // 4, z % 4
    tiles_io = [io_a[t] for t in range(5)] + [io_b[t] for t in range(5)]
    tiles_io += [jnp.zeros((8, 128), F32)] * 2
    for i in range(4):
        for t in range(3):
            zi[i, t] = tiles_io[4 * t + i]
    near_z = [place(x, y, group * 4 + (spot_z + k) % 4, c) for k in range(1, 4)]
    far_z = [place(x, y, (z + 4 * k) % NZ, c) for k in range(1, 4)]
    third_io = []
    for k in (2, 1, 3):
        third_io.append(
            send(zi.at[(spot_z + k) % 4], rzi.at[k - 1], Z_ONE_IO + k, near_z[k - 1])
        )
    arrive(third_io)
    rzi_two[group] = zi[spot_z] + rzi[0] + rzi[1] + rzi[2]
    across_io = []
    for k in (2, 1, 3):
        across_io.append(
            send(rzi_two.at[group], rzi_two.at[group], Z_TWO_IO + k, far_z[k - 1])
        )

    two = []
    arrive(mid_a)
    sa[...] = mid[0, x] + ra_mid[0] + ra_mid[1] + ra_mid[2]
    for k in (2, 1, 3):
        two.append(
            send(sa.at[:, :, lanes((y + k) % NY, 128)], r2a.at[k - 1], A_TWO + k - 1, ys[k - 1])
        )
    arrive(mid_b)
    for i in range(NX):
        sb[i] = mid[1, i, :, :, y_lane] + rb_mid[0, i] + rb_mid[1, i] + rb_mid[2, i]
    for k in (2, 1, 3):
        two.append(send(sb.at[(x + k) % NX], r2b.at[k - 1], B_TWO + k - 1, xs[k - 1]))

    arrive(across_io)
    mine_io[...] = ((rzi_two[0] + rzi_two[1]) + rzi_two[2]) + rzi_two[3]
    share = []
    for k in (2, 1, 3):
        share.append(send(mine_io, ri.at[spot_z], Z_ALL + k, near_z[k - 1]))
    ri[spot_z] = mine_io[...]

    arrive(two)
    sum_a = sa[:, :, y_lane] + r2a[0] + r2a[1] + r2a[2]
    sum_b = sb[x] + r2b[0] + r2b[1] + r2b[2]
    for i in range(4):
        for g in range(4):
            zs[i, g] = sum_a[4 * g + i]
            zs[i, 4 + g] = sum_b[4 * g + i]
    third = []
    for k in (2, 1, 3):
        third.append(send(zs.at[(spot_z + k) % 4], rz.at[k - 1], Z_ONE + k, near_z[k - 1]))

    arrive(share)
    tile = lanes(c * NY + y, 128)
    rows_a, rows_b = pl.ds(x * 5, 5), pl.ds((NX + x) * 5, 5)
    for t in range(10):
        full[(t // 5 * NX + x) * 5 + t % 5, :, tile] = ri[t % 4, t // 4]
    gather = []
    for k in (2, 1, 3):
        spot = full.at[rows_a, :, tile]
        gather.append(send(spot, spot, A_THREE + k - 1, ys[k - 1]))
        spot = full.at[rows_b, :, tile]
        gather.append(send(spot, spot, B_THREE + k - 1, xs[k - 1]))

    arrive(third)
    grouped = zs[spot_z] + rz[0] + rz[1] + rz[2]
    for g in range(4):
        zs_two[g, 0] = grouped[g]
        zs_two[g, 1] = grouped[4 + g]
    across = []
    for k in (2, 1, 3):
        across.append(
            send(zs_two.at[(group + k) % 4], rz_two.at[k - 1], Z_TWO + k, far_z[k - 1])
        )

    arrive(gather)
    fourth = []
    middle, copies = copies, []
    for k in (2, 1, 3):
        spot = full.at[rows_a, :, half]
        fourth.append(send(spot, spot, A_FOUR + k - 1, xs[k - 1]))
        spot = full.at[pl.ds(20, 20), :, tile]
        fourth.append(send(spot, spot, B_FOUR + k - 1, ys[k - 1]))
    drain(middle)
    arrive(fourth)
    spot = full.at[:, :, half]
    pair = send(spot, spot, PAIR, partner)

    arrive(across)
    mine[...] = zs_two[group] + rz_two[0] + rz_two[1] + rz_two[2]
    last = []
    for k in range(NY):
        if k:
            last.append(send(mine.at[c], r4.at[c, y], MID_ALL + k, ys[k - 1]))
        last.append(
            send(
                mine.at[1 - c], r4.at[c, y], MID_ALL + 4 + k, yo[k - 1] if k else partner
            )
        )
    r4[c, y] = mine[c]
    pair.wait_recv()
    out_in[...] = full[0:16].reshape(128, 1024)
    out_out[...] = full[16:40].reshape(192, 1024)[0:172]
    arrive(last)
    for i in range(8):
        out_mid[:, pl.ds(128 * i, 128)] = r4[i // 4, i % 4]

    drain(copies)


def write_kernel(*refs):
    writes = [
        pltpu.make_async_copy(refs[i], refs[4 + i], refs[8].at[i]) for i in range(4)
    ]
    for one in writes:
        one.start()
    for one in writes:
        one.wait()


def train(tile_row, tile_col, tile_count, features, tiles, dest, cotangent, w_in, w_mid, w_out):
    vmem = pl.BlockSpec(memory_space=pltpu.VMEM)
    hbm = pl.BlockSpec(memory_space=pltpu.HBM)
    buf = pltpu.VMEM
    return pl.pallas_call(
        train_kernel,
        out_shape=(
            jax.ShapeDtypeStruct((128, 128), F32),
            jax.ShapeDtypeStruct((128, 1024), F32),
            jax.ShapeDtypeStruct((8, 1024), F32),
            jax.ShapeDtypeStruct((172, 1024), F32),
        ),
        in_specs=[pl.BlockSpec(memory_space=pltpu.SMEM)] + [hbm] * 9,
        out_specs=(vmem,) * 4,
        scratch_shapes=[
            pltpu.SMEM((40,), jnp.int32),
            pltpu.SMEM((40,), jnp.int32),
            buf((32, 512), F32),
            buf((40, 128, 128), BF16),
            buf((4, 128), jnp.int32),
            buf((172, 128), BF16),
            buf((128, 1024), BF16),
            buf((1024, 1024), BF16),
            buf((172, 1024), BF16),
            buf((3, 32, 512), F32),
            buf((3, 32, 512), F32),
            buf((12, 96, 128), BF16),
            buf((512, 512), BF16),
            buf((96, 512), BF16),
            buf((128, 512), BF16),
            buf((NY, 32, 128), F32),
            buf((NY, 32, 128), F32),
            buf((NZ, 8, 128), F32),
            buf((NZ, 8, 128), F32),
            buf((8, NZ, 128), F32),
            buf((8, NZ, 128), F32),
            buf((NZ, 8, 128), F32),
            buf((NZ, 8, 128), F32),
            buf((8, NZ, 128), F32),
            buf((8, NZ, 128), F32),
            buf((128, 128), BF16),
            buf((2, 128, 128), F32),
            buf((2, 192, 128), F32),
            buf((256, 128), BF16),
            buf((256, 192), BF16),
            buf((192, 1024), BF16),
            buf((256, 1024), BF16),
            buf((4, 256, 256), F32),
            buf((256, 512), BF16),
            buf((256, 512), F32),
            buf((256, 512), F32),
            buf((2, NX, NZ, 8, 512), F32),
            buf((40, 8, 512), F32),
            buf((3, NZ, 8, 512), F32),
            buf((3, 5, 8, 512), F32),
            buf((3, NX, NZ, 8, 128), F32),
            buf((3, 20, 8, 128), F32),
            buf((NZ, 8, 512), F32),
            buf((NX, NZ, 8, 128), F32),
            buf((3, NZ, 8, 128), F32),
            buf((3, NZ, 8, 128), F32),
            buf((4, 8, 8, 128), F32),
            buf((3, 8, 8, 128), F32),
            buf((4, 2, 8, 128), F32),
            buf((3, 2, 8, 128), F32),
            buf((2, 8, 128), F32),
            buf((4, 3, 8, 128), F32),
            buf((2, NY, 8, 128), F32),
            buf((40, 8, 1024), F32),
            buf((5, 8, 512), F32),
            buf((20, 8, 128), F32),
            buf((3, 5, 8, 128), F32),
            buf((3, 5, 8, 128), F32),
            buf((4, 3, 8, 128), F32),
            buf((3, 3, 8, 128), F32),
            buf((4, 3, 8, 128), F32),
            buf((3, 8, 128), F32),
            pltpu.SemaphoreType.DMA((SEMS,)),
            pltpu.SemaphoreType.DMA((SEMS,)),
            pltpu.SemaphoreType.DMA((9,)),
            pltpu.SemaphoreType.REGULAR((3,)),
        ],
        compiler_params=pltpu.CompilerParams(
            collective_id=0, has_side_effects=True, vmem_limit_bytes=46 * 1024 * 1024
        ),
    )(tile_count, *(pltpu.with_memory_space_constraint(v, pltpu.HBM) for v in (
        tile_row, tile_col, features, tiles, dest, cotangent, w_in, w_mid, w_out
    )))


def shards(
    features, tiles, tile_row, tile_col, tile_count, dest_slot, w_in, w_mid, w_out, cotangent
):
    dest = dest_slot.reshape(4, 128)
    results = train(
        tile_row, tile_col, tile_count, features, tiles, dest, cotangent, w_in, w_mid, w_out
    )
    return pl.pallas_call(
        write_kernel,
        out_shape=tuple(jax.ShapeDtypeStruct(v.shape, v.dtype) for v in results),
        in_specs=[pl.BlockSpec(memory_space=pltpu.VMEM)] * 4,
        out_specs=(pl.BlockSpec(memory_space=pltpu.HBM),) * 4,
        scratch_shapes=[pltpu.SemaphoreType.DMA((4,))],
    )(*(pltpu.with_memory_space_constraint(v, pltpu.VMEM) for v in results))


def solution(mesh):
    in_specs = (
        P("rep", "dom"),
        P("dom", None, None),
        P("dom"),
        P("dom"),
        P("dom"),
        P("dom"),
        P(),
        P(),
        P(),
        P(None, ("dom", "rep")),
    )
    out_specs = (P(None, ("dom", "rep")), P(), P("dom", None), P())
    return jax.shard_map(shards, mesh=mesh, in_specs=in_specs, out_specs=out_specs, check_vma=False)
```

```python
import jax
import jax.numpy as jnp
from jax import lax
from jax.experimental import pallas as pl
from jax.experimental.pallas import tpu as pltpu
from jax.sharding import PartitionSpec as P

series_zero = 0.3085083
series_one = -0.4305395
series_two = 0.1864784
LEADING = (((0,), (0,)), ((), ()))
TRAILING = (((1,), (1,)), ((), ()))
MESH = pl.DeviceIdType.MESH
NX, NY, NZ = 4, 4, 16
F32 = jnp.float32
BF16 = jnp.bfloat16


EX_X, EX_C, EX_B = 0, 1, 2
A_IO, B_IO = 6, 12
A_TWO, B_TWO = 15, 18
Z_ONE, Z_TWO, Z_ALL = 21, 25, 29
MID_ALL = 53
A_THREE, B_THREE, A_FOUR, B_FOUR, PAIR = 61, 64, 67, 70, 73
HALO_ONE, HALO_TWO = 74, 76
REP_X, Z_X, XC_X = 78, 82, 98
Z_P, XC_P = 106, 122
A_TWO_IO, B_TWO_IO, Z_ONE_IO, Z_TWO_IO = 130, 133, 136, 140
MID_ONE = 144
SEMS = 154


def sigmoid(v):
    return 0.5 + 0.5 * jnp.tanh(0.5 * v)


def split(v):
    high = v.astype(BF16)
    rest = v - high.astype(F32)
    middle = rest.astype(BF16)
    low = (rest - middle.astype(F32)).astype(BF16)
    return high, middle, low


def train_kernel(
    count_ref, row_hbm, col_hbm, feat_hbm, tiles_hbm, dest_hbm, cot_hbm, w_in_hbm, w_mid_hbm, w_out_hbm,
    out_x, out_in, out_mid, out_out,
    row_ref, col_ref, feat, tiles, dest, cot, w_in_ref, w_mid_ref, w_out_ref,
    ext, ext_two, parts, hot, moved, within, amsg, rf, t2, rz2, rx, rq, p2, pz2, px, pq, put,
    x2, cot2, xt, ct, wo, h1, slope1, d2, send_b, recv_b,
    mid, io, ra_mid, ra_io, rb_mid, rb_io, sa, sb, r2a, r2b, zs, rz, zs_two, rz_two, mine, ri, r4, full,
    sai, sbi, r2ai, r2bi, zi, rzi, rzi_two, mine_io,
    ssem, rsem, lsem, relay,
):
    loads = []
    for i, (src, dst) in enumerate((
        (feat_hbm, feat), (dest_hbm, dest), (cot_hbm, cot), (row_hbm, row_ref),
        (col_hbm, col_ref), (tiles_hbm, tiles),
        (w_in_hbm, w_in_ref), (w_out_hbm, w_out_ref), (w_mid_hbm, w_mid_ref),
    )):
        loads.append(pltpu.make_async_copy(src, dst, lsem.at[i]))
        loads[-1].start()
    d = lax.axis_index("dom")
    y = lax.axis_index("rep")
    c = d % 2
    z = (d // 2) % NZ
    x = d // (2 * NZ)

    def place(xx, yy, zz, cc):
        return ((xx * NZ + zz) * 2 + cc, yy)

    def copy(src, dst, slot, dev):
        return pltpu.make_async_remote_copy(
            src_ref=src, dst_ref=dst, send_sem=ssem.at[slot], recv_sem=rsem.at[slot],
            device_id=dev, device_id_type=MESH,
        )

    def lanes(index, width):
        return pl.ds(pl.multiple_of(index * width, width), width)

    partner = place(x, y, z, 1 - c)
    far = ((d + 2 * c - 1 + 2 * NX * NZ) % (2 * NX * NZ), y)
    xs = [place((x + k) % NX, y, z, c) for k in range(1, NX)]
    xo = [place((x + k) % NX, y, z, 1 - c) for k in range(1, NX)]
    ys = [place(x, (y + k) % NY, z, c) for k in range(1, NY)]
    yo = [place(x, (y + k) % NY, z, 1 - c) for k in range(1, NY)]
    barrier = pltpu.get_barrier_semaphore()
    zs_at = lambda k: place(x, y, (z + k) % NZ, c)
    greeted = [partner, far] + xs + xo + ys + yo + [zs_at(1), zs_at(NZ - 1)]
    for dev in greeted:
        pl.semaphore_signal(barrier, inc=1, device_id=dev, device_id_type=MESH)

    def tell(turn):
        for k in (1 << turn, NZ - (1 << turn)):
            pl.semaphore_signal(
                relay.at[turn], inc=1, device_id=zs_at(k), device_id_type=MESH
            )

    for one in loads[:3]:
        one.wait()
    own = jnp.stack([feat[:, pl.ds(128 * b, 128)] for b in range(4)])
    ext[4:8] = own
    for i, part in enumerate(split(own)):
        parts[4:8, pl.ds(32 * i, 32)] = part
    cot2[c] = jnp.zeros((192, 128), F32)
    cot2[c, 0:172] = cot[...].astype(F32)
    j = lax.broadcasted_iota(jnp.int32, (512, 128), 0)
    target = ((((j >> 1) & 3) * NZ + ((j >> 3) & 15)) * 2 + (j & 1)) * NY + (j >> 7)
    for b in range(4):
        line = dest[pl.ds(b, 1), :]
        hot[:, pl.ds(128 * b, 128)] = jnp.where(target == (line >> 7), 1.0, 0.0).astype(BF16)
        within[:, pl.ds(128 * b, 128)] = jnp.broadcast_to(
            (line & 127).astype(F32), (128, 128)
        ).astype(BF16)

    p2[...] = lax.dot_general(
        hot[lanes(y, 128), :], within[...], TRAILING, preferred_element_type=F32
    ).reshape(NZ, 8, 128)
    pl.semaphore_wait(barrier, len(greeted))
    tell(0)

    def halo(field, slot):
        one = copy(field.at[pl.ds(4, 4)], field.at[pl.ds(8 * c, 4)], slot, partner)
        two = copy(field.at[pl.ds(4, 4)], field.at[pl.ds(8 * (1 - c), 4)], slot + 1, far)
        two.start()
        one.start()
        return one, two

    near, wide = halo(ext, HALO_ONE)
    ex_c = copy(cot2.at[c], cot2.at[c], EX_C, partner)
    ex_c.start()
    copies = [near, wide, ex_c]
    mine_xc = x * 2 + c

    def over_z(src, dst, slot):
        def one(k):
            to = (z + k) % NZ
            return copy(src.at[to], dst.at[z], slot + k, place(x, y, to, c))

        def start(k, carry):
            one(k).start()
            return carry

        def recv(k, carry):
            one(k).wait_recv()
            return carry

        def sent(k, carry):
            one(k).wait_send()
            return carry

        return start, recv, sent

    def over_xc(src, dst, slot):
        made = []
        for k in (2, 1, 3, 0):
            to = (x + k) % NX
            if k:
                made.append(copy(src.at[to * 2 + c], dst.at[mine_xc], slot + k, xs[k - 1]))
                made[-1].start()
            dev = xo[k - 1] if k else partner
            made.append(copy(src.at[to * 2 + 1 - c], dst.at[mine_xc], slot + 4 + k, dev))
            made[-1].start()
        return made

    wo[...] = jnp.zeros((192, 1024), BF16)
    for one in loads[3:]:
        one.wait()
    wo[0:172, :] = w_out_ref[...]
    pl.semaphore_wait(relay.at[0], 2)
    tell(1)

    count = count_ref[0]

    def spread(field, near, wide, then=None):
        near.wait_recv()
        for i, part in enumerate(split(field[pl.ds(8 * (1 - c), 4)])):
            parts[pl.ds(8 * (1 - c), 4), pl.ds(32 * i, 32)] = part
        wide.wait_recv()
        for i, part in enumerate(split(field[pl.ds(8 * c, 4)])):
            parts[pl.ds(8 * c, 4), pl.ds(32 * i, 32)] = part
        if then is not None:
            then()

        def slots(i, sums):
            for u in range(10):
                s = i * 10 + u
                at = jnp.minimum((col_ref[s] - 4 * d + 4) & 511, 11)
                product = lax.dot_general(
                    parts[at], tiles[s], TRAILING, preferred_element_type=F32
                )
                total = product[0:32] + product[32:64] + product[64:96]
                row = jnp.where(s < count, row_ref[s], -1)
                sums = tuple(
                    v + jnp.where(row == b, 1.0, 0.0) * total for b, v in enumerate(sums)
                )
            return sums

        zero = jnp.zeros((32, 128), F32)
        return jnp.stack(lax.fori_loop(0, 4, slots, (zero,) * 4))

    first = spread(ext, near, wide)
    ext_two[4:8] = first
    near, wide = halo(ext_two, HALO_TWO)
    copies += [near, wide]
    for i, part in enumerate(split(first)):
        parts[4:8, pl.ds(32 * i, 32)] = part
    pl.semaphore_wait(relay.at[1], 2)
    tell(2)
    pz_start, pz_recv, pz_sent = over_z(p2, pz2, Z_P)

    def positions():
        pl.semaphore_wait(relay.at[2], 2)
        lax.fori_loop(1, NZ, pz_start, 0, unroll=True)
        pz2[z] = p2[z]

    second = spread(ext_two, near, wide, positions)
    second = 2.0 * second - ext[4:8]
    diffused = series_zero * ext[4:8] + series_one * ext_two[4:8] + series_two * second

    for i, part in enumerate(split(diffused)):
        for b in range(4):
            moved[pl.ds(32 * i, 32), pl.ds(128 * b, 128)] = part[b]
    sorted_rows = lax.dot_general(moved[...], hot[...], TRAILING, preferred_element_type=F32)
    columns = sorted_rows[0:32] + sorted_rows[32:64] + sorted_rows[64:96]
    for i in range(NY):
        amsg[i] = columns[:, 128 * i : 128 * i + 128]
    rep_x = []
    for k in (2, 1, 3):
        to = (y + k) % NY
        rep_x.append(copy(amsg.at[to], rf.at[y], REP_X + k, ys[k - 1]))
        rep_x[-1].start()
    rf[y] = amsg[y]
    for one in rep_x:
        one.wait_recv()
    t2[...] = rf[...].reshape(128, 128).T.reshape(NZ, 8, 128)
    zx_start, zx_recv, zx_sent = over_z(t2, rz2, Z_X)
    lax.fori_loop(1, NZ, zx_start, 0, unroll=True)
    rz2[z] = t2[z]
    lax.fori_loop(1, NZ, pz_recv, 0)
    for i in range(8):
        px[i] = pz2[:, i, :]
    xc_p = over_xc(px, pq, XC_P)
    pq[mine_xc] = px[mine_xc]
    copies += xc_p
    lax.fori_loop(1, NZ, zx_recv, 0, unroll=True)
    for i in range(8):
        rx[i] = rz2[:, i, :]
    xc_x = over_xc(rx, rq, XC_X)
    rq[mine_xc] = rx[mine_xc]
    for one in xc_p:
        one.wait_recv()
    at_lane = lax.broadcasted_iota(jnp.int32, (128, 128), 1).astype(F32)
    put[...] = jnp.where(pq[...].reshape(128, 128) == at_lane, 1.0, 0.0).astype(BF16)
    for one in xc_x:
        one.wait_recv()
    copies += rep_x + xc_x
    lines = jnp.concatenate(split(rq[...].reshape(128, 128).T), axis=0)
    placed = jnp.dot(lines, put[...], preferred_element_type=F32)
    batch = placed[0:128] + placed[128:256] + placed[256:384]
    out_x[...] = batch

    x2[c] = batch
    ex_x = copy(x2.at[c], x2.at[c], EX_X, partner)
    ex_x.start()
    ex_c.wait_recv()
    for i in range(2):
        ct[pl.ds(128 * i, 128), :] = cot2[i].T.astype(BF16)

    for side in (c, 1 - c):
        rows = lanes(side, 128)
        if side is not c:
            ex_x.wait_recv()
        xt[rows, :] = x2[side].T.astype(BF16)
        for j in range(4):
            cols = pl.ds(256 * j, 256)
            pre = jnp.dot(xt[rows, :], w_in_ref[:, cols], preferred_element_type=F32)
            g = sigmoid(pre)
            h1[rows, cols] = (pre * g).astype(BF16)
            slope1[j, rows] = g * (1.0 + pre * (1.0 - g))
    half = lanes(c, 512)
    pre_two = jnp.dot(h1[...], w_mid_ref[:, half], preferred_element_type=F32)
    g_two = sigmoid(pre_two)
    h2 = (pre_two * g_two).astype(BF16)
    back_two = jnp.dot(ct[...], wo[:, half], preferred_element_type=F32)
    d2[...] = (back_two * (g_two * (1.0 + pre_two * (1.0 - g_two)))).astype(BF16)

    send_b[...] = lax.dot_general(
        d2[...], w_mid_ref[lanes(1 - c, 512), half], TRAILING, preferred_element_type=F32
    )
    ex_b = copy(send_b, recv_b, EX_B, partner)
    ex_b.start()

    def send(src, dst, slot, dev):
        one = copy(src, dst, slot, dev)
        one.start()
        copies.append(one)
        return one

    def arrive(made):
        for one in made:
            one.wait_recv()

    copies += [ex_x, ex_b]
    mid_a, mid_b = [], []
    for k in (2, 1, 3, 0):
        to = (x + k) % NX
        rows = lax.dot_general(
            h1[:, lanes(to, 256)], d2[...], LEADING, preferred_element_type=F32
        ).reshape(NZ, 2, 8, 512)
        mid[0, to] = rows[:, 0]
        mid[1, to] = rows[:, 1]

    def send_mid(k, part, slot):
        rows = pl.ds(*part)
        mid_a.append(
            send(
                mid.at[0, (x + k) % NX, rows], ra_mid.at[k - 1, rows], slot, xs[k - 1]
            )
        )
        blocks = pl.ds(part[0] // 4, part[1] // 4)
        mid_b.append(
            send(
                mid.at[1, blocks, :, :, lanes((y + k) % NY, 128)],
                rb_mid.at[k - 1, blocks], slot + 1, ys[k - 1],
            )
        )

    send_mid(2, (0, 8), MID_ONE)

    cot_rows = [cot2[i].astype(BF16) for i in range(2)]
    grad_out = jnp.dot(
        jnp.concatenate(cot_rows, axis=1), h2, preferred_element_type=F32
    ).reshape(24, 8, 512)
    io[16:40] = grad_out
    own_back = lax.dot_general(
        d2[...], w_mid_ref[half, half], TRAILING, preferred_element_type=F32
    )
    ex_b.wait_recv()
    slope = jnp.concatenate([slope1[2 * c], slope1[2 * c + 1]], axis=1)
    delta_one = ((own_back + recv_b[...]) * slope).astype(BF16)
    x_rows = jnp.concatenate([x2[i].astype(BF16) for i in range(2)], axis=1)
    grad_in = jnp.dot(x_rows, delta_one, preferred_element_type=F32).reshape(16, 8, 512)
    io[0:16] = grad_in

    first_a, first_b = [], []
    for k in (2, 1, 3):
        first_a.append(
            send(io.at[pl.ds((x + k) % NX * 5, 5)], ra_io.at[k - 1], A_IO + k - 1, xs[k - 1])
        )
        first_b.append(
            send(
                io.at[pl.ds(20, 20), :, lanes((y + k) % NY, 128)],
                rb_io.at[k - 1], B_IO + k - 1, ys[k - 1],
            )
        )
    send_mid(2, (8, 8), MID_ONE + 2)

    y_lane = lanes(y, 128)
    two_io = []
    arrive(first_a)
    sai[...] = io[pl.ds(x * 5, 5)] + ra_io[0] + ra_io[1] + ra_io[2]
    for k in (2, 1, 3):
        two_io.append(
            send(sai.at[:, :, lanes((y + k) % NY, 128)], r2ai.at[k - 1], A_TWO_IO + k - 1, ys[k - 1])
        )
    arrive(first_b)
    sbi[...] = io[20:40, :, y_lane] + rb_io[0] + rb_io[1] + rb_io[2]
    for k in (2, 1, 3):
        two_io.append(
            send(sbi.at[pl.ds((x + k) % NX * 5, 5)], r2bi.at[k - 1], B_TWO_IO + k - 1, xs[k - 1])
        )
    send_mid(1, (0, 16), MID_ONE + 4)
    send_mid(3, (0, 16), MID_ONE + 6)
    arrive(two_io)
    io_a = sai[:, :, y_lane] + r2ai[0] + r2ai[1] + r2ai[2]
    io_b = sbi[pl.ds(x * 5, 5)] + r2bi[0] + r2bi[1] + r2bi[2]

    group, spot_z = z // 4, z % 4
    tiles_io = [io_a[t] for t in range(5)] + [io_b[t] for t in range(5)]
    tiles_io += [jnp.zeros((8, 128), F32)] * 2
    for i in range(4):
        for t in range(3):
            zi[i, t] = tiles_io[4 * t + i]
    near_z = [place(x, y, group * 4 + (spot_z + k) % 4, c) for k in range(1, 4)]
    far_z = [place(x, y, (z + 4 * k) % NZ, c) for k in range(1, 4)]
    third_io = []
    for k in (2, 1, 3):
        third_io.append(
            send(zi.at[(spot_z + k) % 4], rzi.at[k - 1], Z_ONE_IO + k, near_z[k - 1])
        )
    arrive(third_io)
    rzi_two[group] = zi[spot_z] + rzi[0] + rzi[1] + rzi[2]
    across_io = []
    for k in (2, 1, 3):
        across_io.append(
            send(rzi_two.at[group], rzi_two.at[group], Z_TWO_IO + k, far_z[k - 1])
        )

    two = []
    arrive(mid_a)
    sa[...] = mid[0, x] + ra_mid[0] + ra_mid[1] + ra_mid[2]
    for k in (2, 1, 3):
        two.append(
            send(sa.at[:, :, lanes((y + k) % NY, 128)], r2a.at[k - 1], A_TWO + k - 1, ys[k - 1])
        )
    arrive(mid_b)
    for i in range(NX):
        sb[i] = mid[1, i, :, :, y_lane] + rb_mid[0, i] + rb_mid[1, i] + rb_mid[2, i]
    for k in (2, 1, 3):
        two.append(send(sb.at[(x + k) % NX], r2b.at[k - 1], B_TWO + k - 1, xs[k - 1]))

    arrive(across_io)
    mine_io[...] = ((rzi_two[0] + rzi_two[1]) + rzi_two[2]) + rzi_two[3]
    share = []
    for k in (2, 1, 3):
        share.append(send(mine_io, ri.at[spot_z], Z_ALL + k, near_z[k - 1]))
    ri[spot_z] = mine_io[...]

    arrive(two)
    sum_a = sa[:, :, y_lane] + r2a[0] + r2a[1] + r2a[2]
    sum_b = sb[x] + r2b[0] + r2b[1] + r2b[2]
    for i in range(4):
        for g in range(4):
            zs[i, g] = sum_a[4 * g + i]
            zs[i, 4 + g] = sum_b[4 * g + i]
    third = []
    for k in (2, 1, 3):
        third.append(send(zs.at[(spot_z + k) % 4], rz.at[k - 1], Z_ONE + k, near_z[k - 1]))

    arrive(share)
    tile = lanes(c * NY + y, 128)
    rows_a, rows_b = pl.ds(x * 5, 5), pl.ds((NX + x) * 5, 5)
    for t in range(10):
        full[(t // 5 * NX + x) * 5 + t % 5, :, tile] = ri[t % 4, t // 4]
    gather = []
    for k in (2, 1, 3):
        spot = full.at[rows_a, :, tile]
        gather.append(send(spot, spot, A_THREE + k - 1, ys[k - 1]))
        spot = full.at[rows_b, :, tile]
        gather.append(send(spot, spot, B_THREE + k - 1, xs[k - 1]))

    arrive(third)
    grouped = zs[spot_z] + rz[0] + rz[1] + rz[2]
    for g in range(4):
        zs_two[g, 0] = grouped[g]
        zs_two[g, 1] = grouped[4 + g]
    across = []
    for k in (2, 1, 3):
        across.append(
            send(zs_two.at[(group + k) % 4], rz_two.at[k - 1], Z_TWO + k, far_z[k - 1])
        )

    arrive(gather)
    fourth = []
    for k in (2, 1, 3):
        spot = full.at[rows_a, :, half]
        fourth.append(send(spot, spot, A_FOUR + k - 1, xs[k - 1]))
        spot = full.at[pl.ds(20, 20), :, tile]
        fourth.append(send(spot, spot, B_FOUR + k - 1, ys[k - 1]))
    arrive(fourth)
    spot = full.at[:, :, half]
    pair = send(spot, spot, PAIR, partner)

    arrive(across)
    mine[...] = zs_two[group] + rz_two[0] + rz_two[1] + rz_two[2]
    last = []
    for k in range(NY):
        if k:
            last.append(send(mine.at[c], r4.at[c, y], MID_ALL + k, ys[k - 1]))
        last.append(
            send(
                mine.at[1 - c], r4.at[c, y], MID_ALL + 4 + k, yo[k - 1] if k else partner
            )
        )
    r4[c, y] = mine[c]
    pair.wait_recv()
    out_in[...] = full[0:16].reshape(128, 1024)
    out_out[...] = full[16:40].reshape(192, 1024)[0:172]
    arrive(last)
    for i in range(8):
        out_mid[:, pl.ds(128 * i, 128)] = r4[i // 4, i % 4]

    lax.fori_loop(1, NZ, pz_sent, 0)
    lax.fori_loop(1, NZ, zx_sent, 0)
    for one in copies:
        one.wait_send()


def write_kernel(*refs):
    writes = [
        pltpu.make_async_copy(refs[i], refs[4 + i], refs[8].at[i]) for i in range(4)
    ]
    for one in writes:
        one.start()
    for one in writes:
        one.wait()


def train(tile_row, tile_col, tile_count, features, tiles, dest, cotangent, w_in, w_mid, w_out):
    vmem = pl.BlockSpec(memory_space=pltpu.VMEM)
    hbm = pl.BlockSpec(memory_space=pltpu.HBM)
    buf = pltpu.VMEM
    return pl.pallas_call(
        train_kernel,
        out_shape=(
            jax.ShapeDtypeStruct((128, 128), F32),
            jax.ShapeDtypeStruct((128, 1024), F32),
            jax.ShapeDtypeStruct((8, 1024), F32),
            jax.ShapeDtypeStruct((172, 1024), F32),
        ),
        in_specs=[pl.BlockSpec(memory_space=pltpu.SMEM)] + [hbm] * 9,
        out_specs=(vmem,) * 4,
        scratch_shapes=[
            pltpu.SMEM((40,), jnp.int32),
            pltpu.SMEM((40,), jnp.int32),
            buf((32, 512), F32),
            buf((40, 128, 128), BF16),
            buf((4, 128), jnp.int32),
            buf((172, 128), BF16),
            buf((128, 1024), BF16),
            buf((1024, 1024), BF16),
            buf((172, 1024), BF16),
            buf((12, 32, 128), F32),
            buf((12, 32, 128), F32),
            buf((12, 96, 128), BF16),
            buf((512, 512), BF16),
            buf((96, 512), BF16),
            buf((128, 512), BF16),
            buf((NY, 32, 128), F32),
            buf((NY, 32, 128), F32),
            buf((NZ, 8, 128), F32),
            buf((NZ, 8, 128), F32),
            buf((8, NZ, 128), F32),
            buf((8, NZ, 128), F32),
            buf((NZ, 8, 128), F32),
            buf((NZ, 8, 128), F32),
            buf((8, NZ, 128), F32),
            buf((8, NZ, 128), F32),
            buf((128, 128), BF16),
            buf((2, 128, 128), F32),
            buf((2, 192, 128), F32),
            buf((256, 128), BF16),
            buf((256, 192), BF16),
            buf((192, 1024), BF16),
            buf((256, 1024), BF16),
            buf((4, 256, 256), F32),
            buf((256, 512), BF16),
            buf((256, 512), F32),
            buf((256, 512), F32),
            buf((2, NX, NZ, 8, 512), F32),
            buf((40, 8, 512), F32),
            buf((3, NZ, 8, 512), F32),
            buf((3, 5, 8, 512), F32),
            buf((3, NX, NZ, 8, 128), F32),
            buf((3, 20, 8, 128), F32),
            buf((NZ, 8, 512), F32),
            buf((NX, NZ, 8, 128), F32),
            buf((3, NZ, 8, 128), F32),
            buf((3, NZ, 8, 128), F32),
            buf((4, 8, 8, 128), F32),
            buf((3, 8, 8, 128), F32),
            buf((4, 2, 8, 128), F32),
            buf((3, 2, 8, 128), F32),
            buf((2, 8, 128), F32),
            buf((4, 3, 8, 128), F32),
            buf((2, NY, 8, 128), F32),
            buf((40, 8, 1024), F32),
            buf((5, 8, 512), F32),
            buf((20, 8, 128), F32),
            buf((3, 5, 8, 128), F32),
            buf((3, 5, 8, 128), F32),
            buf((4, 3, 8, 128), F32),
            buf((3, 3, 8, 128), F32),
            buf((4, 3, 8, 128), F32),
            buf((3, 8, 128), F32),
            pltpu.SemaphoreType.DMA((SEMS,)),
            pltpu.SemaphoreType.DMA((SEMS,)),
            pltpu.SemaphoreType.DMA((9,)),
            pltpu.SemaphoreType.REGULAR((3,)),
        ],
        compiler_params=pltpu.CompilerParams(
            collective_id=0, has_side_effects=True, vmem_limit_bytes=46 * 1024 * 1024
        ),
    )(tile_count, *(pltpu.with_memory_space_constraint(v, pltpu.HBM) for v in (
        tile_row, tile_col, features, tiles, dest, cotangent, w_in, w_mid, w_out
    )))


def shards(
    features, tiles, tile_row, tile_col, tile_count, dest_slot, w_in, w_mid, w_out, cotangent
):
    dest = dest_slot.reshape(4, 128)
    results = train(
        tile_row, tile_col, tile_count, features, tiles, dest, cotangent, w_in, w_mid, w_out
    )
    return pl.pallas_call(
        write_kernel,
        out_shape=tuple(jax.ShapeDtypeStruct(v.shape, v.dtype) for v in results),
        in_specs=[pl.BlockSpec(memory_space=pltpu.VMEM)] * 4,
        out_specs=(pl.BlockSpec(memory_space=pltpu.HBM),) * 4,
        scratch_shapes=[pltpu.SemaphoreType.DMA((4,))],
    )(*(pltpu.with_memory_space_constraint(v, pltpu.VMEM) for v in results))


def solution(mesh):
    in_specs = (
        P("rep", "dom"),
        P("dom", None, None),
        P("dom"),
        P("dom"),
        P("dom"),
        P("dom"),
        P(),
        P(),
        P(),
        P(None, ("dom", "rep")),
    )
    out_specs = (P(None, ("dom", "rep")), P(), P("dom", None), P())
    return jax.shard_map(shards, mesh=mesh, in_specs=in_specs, out_specs=out_specs, check_vma=False)
```
